128 devices in a mesh: wide: 16 (over x_lo, y, core), narrow: 8 (over z, x_hi).
Axes of the slice: x: 4 (x_hi: 2, x_lo: 2; x = x_hi * 2 + x_lo), y: 4, z: 4, core: 2. Of those that a mesh axis runs over, the one named last changes fastest.
Arguments:
- tokens: bfloat16 [4096, 2048], P('wide', 'narrow'), may hold values from -6 to 6
- norm_gain: bfloat16 [2048], replicated, may hold values from 0.25 to 1.75
- router: bfloat16 [2048, 8], replicated, may hold values from -0.125 to 0.125
- routes: int32 [4096, 2], P('wide'), may hold values from 0 to 7, all different within a row
- kv_weight: bfloat16 [4096, 2048], P('narrow', 'wide'), may hold values from -0.125 to 0.125
- query_weight: bfloat16 [16384, 2048], P('narrow', 'wide'), may hold values from -0.125 to 0.125
- out_weight: bfloat16 [16384, 2048], P('narrow', 'wide'), may hold values from -0.09375 to 0.09375
- prefix_cache: bfloat16 [12288, 4096], P('wide', 'narrow'), may hold values from -225 to 225
- suffix_lengths: int32 [4], replicated, may hold values from 1 to 3328, 4096 in all
- prefix_lengths: int32 [4], replicated, may hold values from 1 to 6144, 12288 in all
Outputs:
- mixed: bfloat16 [4096, 2048], P('wide', 'narrow')
The draws below stay inside these ranges and needn't reach their ends.
Inputs may be any that keep to these rules, and one draw needn't show every extreme that they name: `routes`: each token names 2 different experts. `suffix_lengths`: they sum to 4096. `prefix_lengths`: they sum to 12288.
All inputs are finite; a program needn't handle non-finite values.
Results may differ from the reference program's by a relative error of at most 0.012.
The reference program's roundings to bfloat16 on the way (of `normed`, `kv_rows`, `query_all`, `selected` and `attended`) count: a program that leaves them out, or rounds other values in their place, can miss the bound.
Values may be sent and summed in bfloat16 or wider, within the bound.
No kernel may reach another device: no remote copies, remote signals or barrier semaphores. Data moves between devices by JAX's collectives and lax.ppermute only.
A program may use at most 320 MiB of HBM per device.

```python
import math
import jax
import jax.numpy as jnp
import numpy as np
from jax import lax

D = 2048
KVH = 16
H = 128
E = 8
TOPK = 2
TENANTS = 4
TOK_DEV = 256
TOKENS = 4096
PREFIX = 12288


def draw_prefix_cache(key, part):
    values = jnp.clip(jax.random.normal(key, (PREFIX, KVH * 2 * H), jnp.float32), -4.5, 4.5)
    return values.astype(jnp.bfloat16)


def block_levels(key, dims, shards, low, largest):
    level, own = 1.0, jax.random.fold_in(key, 6)
    for axis_at, blocks in shards:
        heights = jnp.exp(jax.random.uniform(jax.random.fold_in(own, axis_at), (blocks,), jnp.float32, low / len(shards), largest / len(shards)))
        level = level * jnp.repeat(heights, dims[axis_at] // blocks).reshape([-1 if axis == axis_at else 1 for axis in range(len(dims))])
    return level


def distinct(rng, rows, number_of, top, lift):
    order = jax.random.permutation(jax.random.fold_in(rng, 1), number_of)
    favour = order
    for power in range(3):
        favour = favour * favour // number_of
    favour = favour * lift // number_of
    chance = jax.random.randint(jax.random.fold_in(rng, 2), (rows, number_of), 0, 4096) + favour
    holders = jax.random.permutation(jax.random.fold_in(rng, 3), rows)[jnp.arange(number_of) % rows]
    chance = jnp.where(jnp.arange(rows)[:, None] == holders[None, :], 1 << 14, chance)
    score = chance * number_of + jnp.arange(number_of)
    return lax.top_k(score.astype(jnp.int32), top)[1].astype(jnp.int32)


def length_profile(amount, total, bound, slope):
    portions = [(1 << 20) // math.isqrt(grade ** slope) + 1 for grade in range(2, amount + 1)]
    rest, holding = total - bound - (amount - 1), [1] * (amount - 1)
    while rest > 0:
        free = [i for i in range(amount - 1) if holding[i] < bound]
        whole, left = sum([portions[i] for i in free]), rest
        for i in free:
            more = min(bound - holding[i], max(1, left * portions[i] // whole), rest)
            holding[i] = holding[i] + more
            rest = rest - more
    return np.array([bound] + holding)


def ragged(stream_key, count, total, most, skew):
    if count == 2:
        one = jax.random.randint(stream_key, (), max(1, total - most), min(most, total - 1) + 1)
        return jnp.stack([one, total - one])
    tallies = jnp.asarray(length_profile(count, total, most, skew), jnp.int32)
    twos = (count - 1) // 2
    source_of, taker = tallies[1:1 + 2 * twos:2], tallies[2:2 + 2 * twos:2]
    room = jnp.minimum(source_of - 1, most - taker)
    moved = jax.random.randint(jax.random.fold_in(stream_key, 1), (twos,), 0, 1 << 20) % (room + 1)
    tallies = tallies.at[1:1 + 2 * twos:2].set(source_of - moved).at[2:2 + 2 * twos:2].set(taker + moved)
    return tallies[jax.random.permutation(jax.random.fold_in(stream_key, 2), count)]


def bell_draw(own_key, extent, scale, reach, pieces=(), kind=jnp.bfloat16):
    drawn = scale * jax.random.normal(own_key, extent, jnp.float32)
    if pieces:
        drawn = drawn * block_levels(own_key, extent, pieces, -0.22, 0.18)
    return jnp.clip(drawn, -reach, reach).astype(kind)


def setup_inputs(seed: int = 0) -> dict:
    key_of = jax.random.split(jax.random.key(seed), 11)
    return {
        "tokens": bell_draw(key_of[0], (TOKENS, D), 1.0, 6.0, ((0, 16), (1, 8))),
        "norm_gain": jnp.clip(1.0 + 0.15 * jax.random.normal(key_of[1], (D,), jnp.float32), 0.25, 1.75).astype(jnp.bfloat16),
        "router": bell_draw(key_of[2], (D, E), D ** -0.5, 0.125),
        "routes": distinct(key_of[3], TOKENS, E, TOPK, 2048),
        "kv_weight": bell_draw(key_of[4], (KVH * 2 * H, D), D ** -0.5, 0.125, ((0, 8), (1, 16))),
        "query_weight": bell_draw(key_of[5], (KVH * E * H, D), D ** -0.5, 0.125, ((0, 8), (1, 16))),
        "out_weight": bell_draw(key_of[6], (KVH * E * H, D), (TOPK * KVH * H) ** -0.5, 0.09375, ((0, 8), (1, 16))),
        "prefix_cache": draw_prefix_cache(jax.random.fold_in(key_of[10], 71), 0),
        "suffix_lengths": ragged(key_of[8], TENANTS, TOKENS, TOKENS - 3 * TOK_DEV, 2).astype(jnp.int32),
        "prefix_lengths": ragged(key_of[9], TENANTS, PREFIX, PREFIX // 2, 2).astype(jnp.int32),
    }


eps = 1e-06

def tenant_of(positions, lengths):
    bounds = jnp.cumsum(lengths).astype(jnp.int32)
    return lax.optimization_barrier(jnp.sum((positions[:, None] >= bounds[None, :]).astype(jnp.int32), axis=1)).astype(jnp.int32)

def reference(tokens, norm_gain, router, routes, kv_weight, query_weight, out_weight, prefix_cache, suffix_lengths, prefix_lengths):
    floats = tokens.astype(jnp.float32)
    normed = (floats * lax.rsqrt(lax.optimization_barrier(jnp.mean(floats * floats, axis=1, keepdims=True)) + eps) * norm_gain.astype(jnp.float32)).astype(jnp.bfloat16)
    logits = jnp.dot(normed, router, preferred_element_type=jnp.float32)
    choose = (routes[:, :, None] == jnp.arange(E, dtype=jnp.int32)[None, None, :]).astype(jnp.float32)
    chosen = lax.optimization_barrier(jnp.sum(choose * logits[:, None, :], axis=2))
    gate_values = jax.nn.softmax(chosen, axis=1)
    kv_rows = jnp.dot(normed, kv_weight.T, preferred_element_type=jnp.float32).astype(jnp.bfloat16).reshape(TOKENS, KVH, 2, H)
    query_all = jnp.dot(normed, query_weight.T, preferred_element_type=jnp.float32).astype(jnp.bfloat16).reshape(TOKENS, KVH, E, H)
    selected = jnp.einsum('tje,thed->thjd', choose, query_all.astype(jnp.float32)).astype(jnp.bfloat16)
    cache_rows = prefix_cache.reshape(PREFIX, KVH, 2, H)
    key_rows = jnp.concatenate([cache_rows[:, :, 0, :], kv_rows[:, :, 0, :]], axis=0)
    value_rows = jnp.concatenate([cache_rows[:, :, 1, :], kv_rows[:, :, 1, :]], axis=0)
    token_index = jnp.arange(TOKENS, dtype=jnp.int32)
    slot_index = jnp.arange(PREFIX, dtype=jnp.int32)
    token_tenant = tenant_of(token_index, suffix_lengths)
    slot_tenant = tenant_of(slot_index, prefix_lengths)
    prefix_allowed = token_tenant[:, None] == slot_tenant[None, :]
    suffix_allowed = (token_tenant[:, None] == token_tenant[None, :]) & (token_index[None, :] <= token_index[:, None])
    allowed = jnp.concatenate([prefix_allowed, suffix_allowed], axis=1)
    scaling = H ** (-0.5)

    def one_head(inputs):
        queries, keys_here, values_here = inputs
        scores = jnp.einsum('tjd,kd->tjk', queries.astype(jnp.float32), keys_here.astype(jnp.float32), precision=lax.Precision.HIGHEST) * scaling
        scores = jnp.where(allowed[:, None, :], scores, -jnp.inf)
        highest = lax.optimization_barrier(jnp.max(scores, axis=2, keepdims=True))
        weights = jnp.exp(scores - highest)
        totals = lax.optimization_barrier(jnp.sum(weights, axis=2))
        summed = jnp.einsum('tjk,kd->tjd', weights, values_here.astype(jnp.float32), precision=lax.Precision.HIGHEST)
        return summed / totals[:, :, None]
    attended = lax.map(one_head, (jnp.transpose(selected, (1, 0, 2, 3)), jnp.transpose(key_rows, (1, 0, 2)), jnp.transpose(value_rows, (1, 0, 2))))
    weighted = (attended * gate_values[None, :, :, None]).astype(jnp.bfloat16)
    padded = jnp.einsum('tje,htjd->thed', choose, weighted.astype(jnp.float32)).astype(jnp.bfloat16).reshape(TOKENS, KVH * E * H)
    return jnp.dot(padded, out_weight, preferred_element_type=jnp.float32).astype(jnp.bfloat16)
```

```python
import functools
import math

import jax
import jax.numpy as jnp
from jax import lax
from jax.experimental import pallas as pl
from jax.experimental.pallas import tpu as pltpu
from jax.sharding import Mesh
from jax.sharding import PartitionSpec as P

H = 128
E = 8
EPS = 1e-06
FLOOR = -1e30
AXES = ("xl", "y", "c", "z", "xh")
SIZES = (2, 4, 2, 4, 2)
WIDE = ("xl", "y", "c")
NARROW = ("z", "xh")
BF16 = jnp.bfloat16
F32 = jnp.float32
SCALE2 = H ** (-0.5) * math.log2(math.e)
CK = 256
STEPS = [(dz, dx) for dz in range(4) for dx in range(2)]


def along_y(x, k):
    return lax.ppermute(x, "y", [(i, (i + k) % 4) for i in range(4)])


def across_x(x):
    return lax.ppermute(x, "xl", [(0, 1), (1, 0)])


def across_core(x):
    return lax.ppermute(x, "c", [(0, 1), (1, 0)])


def narrow_step(x, dz, dx):
    perm = [(z * 2 + h, ((z + dz) % 4) * 2 + (h ^ dx)) for z in range(4) for h in range(2)]
    return lax.ppermute(x, NARROW, perm)


def gather_wide(w):
    half = w.shape[0] // 2
    a = across_x(w)
    yp, ym = along_y(w, 1), along_y(w, 3)
    ap, am = along_y(a, 1), along_y(a, 3)
    far0 = along_y(yp[:half], 1)
    far1 = along_y(ym[half:], 3)
    afar0, afar1 = across_x(far0), across_x(far1)
    mine = [w, a, yp, ym, ap, am, (far0, far1), (afar0, afar1)]
    other = jax.tree.map(across_core, mine)
    flat = []
    for m, o in zip(mine, other):
        if not isinstance(m, tuple):
            m, o = (m[:half], m[half:]), (o[:half], o[half:])
        flat.append((m, o))
    return mine, other


def chip_order():
    xl, y = lax.axis_index("xl"), lax.axis_index("y")
    pairs = [
        (xl, y),
        (1 - xl, y),
        (xl, y + 3),
        (xl, y + 1),
        (1 - xl, y + 3),
        (1 - xl, y + 1),
        (xl, y + 2),
        (1 - xl, y + 2),
    ]
    return jnp.stack([a * 4 + lax.rem(b, 4) for a, b in pairs]).astype(jnp.int32)


def flatten_blocks(mine, other):
    return jax.tree.leaves(mine) + jax.tree.leaves(other)


N_W = 10


def load_blocks(refs):
    whole = [[r] for r in refs[:6]]
    return whole + [list(refs[6:8]), list(refs[8:10])]


def nt_dot(a, b):
    return lax.dot_general(a, b, (((1,), (1,)), ((), ())), preferred_element_type=F32)


def norm_kv_kernel(idx, *refs):
    blocks = refs[:8]
    gain, router, routes = refs[8:11]
    weights = refs[11 : 11 + 2 * N_W]
    normed, gates, kv = refs[11 + 2 * N_W :]
    core = idx[16]
    total = jnp.zeros((blocks[0].shape[0], 1), F32)
    for b in blocks:
        v = b[...].astype(F32)
        total = total + jnp.sum(v * v, axis=1, keepdims=True)
    scale = lax.rsqrt(total * (1.0 / 2048) + EPS)
    for k in range(8):
        src = idx[k]
        v = (blocks[k][...].astype(F32) * scale * gain[src].astype(F32)).astype(BF16)
        normed[src, core] = v[:, :H]
        normed[src, 1 - core] = v[:, H:]
    logits = jnp.zeros((256, E), F32)
    for nb in range(8):
        logits += jnp.dot(normed[nb, core], router[nb, 0], preferred_element_type=F32)
        logits += jnp.dot(normed[nb, 1 - core], router[nb, 1], preferred_element_type=F32)
    lane = lax.broadcasted_iota(jnp.int32, (256, E), 1)
    chosen = [
        jnp.sum(jnp.where(routes[:, j : j + 1] == lane, logits, 0.0), axis=1, keepdims=True)
        for j in range(2)
    ]
    top = jnp.maximum(chosen[0], chosen[1])
    e0, e1 = jnp.exp(chosen[0] - top), jnp.exp(chosen[1] - top)
    gates[:, 0:1] = e0 / (e0 + e1)
    gates[:, 1:2] = e1 / (e0 + e1)
    mine, other = load_blocks(weights[:N_W]), load_blocks(weights[N_W:])
    acc = jnp.zeros((256, 4 * H), F32)
    for i in range(8):
        nb = idx[8 + i]
        x = jnp.concatenate([normed[nb, 0], normed[nb, 1]], axis=1)
        m = jnp.concatenate([r[...] for r in mine[i]], axis=0)
        o = jnp.concatenate([r[...] for r in other[i]], axis=0)
        acc += nt_dot(x, jnp.concatenate([m, o], axis=1))
    kv[...] = acc.astype(BF16)


def norm_kv(idx, blocks, gain, router, routes, weights):
    vmem = pl.BlockSpec(memory_space=pltpu.VMEM)
    n_in = 8 + 3 + len(weights)
    return pl.pallas_call(
        norm_kv_kernel,
        out_shape=(
            jax.ShapeDtypeStruct((8, 2, 256, H), BF16),
            jax.ShapeDtypeStruct((256, 2), F32),
            jax.ShapeDtypeStruct((256, 4 * H), BF16),
        ),
        in_specs=[pl.BlockSpec(memory_space=pltpu.SMEM)] + [vmem] * n_in,
        out_specs=(vmem, vmem, vmem),
        compiler_params=pltpu.CompilerParams(vmem_limit_bytes=40 << 20),
        cost_estimate=pl.CostEstimate(flops=1 << 30, bytes_accessed=4 << 20, transcendentals=0),
        name="norm_kv",
    )(idx, *blocks, gain, router, routes, *weights)


def query_kernel(idx, normed, routes, *refs):
    weights, out, sel = refs[: 2 * N_W], refs[2 * N_W], refs[2 * N_W + 1]
    group = pl.program_id(1)
    whole = [weights[:6], weights[N_W : N_W + 6]]
    far = [weights[6:N_W], weights[N_W + 6 :]]
    acc = jnp.zeros((256, 4 * H), F32)
    for i in range(8):
        nb = idx[8 + i]
        x = jnp.concatenate([normed[nb, 0], normed[nb, 1]], axis=1)
        if i < 6:
            w = jnp.concatenate([whole[0][i][...], whole[1][i][...]], axis=1)
        else:
            first = pl.program_id(0) == 0
            picked = []
            for side in range(2):
                a, b = far[side][2 * (i - 6)], far[side][2 * (i - 6) + 1]
                picked.append(jnp.where(first, a[...], b[...]))
            w = jnp.concatenate(picked, axis=1)
        acc += nt_dot(x, w)
    for j in range(2):
        value = jnp.where(group == 0, 0.0, sel[j])
        for e in range(4):
            hit = routes[:, j : j + 1] == group * 4 + e
            value = jnp.where(hit, acc[:, e * H : (e + 1) * H], value)
        sel[j] = value
        out[0, j] = value.astype(BF16)


def project_queries(idx, normed, routes, weights):
    rows = 4 * H
    whole = pl.BlockSpec((rows, H), lambda h, g: (h * 2 + g, 0))
    half = pl.BlockSpec((rows, H), lambda h, g: (g, 0))
    side = [whole] * 6 + [half] * 4
    return pl.pallas_call(
        query_kernel,
        grid=(2, 2),
        out_shape=jax.ShapeDtypeStruct((2, 2, 256, H), BF16),
        in_specs=[
            pl.BlockSpec(memory_space=pltpu.SMEM),
            pl.BlockSpec((8, 2, 256, H), lambda h, g: (0, 0, 0, 0)),
            pl.BlockSpec((256, 2), lambda h, g: (0, 0)),
        ]
        + side * 2,
        out_specs=pl.BlockSpec((1, 2, 256, H), lambda h, g: (h, 0, 0, 0)),
        scratch_shapes=[pltpu.VMEM((2, 256, H), F32)],
        compiler_params=pltpu.CompilerParams(vmem_limit_bytes=40 << 20),
        cost_estimate=pl.CostEstimate(flops=4 << 30, bytes_accessed=9 << 20, transcendentals=0),
        name="project_queries",
    )(idx, normed, routes, *weights)


def attend_kernel(count, table, bases, lo, hi, *refs):
    qs = refs[:count]
    prefix, suffix = refs[count : count + 4], refs[count + 4 : count + 8]
    outs = refs[count + 8 : count + 8 + count]
    lses = refs[count + 8 + count : count + 8 + 2 * count]
    store, top, tot, acc, sem = refs[count + 8 + 2 * count :]
    copies = []
    for i in range(4):
        copies.append(
            pltpu.make_async_copy(prefix[i], store.at[pl.ds(i * 768, 768)], sem.at[i])
        )
        copies.append(
            pltpu.make_async_copy(suffix[i], store.at[pl.ds(3072 + i * 256, 256)], sem.at[4 + i])
        )
    for c in copies:
        c.start()
    for c in copies:
        c.wait()

    for b in range(count):
        q = qs[b]
        top[...] = jnp.full(top.shape, FLOOR, F32)
        tot[...] = jnp.zeros(tot.shape, F32)
        acc[...] = jnp.zeros(acc.shape, F32)

        def chunk(i, masked, kind):
            at = pl.multiple_of(i * CK, CK)
            if masked:
                pos = bases[i] + lax.broadcasted_iota(jnp.int32, (CK, 512), 0)
                allowed = (pos >= lo[b, pl.ds(kind, 1), :]) & (pos < hi[b, pl.ds(kind, 1), :])
            for h in range(2):
                keys = store[pl.ds(at, CK), 2 * h * H : (2 * h + 1) * H]
                values = store[pl.ds(at, CK), (2 * h + 1) * H : (2 * h + 2) * H]
                s = nt_dot(keys, q[h])
                if masked:
                    s = jnp.where(allowed, s, -jnp.inf)
                old = top[h]
                new = jnp.maximum(old, jnp.max(s, axis=0, keepdims=True))
                p = jnp.exp2(s * SCALE2 - new * SCALE2)
                factor = jnp.exp2((old - new) * SCALE2)
                top[h] = new
                tot[h] = tot[h] * factor + jnp.sum(p, axis=0, keepdims=True)
                acc[h] = acc[h] * factor + lax.dot_general(
                    values, p.astype(BF16), (((0,), (0,)), ((), ())), preferred_element_type=F32
                )

        def visit(i, _):
            kind = jnp.where(i >= 12, 1, 0)
            base = bases[i]
            cell = (b * 2 + kind) * 4
            lo_first, lo_last = table[cell], table[cell + 1]
            hi_first, hi_last = table[cell + 2], table[cell + 3]
            some = (base + CK > lo_first) & (base < hi_last)
            full = (base >= lo_last) & (base + CK <= hi_first)

            @pl.when(full)
            def _():
                chunk(i, False, kind)

            @pl.when(some & jnp.logical_not(full))
            def _():
                chunk(i, True, kind)

            return 0

        lax.fori_loop(0, 16, visit, 0)
        for h in range(2):
            total = tot[h]
            safe = jnp.where(total > 0.0, total, 1.0)
            outs[b][h] = (acc[h] / safe).astype(BF16)
            lses[b][h] = jnp.where(total > 0.0, top[h] * SCALE2 + jnp.log2(safe), FLOOR)


def attend(table, bases, lo, hi, qs, prefix, suffix):
    count = len(qs)
    smem = pl.BlockSpec(memory_space=pltpu.SMEM)
    vmem = pl.BlockSpec(memory_space=pltpu.VMEM)
    hbm = pl.BlockSpec(memory_space=pl.ANY)
    return pl.pallas_call(
        functools.partial(attend_kernel, count),
        out_shape=tuple(jax.ShapeDtypeStruct((2, H, 512), BF16) for _ in range(count))
        + tuple(jax.ShapeDtypeStruct((2, 1, 512), F32) for _ in range(count)),
        in_specs=[smem, smem, vmem, vmem] + [vmem] * count + [hbm] * 8,
        out_specs=tuple([vmem] * (2 * count)),
        scratch_shapes=[
            pltpu.VMEM((4096, 512), BF16),
            pltpu.VMEM((2, 1, 512), F32),
            pltpu.VMEM((2, 1, 512), F32),
            pltpu.VMEM((2, H, 512), F32),
            pltpu.SemaphoreType.DMA((8,)),
        ],
        compiler_params=pltpu.CompilerParams(vmem_limit_bytes=40 << 20),
        cost_estimate=pl.CostEstimate(
            flops=count * (4 << 30), bytes_accessed=8 << 20, transcendentals=count << 21
        ),
        name="attend",
    )(table, bases, lo, hi, *qs, *prefix, *suffix)


def out_kernel(idx, gates, routes, *refs):
    parts, lses = refs[:4], refs[4:8]
    weights = refs[8 : 8 + 2 * N_W]
    own = refs[8 + 2 * N_W]
    outs = refs[9 + 2 * N_W : 16 + 2 * N_W]
    held, padded, sem = refs[16 + 2 * N_W :]
    core = idx[16]
    copies = []
    for side in range(2):
        at_core = core if side == 0 else 1 - core
        group = weights[side * N_W : (side + 1) * N_W]
        for k in range(N_W):
            if k < 6:
                target = held.at[idx[8 + k], at_core]
            else:
                block, part = 6 + (k - 6) // 2, (k - 6) % 2
                target = held.at[idx[8 + block], at_core, pl.ds(part * 1024, 1024)]
            copies.append(pltpu.make_async_copy(group[k], target, sem.at[side * N_W + k]))
    for c in copies:
        c.start()
    for h in range(2):
        high = lses[0][h]
        for r in lses[1:]:
            high = jnp.maximum(high, r[h])
        share = [jnp.exp2(r[h] - high) for r in lses]
        norm = gates[...] / (share[0] + share[1] + share[2] + share[3])
        total = jnp.zeros((H, 512), F32)
        for r, s in zip(parts, share):
            total += r[h].astype(F32) * s
        attended = jnp.transpose(total * norm)
        for e in range(E):
            value = jnp.zeros((256, H), F32)
            for j in range(2):
                hit = routes[:, j : j + 1] == e
                value = jnp.where(hit, attended[j * 256 : (j + 1) * 256], value)
            at = (h * E + e) * H
            padded[:, at : at + H] = value.astype(BF16)
    for c in copies:
        c.wait()
    for k in range(8):
        nb = idx[17 + k]
        w = jnp.concatenate([held[nb, 0], held[nb, 1]], axis=1)
        value = jnp.dot(padded[...], w, preferred_element_type=F32)
        if k == 0:
            own[...] = value
        else:
            outs[k - 1][...] = value.astype(BF16)


def project_out(idx, gates, routes, parts, lses, weights):
    smem = pl.BlockSpec(memory_space=pltpu.SMEM)
    vmem = pl.BlockSpec(memory_space=pltpu.VMEM)
    hbm = pl.BlockSpec(memory_space=pl.ANY)
    return pl.pallas_call(
        out_kernel,
        out_shape=(jax.ShapeDtypeStruct((256, 256), F32),)
        + tuple(jax.ShapeDtypeStruct((256, 256), BF16) for _ in range(7)),
        in_specs=[smem, vmem, vmem] + [vmem] * 8 + [hbm] * (2 * N_W),
        out_specs=tuple([vmem] * 8),
        scratch_shapes=[
            pltpu.VMEM((8, 2, 2048, H), BF16),
            pltpu.VMEM((256, 2048), BF16),
            pltpu.SemaphoreType.DMA((2 * N_W,)),
        ],
        compiler_params=pltpu.CompilerParams(vmem_limit_bytes=40 << 20),
        cost_estimate=pl.CostEstimate(flops=4 << 30, bytes_accessed=9 << 20, transcendentals=0),
        name="project_out",
    )(idx, gates, routes, *parts, *lses, *weights)


def limits(first_token, suffix_lengths, prefix_lengths):
    token = first_token + jnp.arange(256, dtype=jnp.int32)
    ends = jnp.cumsum(suffix_lengths)
    slot_ends = jnp.cumsum(prefix_lengths)
    tenant = jnp.sum((token[:, None] >= ends[None, :]).astype(jnp.int32), axis=1)
    one_hot = tenant[:, None] == jnp.arange(4, dtype=jnp.int32)[None, :]

    def pick(v):
        return jnp.sum(jnp.where(one_hot, v[None, :], 0), axis=1)

    lo = jnp.stack([pick(slot_ends - prefix_lengths), pick(ends - suffix_lengths)])
    hi = jnp.stack([pick(slot_ends), token + 1])
    table = jnp.stack([lo[:, 0], lo[:, -1], hi[:, 0], hi[:, -1]], axis=1)
    return table, jnp.concatenate([lo, lo], axis=1), jnp.concatenate([hi, hi], axis=1)


def on_device(
    tokens,
    norm_gain,
    router,
    routes,
    kv_weight,
    query_weight,
    out_weight,
    prefix_cache,
    suffix_lengths,
    prefix_lengths,
):
    xl, y, c = (lax.axis_index(a) for a in WIDE)
    z, xh = (lax.axis_index(a) for a in NARROW)
    chips = chip_order()
    token_src = jnp.stack([lax.rem(z + 4 - dz, 4) * 2 + (xh ^ dx) for dz, dx in STEPS])
    out_dest = jnp.stack([lax.rem(z + dz, 4) * 2 + (xh ^ dx) for dz, dx in STEPS])
    idx = jnp.concatenate([token_src, chips, c[None], out_dest]).astype(jnp.int32)

    blocks = [tokens] + [narrow_step(tokens, *s) for s in STEPS[1:]]
    kv_blocks = flatten_blocks(*gather_wide(kv_weight))
    query_blocks = flatten_blocks(*gather_wide(query_weight))
    out_blocks = flatten_blocks(*gather_wide(out_weight))
    prefix = [prefix_cache, across_x(prefix_cache)]
    prefix += [across_core(p) for p in prefix]

    gain = norm_gain.reshape(8, 1, 256)
    normed, gates, kv = norm_kv(
        idx, blocks, gain, router.reshape(8, 2, H, E), routes, kv_blocks
    )
    q = project_queries(idx, normed, routes, query_blocks).reshape(2, 512, H)
    suffix = [kv, across_x(kv)]
    suffix += [across_core(s) for s in suffix]
    qs = [q] + [along_y(q, k) for k in (1, 2, 3)]

    holders = [xl * 8 + y * 2 + c, (1 - xl) * 8 + y * 2 + c]
    holders += [xl * 8 + y * 2 + 1 - c, (1 - xl) * 8 + y * 2 + 1 - c]
    bases = [w * 768 + s * CK for w in holders for s in range(3)] + [w * 256 for w in holders]
    bases = jnp.stack(bases).astype(jnp.int32)
    tables, los, his = [], [], []
    for k in range(4):
        first = (xl * 8 + lax.rem(y + 4 - k, 4) * 2 + c) * 256
        t, lo, hi = limits(first, suffix_lengths, prefix_lengths)
        tables.append(t)
        los.append(lo)
        his.append(hi)
    table = jnp.stack(tables).reshape(-1).astype(jnp.int32)
    done = attend(table, bases, jnp.stack(los), jnp.stack(his), qs, prefix, suffix)
    parts, lses = list(done[:4]), list(done[4:])
    for k in range(1, 4):
        parts[k] = along_y(parts[k], 4 - k)
        lses[k] = along_y(lses[k], 4 - k)
    gate_row = gates.T.reshape(1, 512)
    sums = project_out(idx, gate_row, routes, parts, lses, out_blocks)
    total = sums[0]
    for s, v in zip(STEPS[1:], sums[1:]):
        total = total + narrow_step(v, *s).astype(F32)
    return total.astype(BF16)


def solution(mesh):
    fine = Mesh(mesh.devices.reshape(SIZES), AXES)
    placed = (
        P(WIDE, NARROW),
        P(),
        P(),
        P(WIDE, None),
        P(NARROW, WIDE),
        P(NARROW, WIDE),
        P(NARROW, WIDE),
        P(WIDE, NARROW),
        P(),
        P(),
    )
    return jax.shard_map(
        on_device, mesh=fine, in_specs=placed, out_specs=P(WIDE, NARROW), check_vma=False
    )
```

```python
import functools
import math

import jax
import jax.numpy as jnp
from jax import lax
from jax.experimental import pallas as pl
from jax.experimental.pallas import tpu as pltpu
from jax.sharding import Mesh
from jax.sharding import PartitionSpec as P

H = 128
E = 8
EPS = 1e-06
FLOOR = -1e30
AXES = ("xl", "y", "c", "z", "xh")
SIZES = (2, 4, 2, 4, 2)
WIDE = ("xl", "y", "c")
NARROW = ("z", "xh")
BF16 = jnp.bfloat16
F32 = jnp.float32
SCALE2 = H ** (-0.5) * math.log2(math.e)
CK = 512
R = 512
CHUNKS = 8
TILES = 8
DUMMY = 8
UNROLL = 4

SMEM = pl.BlockSpec(memory_space=pltpu.SMEM)
VMEM = pl.BlockSpec(memory_space=pltpu.VMEM)
HBM = pl.BlockSpec(memory_space=pltpu.HBM)


def along_y(x, k):
    return lax.ppermute(x, "y", [(i, (i + k) % 4) for i in range(4)])


def along_z(x, k):
    return lax.ppermute(x, "z", [(i, (i + k) % 4) for i in range(4)])


def across_x(x):
    return lax.ppermute(x, "xl", [(0, 1), (1, 0)])


def across_far(x):
    return lax.ppermute(x, "xh", [(0, 1), (1, 0)])


def across_core(x):
    return lax.ppermute(x, "c", [(0, 1), (1, 0)])


def tie(a, b):
    return lax.optimization_barrier((a, b))


def gather_chips(w):
    a = across_x(w)
    yp, ym = along_y(w, 1), along_y(w, 3)
    ap, am = along_y(a, 1), along_y(a, 3)
    far0, far1 = along_y(yp[0], 1), along_y(ym[1], 3)
    afar0, afar1 = across_x(far0), across_x(far1)
    return [w, a, yp, ym, ap, am, far0, far1, afar0, afar1]


def chip_order():
    xl, y = lax.axis_index("xl"), lax.axis_index("y")
    pairs = [
        (xl, y),
        (1 - xl, y),
        (xl, y + 3),
        (xl, y + 1),
        (1 - xl, y + 3),
        (1 - xl, y + 1),
        (xl, y + 2),
        (1 - xl, y + 2),
    ]
    return [a * 4 + lax.rem(b, 4) for a, b in pairs]


def nt_dot(a, b):
    return lax.dot_general(a, b, (((1,), (1,)), ((), ())), preferred_element_type=F32)


def run(copies):
    for c in copies:
        c.start()
    for c in copies:
        c.wait()


def norm_kernel(idx, gain, b0, b1, b2, b3, normed, held, sem):
    refs = (b0, b1, b2, b3)
    run([pltpu.make_async_copy(r, held.at[i], sem.at[i]) for i, r in enumerate(refs)])
    total = jnp.zeros((256, 1), F32)
    for k in range(8):
        v = held[k // 2, k % 2].astype(F32)
        total = total + jnp.sum(v * v, axis=1, keepdims=True)
    scale = lax.rsqrt(total * (1.0 / 2048) + EPS)
    for k in range(8):
        src = idx[k]
        v = held[k // 2, k % 2].astype(F32) * scale * gain[src].astype(F32)
        normed[src, 0] = v[:, :H].astype(BF16)
        normed[src, 1] = v[:, H:].astype(BF16)


def normalise(idx, gain, blocks):
    return pl.pallas_call(
        norm_kernel,
        out_shape=jax.ShapeDtypeStruct((8, 2, 256, H), BF16),
        in_specs=[SMEM, VMEM] + [HBM] * 4,
        out_specs=VMEM,
        scratch_shapes=[pltpu.VMEM((4, 2, 256, 256), BF16), pltpu.SemaphoreType.DMA((4,))],
        compiler_params=pltpu.CompilerParams(vmem_limit_bytes=8 << 20),
        cost_estimate=pl.CostEstimate(flops=1 << 24, bytes_accessed=2 << 20, transcendentals=0),
        name="normalise",
    )(idx, gain, *blocks)


def project_kernel(idx, routes, router, own, other, *refs):
    blocks = refs[:10]
    q_out, kv_out, gates, xs, held, sel, sem = refs[10:]
    core = idx[8]
    rows_of = [pl.multiple_of(core * 256, 256), pl.multiple_of((1 - core) * 256, 256)]
    x_copies = [
        pltpu.make_async_copy(r, xs.at[:, :, pl.ds(at, 256)], sem.at[5 + i])
        for i, (r, at) in enumerate(zip((own, other), rows_of))
    ]

    def tile_copies(r):
        at = pl.ds(r * 256, 256)
        copies = []
        for k in range(10):
            if k < 6:
                src, dst = blocks[k].at[:, at], held.at[k, :, at]
            else:
                src, dst = blocks[k].at[at], held.at[6 + (k - 6) // 2, (k - 6) % 2, at]
            copies.append(pltpu.make_async_copy(src, dst, sem.at[r]))
        return copies

    tiles = [tile_copies(r) for r in range(5)]
    for c in x_copies:
        c.start()
    for group in tiles:
        for c in group:
            c.start()
    for c in x_copies:
        c.wait()
    logits = jnp.zeros((512, E), F32)
    for nb in range(8):
        for side in range(2):
            logits += jnp.dot(xs[nb, side], router[nb, side], preferred_element_type=F32)
    lane = lax.broadcasted_iota(jnp.int32, (512, E), 1)
    chosen = [
        jnp.sum(jnp.where(routes[:, j : j + 1] == lane, logits, 0.0), axis=1, keepdims=True)
        for j in range(2)
    ]
    top = jnp.maximum(chosen[0], chosen[1])
    e0, e1 = jnp.exp(chosen[0] - top), jnp.exp(chosen[1] - top)
    gates[:, 0:1] = e0 / (e0 + e1)
    gates[:, 1:2] = e1 / (e0 + e1)

    for r in range(5):
        for c in tiles[r]:
            c.wait()
        acc = jnp.zeros((512, 256), F32)
        for i in range(8):
            nb = idx[i]
            x = jnp.concatenate([xs[nb, core], xs[nb, 1 - core]], axis=1)
            at = slice(r * 256, (r + 1) * 256)
            w = jnp.concatenate([held[i, 0, at], held[i, 1, at]], axis=1)
            acc += nt_dot(x, w)
        if r == 4:
            kv_out[...] = acc.astype(BF16)
            continue
        for j in range(2):
            value = jnp.zeros((512, H), F32) if r == 0 else sel[j]
            for e in range(2):
                hit = routes[:, j : j + 1] == 2 * r + e
                value = jnp.where(hit, acc[:, e * H : (e + 1) * H], value)
            if r < 3:
                sel[j] = value
            else:
                for half in range(2):
                    at = (half * 2 + j) * 256
                    q_out[at : at + 256] = value[half * 256 : (half + 1) * 256].astype(BF16)


def project(idx, routes, router, own, other, blocks):
    return pl.pallas_call(
        project_kernel,
        out_shape=(
            jax.ShapeDtypeStruct((1024, H), BF16),
            jax.ShapeDtypeStruct((512, 2 * H), BF16),
            jax.ShapeDtypeStruct((512, 2), F32),
        ),
        in_specs=[SMEM, VMEM, VMEM] + [HBM] * 12,
        out_specs=(VMEM, VMEM, VMEM),
        scratch_shapes=[
            pltpu.VMEM((8, 2, 512, H), BF16),
            pltpu.VMEM((8, 2, 1280, H), BF16),
            pltpu.VMEM((2, 512, H), F32),
            pltpu.SemaphoreType.DMA((7,)),
        ],
        compiler_params=pltpu.CompilerParams(vmem_limit_bytes=20 << 20),
        cost_estimate=pl.CostEstimate(flops=6 << 30, bytes_accessed=8 << 20, transcendentals=0),
        name="project",
    )(idx, routes, router, own, other, *blocks)


def attend_kernel(idx, ends_s, ends_p, q0, q1, q2, q3, cache0, cache1, kv0, kv1, *refs):
    outs = refs[:4]
    q, keep, limits, top, tot, acc, sa, sb, chunk_of, tile_of, sem = refs[4:]
    core = idx[0]
    copies = [
        pltpu.make_async_copy(r, q.at[pl.ds(1024 * b, 1024)], sem.at[b])
        for b, r in enumerate((q0, q1, q2, q3))
    ]
    for i, r in enumerate((cache0, cache1)):
        for side in range(2):
            at = pl.multiple_of(i * 1536 + 768 * (core if side == 0 else 1 - core), 256)
            copies.append(
                pltpu.make_async_copy(r.at[side], keep.at[pl.ds(at, 768)], sem.at[4 + 2 * i + side])
            )
    for i, r in enumerate((kv0, kv1)):
        copies.append(
            pltpu.make_async_copy(r, keep.at[pl.ds(3072 + 512 * i, 512)], sem.at[8 + i])
        )
    for c in copies:
        c.start()

    se, pe = [ends_s[0]], [ends_p[0]]
    for k in range(1, 4):
        se.append(se[-1] + ends_s[k])
        pe.append(pe[-1] + ends_p[k])

    def allowed_of(token):
        lo, hi, own = 0 * token, 0 * token + pe[0], 0 * token
        for k in range(3):
            later = token >= se[k]
            lo = jnp.where(later, pe[k], lo)
            hi = jnp.where(later, pe[k + 1], hi)
            own = jnp.where(later, se[k], own)
        return lo, hi, own

    for t in range(TILES):
        first = idx[1 + t // 2] + (t % 2) * 256
        token = first + lax.rem(lax.broadcasted_iota(jnp.int32, (1, R), 1), 256)
        lo, hi, own = allowed_of(token)
        limits[t, 0:1] = lo
        limits[t, 1:2] = hi
        limits[t, 2:3] = own
        limits[t, 3:4] = token + 1
    limits[DUMMY] = jnp.zeros((4, R), jnp.int32)
    top[...] = jnp.full(top.shape, FLOOR, F32)
    tot[...] = jnp.zeros(tot.shape, F32)
    acc[...] = jnp.zeros(acc.shape, F32)

    def base_of(i):
        slot = jnp.where(i < 3, idx[5] + i * CK, idx[6] + (i - 3) * CK)
        return jnp.where(i < 6, slot, jnp.where(i == 6, idx[7], idx[8]))

    def collect(want_full, start):
        def visit(n, count):
            i, t = n // TILES, lax.rem(n, TILES)
            base = base_of(i)
            first = idx[1 + t // 2] + lax.rem(t, 2) * 256
            last = first + 255
            lo_a, hi_a, own_a = allowed_of(first)
            lo_b, hi_b, own_b = allowed_of(last)
            pre = i < 6
            lo_first, lo_last = jnp.where(pre, lo_a, own_a), jnp.where(pre, lo_b, own_b)
            hi_first, hi_last = jnp.where(pre, hi_a, first + 1), jnp.where(pre, hi_b, last + 1)
            some = (base + CK > lo_first) & (base < hi_last)
            full = (base >= lo_last) & (base + CK <= hi_first)
            hit = full if want_full else (some & jnp.logical_not(full))

            @pl.when(hit)
            def _():
                chunk_of[count] = i
                tile_of[count] = t

            return count + hit.astype(jnp.int32)

        count = lax.fori_loop(0, CHUNKS * TILES, visit, start)
        rounds = (count + UNROLL - 1) // UNROLL
        for k in range(UNROLL):
            chunk_of[count + k] = 0
            tile_of[count + k] = DUMMY
        return rounds

    full_rounds = collect(True, 0)
    all_rounds = collect(False, full_rounds * UNROLL)
    for c in copies:
        c.wait()
    q[4096:4608] = jnp.zeros((R, H), BF16)

    def scores(n, out):
        keys = keep[pl.ds(pl.multiple_of(chunk_of[n] * CK, CK), CK), :H]
        out[...] = nt_dot(keys, q[pl.ds(pl.multiple_of(tile_of[n] * R, R), R), :])

    def consume(n, s_ref, masked):
        i, t = chunk_of[n], tile_of[n]
        s = s_ref[...]
        if masked:
            pos = base_of(i) + lax.broadcasted_iota(jnp.int32, (CK, R), 0)
            kind = jnp.where(i < 6, 0, 2)
            lo, hi = limits[t, pl.ds(kind, 1)], limits[t, pl.ds(kind + 1, 1)]
            s = jnp.where((pos >= lo) & (pos < hi), s, -jnp.inf)
        old = top[t]
        new = jnp.maximum(old, jnp.max(s, axis=0, keepdims=True))
        p = jnp.exp2(s * SCALE2 - new * SCALE2)
        factor = jnp.exp2((old - new) * SCALE2)
        top[t] = new
        tot[t] = tot[t] * factor + jnp.sum(p, axis=0, keepdims=True)
        values = keep[pl.ds(pl.multiple_of(i * CK, CK), CK), H:]
        acc[t] = acc[t] * factor + lax.dot_general(
            values, p.astype(BF16), (((0,), (0,)), ((), ())), preferred_element_type=F32
        )

    def rounds(masked):
        def body(n, _):
            for k in range(UNROLL):
                cur, nxt = (sa, sb) if k % 2 == 0 else (sb, sa)
                scores(n * UNROLL + k + 1, nxt)
                consume(n * UNROLL + k, cur, masked)
            return 0

        return body

    chunk_of[all_rounds * UNROLL] = 0
    tile_of[all_rounds * UNROLL] = DUMMY
    scores(0, sa)
    lax.fori_loop(0, full_rounds, rounds(False), 0)
    lax.fori_loop(full_rounds, all_rounds, rounds(True), 0)

    for t in range(TILES):
        total = tot[t]
        safe = jnp.where(total > 0.0, total, 1.0)
        cols = slice((t % 2) * R, (t % 2 + 1) * R)
        out = outs[t // 2]
        out[0:H, cols] = (acc[t] / safe).astype(BF16)
        lse = jnp.where(total > 0.0, top[t] * SCALE2 + jnp.log2(safe), FLOOR)
        high = lse.astype(BF16).astype(F32)
        mid = (lse - high).astype(BF16).astype(F32)
        low = lse - high - mid
        row = lax.broadcasted_iota(jnp.int32, (16, R), 0)
        packed = jnp.where(row == 0, high, jnp.where(row == 1, mid, jnp.where(row == 2, low, 0.0)))
        out[H : H + 16, cols] = packed.astype(BF16)


def attend(idx, suffix_lengths, prefix_lengths, qs, caches, kvs):
    return pl.pallas_call(
        attend_kernel,
        out_shape=tuple(jax.ShapeDtypeStruct((H + 16, 1024), BF16) for _ in range(4)),
        in_specs=[SMEM] * 3 + [HBM] * 8,
        out_specs=tuple([VMEM] * 4),
        scratch_shapes=[
            pltpu.VMEM((9 * R, H), BF16),
            pltpu.VMEM((CHUNKS * CK, 2 * H), BF16),
            pltpu.VMEM((TILES + 1, 4, R), jnp.int32),
            pltpu.VMEM((TILES + 1, 1, R), F32),
            pltpu.VMEM((TILES + 1, 1, R), F32),
            pltpu.VMEM((TILES + 1, H, R), F32),
            pltpu.VMEM((CK, R), F32),
            pltpu.VMEM((CK, R), F32),
            pltpu.SMEM((CHUNKS * TILES + 4 * UNROLL,), jnp.int32),
            pltpu.SMEM((CHUNKS * TILES + 4 * UNROLL,), jnp.int32),
            pltpu.SemaphoreType.DMA((10,)),
        ],
        compiler_params=pltpu.CompilerParams(vmem_limit_bytes=20 << 20),
        cost_estimate=pl.CostEstimate(
            flops=12 << 30, bytes_accessed=6 << 20, transcendentals=10 << 20
        ),
        name="attend",
    )(idx, suffix_lengths, prefix_lengths, *qs, *caches, *kvs)


def combine_kernel(gates, p0, p1, p2, p3, out):
    parts = (p0, p1, p2, p3)
    lses = []
    for p in parts:
        rows = p[H : H + 16].astype(F32)
        lses.append(rows[0:1] + rows[1:2] + rows[2:3])
    high = jnp.maximum(jnp.maximum(lses[0], lses[1]), jnp.maximum(lses[2], lses[3]))
    share = [jnp.exp2(v - high) for v in lses]
    norm = gates[...] / (share[0] + share[1] + share[2] + share[3])
    for at in range(0, 1024, 256):
        cols = slice(at, at + 256)
        total = jnp.zeros((H, 256), F32)
        for p, s in zip(parts, share):
            total += p[0:H, cols].astype(F32) * s[:, cols]
        out[cols] = jnp.transpose(total * norm[:, cols]).astype(BF16)


def combine(gates, parts):
    return pl.pallas_call(
        combine_kernel,
        out_shape=jax.ShapeDtypeStruct((1024, H), BF16),
        in_specs=[VMEM] * 5,
        out_specs=VMEM,
        compiler_params=pltpu.CompilerParams(vmem_limit_bytes=8 << 20),
        cost_estimate=pl.CostEstimate(flops=1 << 22, bytes_accessed=2 << 20, transcendentals=0),
        name="combine",
    )(gates, *parts)


def out_kernel(idx, routes, own, other, *refs):
    blocks = refs[:10]
    outs = refs[10:14]
    held, padded, sem = refs[14:]
    core = idx[8]
    copies = []
    for k in range(10):
        if k < 6:
            src, dst = blocks[k], held.at[idx[k]]
        else:
            src, dst = blocks[k], held.at[idx[6 + (k - 6) // 2], (k - 6) % 2]
        copies.append(pltpu.make_async_copy(src, dst, sem.at[k]))
    for c in copies:
        c.start()
    for side, source in enumerate((own, other)):
        for half in range(2):
            for e in range(E):
                value = jnp.zeros((256, H), F32)
                for j in range(2):
                    hit = routes[half * 256 : (half + 1) * 256, j : j + 1] == e
                    at = (half * 2 + j) * 256
                    value = jnp.where(hit, source[at : at + 256].astype(F32), value)
                padded[side, half * 256 : (half + 1) * 256, e * H : (e + 1) * H] = value.astype(
                    BF16
                )
    for c in copies:
        c.wait()
    for dz in range(4):
        value = jnp.zeros((512, 256), F32)
        for side in range(2):
            head = core if side == 0 else 1 - core
            w = jnp.concatenate(
                [held[idx[9 + 2 * dz], head], held[idx[10 + 2 * dz], head]], axis=1
            )
            value += jnp.dot(padded[side], w, preferred_element_type=F32)
        for s in range(2):
            outs[dz][s] = value[:, s * H : (s + 1) * H].astype(outs[dz].dtype)


def project_out(idx, routes, own, other, blocks):
    return pl.pallas_call(
        out_kernel,
        out_shape=(jax.ShapeDtypeStruct((2, 512, H), F32),)
        + tuple(jax.ShapeDtypeStruct((2, 512, H), BF16) for _ in range(3)),
        in_specs=[SMEM, VMEM, VMEM, VMEM] + [HBM] * 10,
        out_specs=tuple([VMEM] * 4),
        scratch_shapes=[
            pltpu.VMEM((8, 2, 1024, H), BF16),
            pltpu.VMEM((2, 512, 1024), BF16),
            pltpu.SemaphoreType.DMA((10,)),
        ],
        compiler_params=pltpu.CompilerParams(vmem_limit_bytes=20 << 20),
        cost_estimate=pl.CostEstimate(flops=4 << 30, bytes_accessed=6 << 20, transcendentals=0),
        name="project_out",
    )(idx, routes, own, other, *blocks)


def on_device(
    tokens,
    norm_gain,
    router,
    routes,
    kv_weight,
    query_weight,
    out_weight,
    prefix_cache,
    suffix_lengths,
    prefix_lengths,
):
    xl, y, c = (lax.axis_index(a) for a in WIDE)
    z, xh = (lax.axis_index(a) for a in NARROW)
    first_core = c == 0
    chips = chip_order()

    def table(values):
        return jnp.stack([jnp.asarray(v, jnp.int32) for v in values])

    def head_rows(w, h):
        rows = w.shape[0] // 2
        return lax.dynamic_slice_in_dim(w, h * rows, rows, 0)

    def weights_of(h):
        return jnp.concatenate([head_rows(query_weight, h), head_rows(kv_weight, h)], axis=0)

    pair = jnp.stack([tokens, across_far(tokens)])
    blocks = [pair] + [along_z(pair, k) for k in (1, 2, 3)]
    w = jnp.stack([weights_of(c), across_core(weights_of(1 - c))])
    gathered = gather_chips(w)
    other_routes = across_core(routes)
    both_routes = jnp.where(
        first_core,
        jnp.concatenate([routes, other_routes]),
        jnp.concatenate([other_routes, routes]),
    )

    def cache_of(h):
        return lax.dynamic_slice_in_dim(prefix_cache, h * 2 * H, 2 * H, 1)

    cache = jnp.stack([cache_of(c), across_core(cache_of(1 - c))])
    cache_out, gathered[1] = tie(cache, gathered[1])
    caches = [cache, across_x(cache_out)]

    token_src = [lax.rem(z + 4 - dz, 4) * 2 + (xh ^ s) for dz in range(4) for s in range(2)]
    normed = normalise(table(token_src), norm_gain.reshape(8, 1, 256), blocks)
    q, kv, gates = project(
        table(chips + [c]),
        both_routes,
        router.reshape(8, 2, H, E),
        normed,
        across_core(normed),
        gathered,
    )
    out_weight, q = tie(out_weight, q)
    out_blocks = gather_chips(out_weight.reshape(2, 1024, H))

    kvs = [kv, across_x(kv)]
    qs = [q] + [along_y(q, k) for k in (1, 2, 3)]
    firsts = [(xl * 4 + lax.rem(y + 4 - k, 4)) * 512 for k in range(4)]
    mine, partner = xl * 4 + y, (1 - xl) * 4 + y
    at = [c] + firsts + [mine * 1536, partner * 1536, mine * 512, partner * 512]
    parts = list(attend(table(at), suffix_lengths, prefix_lengths, qs, caches, kvs))
    for k in range(1, 4):
        parts[k] = along_y(parts[k], 4 - k)
    gate_row = gates.reshape(2, 256, 2).transpose(0, 2, 1).reshape(1, 1024)
    attended = combine(gate_row, parts)

    dests = [lax.rem(z + dz, 4) * 2 + (xh ^ s) for dz in range(4) for s in range(2)]
    sums = project_out(
        table(chips + [c] + dests), both_routes, attended, across_core(attended), out_blocks
    )
    total = sums[0]
    for k in (1, 2, 3):
        total = total + along_z(sums[k], k).astype(F32)
    total = total[0] + across_far(total[1].astype(BF16)).astype(F32)
    here = lax.dynamic_slice_in_dim(total, c * 256, 256, 0).astype(BF16)
    there = lax.dynamic_slice_in_dim(total, (1 - c) * 256, 256, 0).astype(BF16)
    there = across_core(there)
    return jnp.where(
        first_core,
        jnp.concatenate([here, there], axis=1),
        jnp.concatenate([there, here], axis=1),
    )


def solution(mesh):
    fine = Mesh(mesh.devices.reshape(SIZES), AXES)
    placed = (
        P(WIDE, NARROW),
        P(),
        P(),
        P(WIDE, None),
        P(NARROW, WIDE),
        P(NARROW, WIDE),
        P(NARROW, WIDE),
        P(WIDE, NARROW),
        P(),
        P(),
    )
    return jax.shard_map(
        on_device, mesh=fine, in_specs=placed, out_specs=P(WIDE, NARROW), check_vma=False
    )
```

```python
import functools
import math

import jax
import jax.numpy as jnp
from jax import lax
from jax.experimental import pallas as pl
from jax.experimental.pallas import tpu as pltpu
from jax.sharding import Mesh
from jax.sharding import PartitionSpec as P

H = 128
E = 8
EPS = 1e-06
FLOOR = -1e30
AXES = ("xl", "y", "c", "z", "xh")
SIZES = (2, 4, 2, 4, 2)
WIDE = ("xl", "y", "c")
NARROW = ("z", "xh")
BF16 = jnp.bfloat16
F32 = jnp.float32
SCALE2 = H ** (-0.5) * math.log2(math.e)
CK = 512
R = 512
CHUNKS = 8
TILES = 8
DUMMY = 8
UNROLL = 4

SMEM = pl.BlockSpec(memory_space=pltpu.SMEM)
VMEM = pl.BlockSpec(memory_space=pltpu.VMEM)
HBM = pl.BlockSpec(memory_space=pltpu.HBM)
ANY = pl.BlockSpec(memory_space=pl.ANY)


def along_y(x, k):
    return lax.ppermute(x, "y", [(i, (i + k) % 4) for i in range(4)])


def along_z(x, k):
    return lax.ppermute(x, "z", [(i, (i + k) % 4) for i in range(4)])


def across_x(x):
    return lax.ppermute(x, "xl", [(0, 1), (1, 0)])


def across_far(x):
    return lax.ppermute(x, "xh", [(0, 1), (1, 0)])


def across_core(x):
    return lax.ppermute(x, "c", [(0, 1), (1, 0)])


def tie(a, b):
    return lax.optimization_barrier((a, b))


def gather_parts(w0, w1):
    ym0, yp0, a0 = along_y(w0, 3), along_y(w0, 1), across_x(w0)
    ym1, yp1, a1 = along_y(w1, 3), along_y(w1, 1), across_x(w1)
    far0, far1 = along_y(yp0, 1), along_y(ym1, 3)
    am0, ap0 = along_y(a0, 3), along_y(a0, 1)
    am1, ap1 = along_y(a1, 3), along_y(a1, 1)
    afar0, afar1 = across_x(far0), across_x(far1)
    pairs = [(w0, w1), (a0, a1), (ym0, ym1), (am0, am1), (far0, far1), (afar0, afar1), (yp0, yp1), (ap0, ap1)]
    return [part for pair in pairs for part in pair]


def chip_order():
    xl, y = lax.axis_index("xl"), lax.axis_index("y")
    return [(xl ^ dx) * 4 + lax.rem(y + dy, 4) for dy in range(4) for dx in range(2)]


def pin(arrays):
    return [pltpu.with_memory_space_constraint(a, pltpu.HBM) for a in arrays]


def nt_dot(a, b):
    return lax.dot_general(a, b, (((1,), (1,)), ((), ())), preferred_element_type=F32)


def run(copies):
    for c in copies:
        c.start()
    for c in copies:
        c.wait()


def norm_kernel(idx, gain, b0, b1, b2, b3, normed, held, sem):
    refs = (b0, b1, b2, b3)
    run([pltpu.make_async_copy(r, held.at[i], sem.at[i]) for i, r in enumerate(refs)])
    total = jnp.zeros((256, 1), F32)
    for k in range(8):
        v = held[k // 2, k % 2].astype(F32)
        total = total + jnp.sum(v * v, axis=1, keepdims=True)
    scale = lax.rsqrt(total * (1.0 / 2048) + EPS)
    for k in range(8):
        v = held[k // 2, k % 2].astype(F32) * scale * gain[idx[k]].astype(F32)
        normed[:, pl.ds(pl.multiple_of(idx[8 + k] * 256, 256), 256)] = v.astype(BF16)


def normalise(idx, gain, blocks):
    return pl.pallas_call(
        norm_kernel,
        out_shape=jax.ShapeDtypeStruct((256, 2048), BF16),
        in_specs=[SMEM, VMEM] + [HBM] * 4,
        out_specs=VMEM,
        scratch_shapes=[pltpu.VMEM((4, 2, 256, 256), BF16), pltpu.SemaphoreType.DMA((4,))],
        compiler_params=pltpu.CompilerParams(vmem_limit_bytes=8 << 20),
        cost_estimate=pl.CostEstimate(flops=1 << 24, bytes_accessed=2 << 20, transcendentals=0),
        name="normalise",
    )(idx, gain, *blocks)


GROUPS = ((0, 512), (512, 768))


def project_kernel(idx, routes, router, own, other, *refs):
    blocks = refs[:16]
    q_out, kv_out, gates, xs, held, sel, sem = refs[16:]
    core = idx[8]
    copies = []
    for i, r in enumerate((own, other)):
        at = pl.multiple_of((core if i == 0 else 1 - core) * 256, 256)
        copies.append(pltpu.make_async_copy(r, xs.at[pl.ds(at, 256)], sem.at[32 + i]))
    for g, (start, rows) in enumerate(GROUPS):
        for k in range(16):
            lane = (k // 2) * 256 + H * (core if k % 2 == 0 else 1 - core)
            at = pl.ds(pl.multiple_of(lane, H), H)
            copies.append(
                pltpu.make_async_copy(
                    blocks[k].at[pl.ds(start, rows)],
                    held.at[pl.ds(start, rows), at],
                    sem.at[16 * g + k],
                )
            )
    for c in copies:
        c.start()
    for c in copies[:2]:
        c.wait()
    logits = jnp.zeros((512, E), F32)
    for i in range(8):
        part = router[:, pl.ds(pl.multiple_of(idx[i] * 256, 256), 256)]
        logits += nt_dot(xs[:, i * 256 : (i + 1) * 256], part)
    lane = lax.broadcasted_iota(jnp.int32, (512, E), 1)
    chosen = [
        jnp.sum(jnp.where(routes[:, j : j + 1] == lane, logits, 0.0), axis=1, keepdims=True)
        for j in range(2)
    ]
    top = jnp.maximum(chosen[0], chosen[1])
    e0, e1 = jnp.exp(chosen[0] - top), jnp.exp(chosen[1] - top)
    gates[:, 0:1] = e0 / (e0 + e1)
    gates[:, 1:2] = e1 / (e0 + e1)

    for r in range(5):
        if r == 0:
            for c in copies[2:18]:
                c.wait()
        if r == 2:
            for c in copies[18:]:
                c.wait()
        acc = nt_dot(xs[...], held[r * 256 : (r + 1) * 256])
        if r == 4:
            kv_out[...] = acc.astype(BF16)
            continue
        for j in range(2):
            value = jnp.zeros((512, H), F32) if r == 0 else sel[j]
            for e in range(2):
                hit = routes[:, j : j + 1] == 2 * r + e
                value = jnp.where(hit, acc[:, e * H : (e + 1) * H], value)
            if r < 3:
                sel[j] = value
            else:
                for half in range(2):
                    at = (half * 2 + j) * 256
                    q_out[at : at + 256] = value[half * 256 : (half + 1) * 256].astype(BF16)


def project(idx, routes, router, own, other, blocks):
    return pl.pallas_call(
        project_kernel,
        out_shape=(
            jax.ShapeDtypeStruct((1024, H), BF16),
            jax.ShapeDtypeStruct((512, 2 * H), BF16),
            jax.ShapeDtypeStruct((512, 2), F32),
        ),
        in_specs=[SMEM, VMEM, VMEM] + [HBM] * 18,
        out_specs=(VMEM, VMEM, VMEM),
        scratch_shapes=[
            pltpu.VMEM((512, 2048), BF16),
            pltpu.VMEM((1280, 2048), BF16),
            pltpu.VMEM((2, 512, H), F32),
            pltpu.SemaphoreType.DMA((34,)),
        ],
        compiler_params=pltpu.CompilerParams(vmem_limit_bytes=20 << 20),
        cost_estimate=pl.CostEstimate(flops=6 << 30, bytes_accessed=8 << 20, transcendentals=0),
        name="project",
    )(idx, routes, router, *pin([own, other, *blocks]))


def attend_kernel(idx, ends_s, ends_p, q0, q1, q2, q3, cache0, cache1, kv0, kv1, *refs):
    outs = refs[:4]
    q, keep, limits, top, tot, acc, sa, sb, chunk_of, tile_of, sem = refs[4:]
    core = idx[0]
    copies = [
        pltpu.make_async_copy(r, q.at[pl.ds(1024 * b, 1024)], sem.at[b])
        for b, r in enumerate((q0, q1, q2, q3))
    ]
    for i, r in enumerate((cache0, cache1)):
        for side in range(2):
            at = pl.multiple_of(i * 1536 + 768 * (core if side == 0 else 1 - core), 256)
            copies.append(
                pltpu.make_async_copy(r.at[side], keep.at[pl.ds(at, 768)], sem.at[4 + 2 * i + side])
            )
    for i, r in enumerate((kv0, kv1)):
        copies.append(
            pltpu.make_async_copy(r, keep.at[pl.ds(3072 + 512 * i, 512)], sem.at[8 + i])
        )
    for c in copies:
        c.start()

    se, pe = [ends_s[0]], [ends_p[0]]
    for k in range(1, 4):
        se.append(se[-1] + ends_s[k])
        pe.append(pe[-1] + ends_p[k])

    def allowed_of(token):
        lo, hi, own = 0 * token, 0 * token + pe[0], 0 * token
        for k in range(3):
            later = token >= se[k]
            lo = jnp.where(later, pe[k], lo)
            hi = jnp.where(later, pe[k + 1], hi)
            own = jnp.where(later, se[k], own)
        return lo, hi, own

    for t in range(TILES):
        first = idx[1 + t // 2] + (t % 2) * 256
        token = first + lax.rem(lax.broadcasted_iota(jnp.int32, (1, R), 1), 256)
        lo, hi, own = allowed_of(token)
        limits[t, 0:1] = lo
        limits[t, 1:2] = hi
        limits[t, 2:3] = own
        limits[t, 3:4] = token + 1
    limits[DUMMY] = jnp.zeros((4, R), jnp.int32)
    top[...] = jnp.full(top.shape, FLOOR, F32)
    tot[...] = jnp.zeros(tot.shape, F32)
    acc[...] = jnp.zeros(acc.shape, F32)

    def base_of(i):
        slot = jnp.where(i < 3, idx[5] + i * CK, idx[6] + (i - 3) * CK)
        return jnp.where(i < 6, slot, jnp.where(i == 6, idx[7], idx[8]))

    def collect(want_full, start):
        def visit(n, count):
            i, t = n // TILES, lax.rem(n, TILES)
            base = base_of(i)
            first = idx[1 + t // 2] + lax.rem(t, 2) * 256
            last = first + 255
            lo_a, hi_a, own_a = allowed_of(first)
            lo_b, hi_b, own_b = allowed_of(last)
            pre = i < 6
            lo_first, lo_last = jnp.where(pre, lo_a, own_a), jnp.where(pre, lo_b, own_b)
            hi_first, hi_last = jnp.where(pre, hi_a, first + 1), jnp.where(pre, hi_b, last + 1)
            some = (base + CK > lo_first) & (base < hi_last)
            full = (base >= lo_last) & (base + CK <= hi_first)
            hit = full if want_full else (some & jnp.logical_not(full))

            @pl.when(hit)
            def _():
                chunk_of[count] = i
                tile_of[count] = t

            return count + hit.astype(jnp.int32)

        count = lax.fori_loop(0, CHUNKS * TILES, visit, start)
        rounds = (count + UNROLL - 1) // UNROLL
        for k in range(UNROLL):
            chunk_of[count + k] = 0
            tile_of[count + k] = DUMMY
        return rounds

    full_rounds = collect(True, 0)
    all_rounds = collect(False, full_rounds * UNROLL)
    for c in copies:
        c.wait()
    q[4096:4608] = jnp.zeros((R, H), BF16)

    def scores(n, out):
        keys = keep[pl.ds(pl.multiple_of(chunk_of[n] * CK, CK), CK), :H]
        out[...] = nt_dot(keys, q[pl.ds(pl.multiple_of(tile_of[n] * R, R), R), :])

    def consume(n, s_ref, masked):
        i, t = chunk_of[n], tile_of[n]
        s = s_ref[...]
        if masked:
            pos = base_of(i) + lax.broadcasted_iota(jnp.int32, (CK, R), 0)
            kind = jnp.where(i < 6, 0, 2)
            lo, hi = limits[t, pl.ds(kind, 1)], limits[t, pl.ds(kind + 1, 1)]
            s = jnp.where((pos >= lo) & (pos < hi), s, -jnp.inf)
        old = top[t]
        new = jnp.maximum(old, jnp.max(s, axis=0, keepdims=True))
        p = jnp.exp2(s * SCALE2 - new * SCALE2)
        factor = jnp.exp2((old - new) * SCALE2)
        top[t] = new
        tot[t] = tot[t] * factor + jnp.sum(p, axis=0, keepdims=True)
        values = keep[pl.ds(pl.multiple_of(i * CK, CK), CK), H:]
        acc[t] = acc[t] * factor + lax.dot_general(
            values, p.astype(BF16), (((0,), (0,)), ((), ())), preferred_element_type=F32
        )

    def rounds(masked):
        def body(n, _):
            for k in range(UNROLL):
                cur, nxt = (sa, sb) if k % 2 == 0 else (sb, sa)
                scores(n * UNROLL + k + 1, nxt)
                consume(n * UNROLL + k, cur, masked)
            return 0

        return body

    chunk_of[all_rounds * UNROLL] = 0
    tile_of[all_rounds * UNROLL] = DUMMY
    scores(0, sa)
    lax.fori_loop(0, full_rounds, rounds(False), 0)
    lax.fori_loop(full_rounds, all_rounds, rounds(True), 0)

    for t in range(TILES):
        total = tot[t]
        safe = jnp.where(total > 0.0, total, 1.0)
        cols = slice((t % 2) * R, (t % 2 + 1) * R)
        out = outs[t // 2]
        out[0:H, cols] = (acc[t] / safe).astype(BF16)
        lse = jnp.where(total > 0.0, top[t] * SCALE2 + jnp.log2(safe), FLOOR)
        high = lse.astype(BF16).astype(F32)
        mid = (lse - high).astype(BF16).astype(F32)
        low = lse - high - mid
        row = lax.broadcasted_iota(jnp.int32, (16, R), 0)
        packed = jnp.where(row == 0, high, jnp.where(row == 1, mid, jnp.where(row == 2, low, 0.0)))
        out[H : H + 16, cols] = packed.astype(BF16)


def attend(idx, suffix_lengths, prefix_lengths, qs, caches, kvs):
    return pl.pallas_call(
        attend_kernel,
        out_shape=tuple(jax.ShapeDtypeStruct((H + 16, 1024), BF16) for _ in range(4)),
        in_specs=[SMEM] * 3 + [HBM] * 8,
        out_specs=tuple([VMEM] * 4),
        scratch_shapes=[
            pltpu.VMEM((9 * R, H), BF16),
            pltpu.VMEM((CHUNKS * CK, 2 * H), BF16),
            pltpu.VMEM((TILES + 1, 4, R), jnp.int32),
            pltpu.VMEM((TILES + 1, 1, R), F32),
            pltpu.VMEM((TILES + 1, 1, R), F32),
            pltpu.VMEM((TILES + 1, H, R), F32),
            pltpu.VMEM((CK, R), F32),
            pltpu.VMEM((CK, R), F32),
            pltpu.SMEM((CHUNKS * TILES + 4 * UNROLL,), jnp.int32),
            pltpu.SMEM((CHUNKS * TILES + 4 * UNROLL,), jnp.int32),
            pltpu.SemaphoreType.DMA((10,)),
        ],
        compiler_params=pltpu.CompilerParams(vmem_limit_bytes=20 << 20),
        cost_estimate=pl.CostEstimate(
            flops=12 << 30, bytes_accessed=6 << 20, transcendentals=10 << 20
        ),
        name="attend",
    )(idx, suffix_lengths, prefix_lengths, *pin([*qs, *caches, *kvs]))


def combine_kernel(gates, p0, p1, p2, p3, out):
    parts = (p0, p1, p2, p3)
    lses = []
    for p in parts:
        rows = p[H : H + 16].astype(F32)
        lses.append(rows[0:1] + rows[1:2] + rows[2:3])
    high = jnp.maximum(jnp.maximum(lses[0], lses[1]), jnp.maximum(lses[2], lses[3]))
    share = [jnp.exp2(v - high) for v in lses]
    norm = gates[...] / (share[0] + share[1] + share[2] + share[3])
    for at in range(0, 1024, 256):
        cols = slice(at, at + 256)
        total = jnp.zeros((H, 256), F32)
        for p, s in zip(parts, share):
            total += p[0:H, cols].astype(F32) * s[:, cols]
        out[cols] = jnp.transpose(total * norm[:, cols]).astype(BF16)


def combine(gates, parts):
    return pl.pallas_call(
        combine_kernel,
        out_shape=jax.ShapeDtypeStruct((1024, H), BF16),
        in_specs=[VMEM] * 5,
        out_specs=VMEM,
        compiler_params=pltpu.CompilerParams(vmem_limit_bytes=8 << 20),
        cost_estimate=pl.CostEstimate(flops=1 << 22, bytes_accessed=2 << 20, transcendentals=0),
        name="combine",
    )(gates, *parts)


def out_kernel(idx, routes, own, other, *refs):
    blocks = refs[:8]
    outs = refs[8:12]
    held, padded, sem = refs[12:]
    core = idx[8]
    copies = [
        pltpu.make_async_copy(r, held.at[idx[k]], sem.at[k]) for k, r in enumerate(blocks)
    ]
    for c in copies:
        c.start()
    for side, source in enumerate((own, other)):
        for half in range(2):
            for e in range(E):
                value = jnp.zeros((256, H), F32)
                for j in range(2):
                    hit = routes[half * 256 : (half + 1) * 256, j : j + 1] == e
                    at = (half * 2 + j) * 256
                    value = jnp.where(hit, source[at : at + 256].astype(F32), value)
                padded[side, half * 256 : (half + 1) * 256, e * H : (e + 1) * H] = value.astype(
                    BF16
                )
    for c in copies:
        c.wait()
    for dz in range(4):
        value = jnp.zeros((512, 256), F32)
        for side in range(2):
            head = core if side == 0 else 1 - core
            rows = pl.ds(pl.multiple_of(head * 1024, 1024), 1024)
            w = jnp.concatenate(
                [held[idx[9 + 2 * dz], rows], held[idx[10 + 2 * dz], rows]], axis=1
            )
            value += jnp.dot(padded[side], w, preferred_element_type=F32)
        for s in range(2):
            outs[dz][s] = value[:, s * H : (s + 1) * H].astype(outs[dz].dtype)


def project_out(idx, routes, own, other, blocks):
    return pl.pallas_call(
        out_kernel,
        out_shape=(jax.ShapeDtypeStruct((2, 512, H), F32),)
        + tuple(jax.ShapeDtypeStruct((2, 512, H), BF16) for _ in range(3)),
        in_specs=[SMEM, VMEM, VMEM, VMEM] + [HBM] * 8,
        out_specs=tuple([VMEM] * 4),
        scratch_shapes=[
            pltpu.VMEM((8, 2048, H), BF16),
            pltpu.VMEM((2, 512, 1024), BF16),
            pltpu.SemaphoreType.DMA((8,)),
        ],
        compiler_params=pltpu.CompilerParams(vmem_limit_bytes=20 << 20),
        cost_estimate=pl.CostEstimate(flops=4 << 30, bytes_accessed=6 << 20, transcendentals=0),
        name="project_out",
    )(idx, routes, own, other, *pin(blocks))


def on_device(
    tokens,
    norm_gain,
    router,
    routes,
    kv_weight,
    query_weight,
    out_weight,
    prefix_cache,
    suffix_lengths,
    prefix_lengths,
):
    xl, y, c = (lax.axis_index(a) for a in WIDE)
    z, xh = (lax.axis_index(a) for a in NARROW)
    first_core = c == 0
    chips = chip_order()

    def table(values):
        return jnp.stack([jnp.asarray(v, jnp.int32) for v in values])

    def head_rows(w, h):
        rows = w.shape[0] // 2
        return lax.dynamic_slice_in_dim(w, h * rows, rows, 0)

    def weights_of(h):
        return jnp.concatenate([head_rows(query_weight, h), head_rows(kv_weight, h)], axis=0)

    gathered = gather_parts(weights_of(c), across_core(weights_of(1 - c)))
    pair = jnp.stack([tokens, across_far(tokens)])
    blocks = [pair] + [along_z(pair, k) for k in (1, 2, 3)]
    other_routes = across_core(routes)
    both_routes = jnp.where(
        first_core,
        jnp.concatenate([routes, other_routes]),
        jnp.concatenate([other_routes, routes]),
    )

    def cache_of(h):
        return lax.dynamic_slice_in_dim(prefix_cache, h * 2 * H, 2 * H, 1)

    cache = jnp.stack([cache_of(c), across_core(cache_of(1 - c))])
    cache_out, gathered[2] = tie(cache, gathered[2])
    caches = [cache, across_x(cache_out)]

    token_src = [lax.rem(z + 4 - dz, 4) * 2 + (xh ^ s) for dz in range(4) for s in range(2)]
    places = [lax.rem(lax.rem(v, 4) + 4 - y, 4) * 2 + (v // 4 ^ xl) for v in token_src]
    normed = normalise(table(token_src + places), norm_gain.reshape(8, 1, 256), blocks)
    out_early, gathered[7] = tie(out_weight, gathered[7])
    o_ym, o_yp, o_a = along_y(out_early, 3), along_y(out_early, 1), across_x(out_early)
    q, kv, gates = project(
        table(chips + [c]), both_routes, router.T, normed, across_core(normed), gathered
    )
    kvs = [kv, across_x(kv)]
    q_out, o_a, o_ym, o_yp = lax.optimization_barrier((q, o_a, o_ym, o_yp))
    qs = [q] + [along_y(q_out, k) for k in (1, 2, 3)]
    out_late, o_a_late, qs[2] = lax.optimization_barrier((out_weight, o_a, qs[2]))
    o_far, o_am, o_ap = along_y(out_late, 2), along_y(o_a_late, 3), along_y(o_a_late, 1)

    firsts = [(xl * 4 + lax.rem(y + 4 - k, 4)) * 512 for k in range(4)]
    mine, partner = xl * 4 + y, (1 - xl) * 4 + y
    at = [c] + firsts + [mine * 1536, partner * 1536, mine * 512, partner * 512]
    parts = list(attend(table(at), suffix_lengths, prefix_lengths, qs, caches, kvs))
    parts[1:], o_far, o_am, o_ap = lax.optimization_barrier((parts[1:], o_far, o_am, o_ap))
    for k in range(1, 4):
        parts[k] = along_y(parts[k], 4 - k)
    out_blocks = [out_weight, o_a, o_ym, o_am, o_far, across_x(o_far), o_yp, o_ap]
    gate_row = gates.reshape(2, 256, 2).transpose(0, 2, 1).reshape(1, 1024)
    attended = combine(gate_row, parts)

    dests = [lax.rem(z + dz, 4) * 2 + (xh ^ s) for dz in range(4) for s in range(2)]
    sums = project_out(
        table(chips + [c] + dests), both_routes, attended, across_core(attended), out_blocks
    )
    total = sums[0]
    for k in (1, 2, 3):
        total = total + along_z(sums[k], k).astype(F32)
    total = total[0] + across_far(total[1].astype(BF16)).astype(F32)
    here = lax.dynamic_slice_in_dim(total, c * 256, 256, 0).astype(BF16)
    there = lax.dynamic_slice_in_dim(total, (1 - c) * 256, 256, 0).astype(BF16)
    there = across_core(there)
    return jnp.where(
        first_core,
        jnp.concatenate([here, there], axis=1),
        jnp.concatenate([there, here], axis=1),
    )


def solution(mesh):
    fine = Mesh(mesh.devices.reshape(SIZES), AXES)
    placed = (
        P(WIDE, NARROW),
        P(),
        P(),
        P(WIDE, None),
        P(NARROW, WIDE),
        P(NARROW, WIDE),
        P(NARROW, WIDE),
        P(WIDE, NARROW),
        P(),
        P(),
    )
    return jax.shard_map(
        on_device, mesh=fine, in_specs=placed, out_specs=P(WIDE, NARROW), check_vma=False
    )
```

```python
import functools
import math

import jax
import jax.numpy as jnp
from jax import lax
from jax.experimental import pallas as pl
from jax.experimental.pallas import tpu as pltpu
from jax.sharding import Mesh
from jax.sharding import PartitionSpec as P

H = 128
E = 8
EPS = 1e-06
FLOOR = -1e30
AXES = ("xl", "y", "c", "z", "xh")
SIZES = (2, 4, 2, 4, 2)
WIDE = ("xl", "y", "c")
NARROW = ("z", "xh")
BF16 = jnp.bfloat16
F32 = jnp.float32
SCALE2 = H ** (-0.5) * math.log2(math.e)
CK = 512
R = 512
CHUNKS = 8
TILES = 8
DUMMY = 8
UNROLL = 4

SMEM = pl.BlockSpec(memory_space=pltpu.SMEM)
VMEM = pl.BlockSpec(memory_space=pltpu.VMEM)
HBM = pl.BlockSpec(memory_space=pltpu.HBM)
ANY = pl.BlockSpec(memory_space=pl.ANY)


def along_y(x, k):
    return lax.ppermute(x, "y", [(i, (i + k) % 4) for i in range(4)])


def along_z(x, k):
    return lax.ppermute(x, "z", [(i, (i + k) % 4) for i in range(4)])


def across_x(x):
    return lax.ppermute(x, "xl", [(0, 1), (1, 0)])


def across_far(x):
    return lax.ppermute(x, "xh", [(0, 1), (1, 0)])


def across_core(x):
    return lax.ppermute(x, "c", [(0, 1), (1, 0)])


def tie(a, b):
    return lax.optimization_barrier((a, b))


def first_step(w):
    return along_y(w, 3), along_y(w, 1), across_x(w)


def gather_parts(w0, w1, step0, step1):
    ym0, yp0, a0 = step0
    ym1, yp1, a1 = step1
    far0, far1 = along_y(yp0, 1), along_y(ym1, 3)
    am0, ap0 = along_y(a0, 3), along_y(a0, 1)
    am1, ap1 = along_y(a1, 3), along_y(a1, 1)
    afar0, afar1 = across_x(far0), across_x(far1)
    pairs = [(w0, w1), (a0, a1), (ym0, ym1), (am0, am1), (far0, far1), (afar0, afar1), (yp0, yp1), (ap0, ap1)]
    return [part for pair in pairs for part in pair]


def chip_order():
    xl, y = lax.axis_index("xl"), lax.axis_index("y")
    return [(xl ^ dx) * 4 + lax.rem(y + dy, 4) for dy in range(4) for dx in range(2)]


def pin(arrays):
    return [pltpu.with_memory_space_constraint(a, pltpu.HBM) for a in arrays]


def nt_dot(a, b):
    return lax.dot_general(a, b, (((1,), (1,)), ((), ())), preferred_element_type=F32)


def run(copies):
    for c in copies:
        c.start()
    for c in copies:
        c.wait()


def norm_kernel(idx, gain, b0, b1, b2, b3, normed, held, sem):
    refs = (b0, b1, b2, b3)
    run([pltpu.make_async_copy(r, held.at[i], sem.at[i]) for i, r in enumerate(refs)])
    total = jnp.zeros((256, 1), F32)
    for k in range(8):
        v = held[k // 2, k % 2].astype(F32)
        total = total + jnp.sum(v * v, axis=1, keepdims=True)
    scale = lax.rsqrt(total * (1.0 / 2048) + EPS)
    for k in range(8):
        v = held[k // 2, k % 2].astype(F32) * scale * gain[idx[k]].astype(F32)
        normed[:, pl.ds(pl.multiple_of(idx[8 + k] * 256, 256), 256)] = v.astype(BF16)


def normalise(idx, gain, blocks):
    return pl.pallas_call(
        norm_kernel,
        out_shape=jax.ShapeDtypeStruct((256, 2048), BF16),
        in_specs=[SMEM, VMEM] + [HBM] * 4,
        out_specs=VMEM,
        scratch_shapes=[pltpu.VMEM((4, 2, 256, 256), BF16), pltpu.SemaphoreType.DMA((4,))],
        compiler_params=pltpu.CompilerParams(vmem_limit_bytes=8 << 20),
        cost_estimate=pl.CostEstimate(flops=1 << 24, bytes_accessed=2 << 20, transcendentals=0),
        name="normalise",
    )(idx, gain, *blocks)


GROUPS = ((0, 512), (512, 768))


def project_kernel(idx, routes, router, own, other, *refs):
    blocks = refs[:16]
    q_out, kv_out, gates, xs, held, sel, sem = refs[16:]
    core = idx[8]
    copies = []
    for i, r in enumerate((own, other)):
        at = pl.multiple_of((core if i == 0 else 1 - core) * 256, 256)
        copies.append(pltpu.make_async_copy(r, xs.at[pl.ds(at, 256)], sem.at[32 + i]))
    for g, (start, rows) in enumerate(GROUPS):
        for k in range(16):
            lane = (k // 2) * 256 + H * (core if k % 2 == 0 else 1 - core)
            at = pl.ds(pl.multiple_of(lane, H), H)
            copies.append(
                pltpu.make_async_copy(
                    blocks[k].at[pl.ds(start, rows)],
                    held.at[pl.ds(start, rows), at],
                    sem.at[16 * g + k],
                )
            )
    for c in copies:
        c.start()
    for c in copies[:2]:
        c.wait()
    logits = jnp.zeros((512, E), F32)
    for i in range(8):
        part = router[:, pl.ds(pl.multiple_of(idx[i] * 256, 256), 256)]
        logits += nt_dot(xs[:, i * 256 : (i + 1) * 256], part)
    lane = lax.broadcasted_iota(jnp.int32, (512, E), 1)
    chosen = [
        jnp.sum(jnp.where(routes[:, j : j + 1] == lane, logits, 0.0), axis=1, keepdims=True)
        for j in range(2)
    ]
    top = jnp.maximum(chosen[0], chosen[1])
    e0, e1 = jnp.exp(chosen[0] - top), jnp.exp(chosen[1] - top)
    gates[:, 0:1] = e0 / (e0 + e1)
    gates[:, 1:2] = e1 / (e0 + e1)

    for r in range(5):
        if r == 0:
            for c in copies[2:18]:
                c.wait()
        if r == 2:
            for c in copies[18:]:
                c.wait()
        acc = nt_dot(xs[...], held[r * 256 : (r + 1) * 256])
        if r == 4:
            kv_out[...] = acc.astype(BF16)
            continue
        for j in range(2):
            value = jnp.zeros((512, H), F32) if r == 0 else sel[j]
            for e in range(2):
                hit = routes[:, j : j + 1] == 2 * r + e
                value = jnp.where(hit, acc[:, e * H : (e + 1) * H], value)
            if r < 3:
                sel[j] = value
            else:
                for half in range(2):
                    at = (half * 2 + j) * 256
                    q_out[at : at + 256] = value[half * 256 : (half + 1) * 256].astype(BF16)


def project(idx, routes, router, own, other, blocks):
    return pl.pallas_call(
        project_kernel,
        out_shape=(
            jax.ShapeDtypeStruct((1024, H), BF16),
            jax.ShapeDtypeStruct((512, 2 * H), BF16),
            jax.ShapeDtypeStruct((512, 2), F32),
        ),
        in_specs=[SMEM, VMEM, VMEM] + [HBM] * 18,
        out_specs=(VMEM, VMEM, VMEM),
        scratch_shapes=[
            pltpu.VMEM((512, 2048), BF16),
            pltpu.VMEM((1280, 2048), BF16),
            pltpu.VMEM((2, 512, H), F32),
            pltpu.SemaphoreType.DMA((34,)),
        ],
        compiler_params=pltpu.CompilerParams(vmem_limit_bytes=20 << 20),
        cost_estimate=pl.CostEstimate(flops=6 << 30, bytes_accessed=8 << 20, transcendentals=0),
        name="project",
    )(idx, routes, router, *pin([own, other, *blocks]))


def attend_kernel(idx, ends_s, ends_p, q0, q1, q2, q3, cache0, cache1, kv0, kv1, *refs):
    outs = refs[:4]
    q, keep, limits, top, tot, acc, sa, sb, chunk_of, tile_of, sem = refs[4:]
    core = idx[0]
    copies = [
        pltpu.make_async_copy(r, q.at[pl.ds(1024 * b, 1024)], sem.at[b])
        for b, r in enumerate((q0, q1, q2, q3))
    ]
    for i, r in enumerate((cache0, cache1)):
        for side in range(2):
            at = pl.multiple_of(i * 1536 + 768 * (core if side == 0 else 1 - core), 256)
            copies.append(
                pltpu.make_async_copy(r.at[side], keep.at[pl.ds(at, 768)], sem.at[4 + 2 * i + side])
            )
    for i, r in enumerate((kv0, kv1)):
        copies.append(
            pltpu.make_async_copy(r, keep.at[pl.ds(3072 + 512 * i, 512)], sem.at[8 + i])
        )
    for c in copies:
        c.start()

    se, pe = [ends_s[0]], [ends_p[0]]
    for k in range(1, 4):
        se.append(se[-1] + ends_s[k])
        pe.append(pe[-1] + ends_p[k])

    def allowed_of(token):
        lo, hi, own = 0 * token, 0 * token + pe[0], 0 * token
        for k in range(3):
            later = token >= se[k]
            lo = jnp.where(later, pe[k], lo)
            hi = jnp.where(later, pe[k + 1], hi)
            own = jnp.where(later, se[k], own)
        return lo, hi, own

    for t in range(TILES):
        first = idx[1 + t // 2] + (t % 2) * 256
        token = first + lax.rem(lax.broadcasted_iota(jnp.int32, (1, R), 1), 256)
        lo, hi, own = allowed_of(token)
        limits[t, 0:1] = lo
        limits[t, 1:2] = hi
        limits[t, 2:3] = own
        limits[t, 3:4] = token + 1
    limits[DUMMY] = jnp.zeros((4, R), jnp.int32)
    top[...] = jnp.full(top.shape, FLOOR, F32)
    tot[...] = jnp.zeros(tot.shape, F32)
    acc[...] = jnp.zeros(acc.shape, F32)

    def base_of(i):
        slot = jnp.where(i < 3, idx[5] + i * CK, idx[6] + (i - 3) * CK)
        return jnp.where(i < 6, slot, jnp.where(i == 6, idx[7], idx[8]))

    def collect(want_full, start):
        def visit(n, count):
            i, t = n // TILES, lax.rem(n, TILES)
            base = base_of(i)
            first = idx[1 + t // 2] + lax.rem(t, 2) * 256
            last = first + 255
            lo_a, hi_a, own_a = allowed_of(first)
            lo_b, hi_b, own_b = allowed_of(last)
            pre = i < 6
            lo_first, lo_last = jnp.where(pre, lo_a, own_a), jnp.where(pre, lo_b, own_b)
            hi_first, hi_last = jnp.where(pre, hi_a, first + 1), jnp.where(pre, hi_b, last + 1)
            some = (base + CK > lo_first) & (base < hi_last)
            full = (base >= lo_last) & (base + CK <= hi_first)
            hit = full if want_full else (some & jnp.logical_not(full))

            @pl.when(hit)
            def _():
                chunk_of[count] = i
                tile_of[count] = t

            return count + hit.astype(jnp.int32)

        count = lax.fori_loop(0, CHUNKS * TILES, visit, start)
        rounds = (count + UNROLL - 1) // UNROLL
        for k in range(UNROLL):
            chunk_of[count + k] = 0
            tile_of[count + k] = DUMMY
        return rounds

    full_rounds = collect(True, 0)
    all_rounds = collect(False, full_rounds * UNROLL)
    for c in copies:
        c.wait()
    q[4096:4608] = jnp.zeros((R, H), BF16)

    def scores(n, out):
        keys = keep[pl.ds(pl.multiple_of(chunk_of[n] * CK, CK), CK), :H]
        out[...] = nt_dot(keys, q[pl.ds(pl.multiple_of(tile_of[n] * R, R), R), :])

    def consume(n, s_ref, masked):
        i, t = chunk_of[n], tile_of[n]
        s = s_ref[...]
        if masked:
            pos = base_of(i) + lax.broadcasted_iota(jnp.int32, (CK, R), 0)
            kind = jnp.where(i < 6, 0, 2)
            lo, hi = limits[t, pl.ds(kind, 1)], limits[t, pl.ds(kind + 1, 1)]
            s = jnp.where((pos >= lo) & (pos < hi), s, -jnp.inf)
        old = top[t]
        new = jnp.maximum(old, jnp.max(s, axis=0, keepdims=True))
        p = jnp.exp2(s * SCALE2 - new * SCALE2)
        factor = jnp.exp2((old - new) * SCALE2)
        top[t] = new
        tot[t] = tot[t] * factor + jnp.sum(p, axis=0, keepdims=True)
        values = keep[pl.ds(pl.multiple_of(i * CK, CK), CK), H:]
        acc[t] = acc[t] * factor + lax.dot_general(
            values, p.astype(BF16), (((0,), (0,)), ((), ())), preferred_element_type=F32
        )

    def rounds(masked):
        def body(n, _):
            for k in range(UNROLL):
                cur, nxt = (sa, sb) if k % 2 == 0 else (sb, sa)
                scores(n * UNROLL + k + 1, nxt)
                consume(n * UNROLL + k, cur, masked)
            return 0

        return body

    chunk_of[all_rounds * UNROLL] = 0
    tile_of[all_rounds * UNROLL] = DUMMY
    scores(0, sa)
    lax.fori_loop(0, full_rounds, rounds(False), 0)
    lax.fori_loop(full_rounds, all_rounds, rounds(True), 0)

    for t in range(TILES):
        total = tot[t]
        safe = jnp.where(total > 0.0, total, 1.0)
        cols = slice((t % 2) * R, (t % 2 + 1) * R)
        out = outs[t // 2]
        out[0:H, cols] = (acc[t] / safe).astype(BF16)
        lse = jnp.where(total > 0.0, top[t] * SCALE2 + jnp.log2(safe), FLOOR)
        high = lse.astype(BF16).astype(F32)
        mid = (lse - high).astype(BF16).astype(F32)
        low = lse - high - mid
        row = lax.broadcasted_iota(jnp.int32, (16, R), 0)
        packed = jnp.where(row == 0, high, jnp.where(row == 1, mid, jnp.where(row == 2, low, 0.0)))
        out[H : H + 16, cols] = packed.astype(BF16)


def attend(idx, suffix_lengths, prefix_lengths, qs, caches, kvs):
    return pl.pallas_call(
        attend_kernel,
        out_shape=tuple(jax.ShapeDtypeStruct((H + 16, 1024), BF16) for _ in range(4)),
        in_specs=[SMEM] * 3 + [HBM] * 8,
        out_specs=tuple([VMEM] * 4),
        scratch_shapes=[
            pltpu.VMEM((9 * R, H), BF16),
            pltpu.VMEM((CHUNKS * CK, 2 * H), BF16),
            pltpu.VMEM((TILES + 1, 4, R), jnp.int32),
            pltpu.VMEM((TILES + 1, 1, R), F32),
            pltpu.VMEM((TILES + 1, 1, R), F32),
            pltpu.VMEM((TILES + 1, H, R), F32),
            pltpu.VMEM((CK, R), F32),
            pltpu.VMEM((CK, R), F32),
            pltpu.SMEM((CHUNKS * TILES + 4 * UNROLL,), jnp.int32),
            pltpu.SMEM((CHUNKS * TILES + 4 * UNROLL,), jnp.int32),
            pltpu.SemaphoreType.DMA((10,)),
        ],
        compiler_params=pltpu.CompilerParams(vmem_limit_bytes=20 << 20),
        cost_estimate=pl.CostEstimate(
            flops=12 << 30, bytes_accessed=6 << 20, transcendentals=10 << 20
        ),
        name="attend",
    )(idx, suffix_lengths, prefix_lengths, *pin([*qs, *caches, *kvs]))


def combine_kernel(gates, p0, p1, p2, p3, out):
    parts = (p0, p1, p2, p3)
    lses = []
    for p in parts:
        rows = p[H : H + 16].astype(F32)
        lses.append(rows[0:1] + rows[1:2] + rows[2:3])
    high = jnp.maximum(jnp.maximum(lses[0], lses[1]), jnp.maximum(lses[2], lses[3]))
    share = [jnp.exp2(v - high) for v in lses]
    norm = gates[...] / (share[0] + share[1] + share[2] + share[3])
    for at in range(0, 1024, 256):
        cols = slice(at, at + 256)
        total = jnp.zeros((H, 256), F32)
        for p, s in zip(parts, share):
            total += p[0:H, cols].astype(F32) * s[:, cols]
        out[cols] = jnp.transpose(total * norm[:, cols]).astype(BF16)


def combine(gates, parts):
    return pl.pallas_call(
        combine_kernel,
        out_shape=jax.ShapeDtypeStruct((1024, H), BF16),
        in_specs=[VMEM] * 5,
        out_specs=VMEM,
        compiler_params=pltpu.CompilerParams(vmem_limit_bytes=8 << 20),
        cost_estimate=pl.CostEstimate(flops=1 << 22, bytes_accessed=2 << 20, transcendentals=0),
        name="combine",
    )(gates, *parts)


def out_kernel(idx, routes, own, other, blocks, *refs):
    outs = refs[:4]
    held, padded, sem = refs[4:]
    core = idx[8]
    copy = pltpu.make_async_copy(blocks, held, sem.at[0])
    copy.start()
    for side, source in enumerate((own, other)):
        for half in range(2):
            for e in range(E):
                value = jnp.zeros((256, H), F32)
                for j in range(2):
                    hit = routes[half * 256 : (half + 1) * 256, j : j + 1] == e
                    at = (half * 2 + j) * 256
                    value = jnp.where(hit, source[at : at + 256].astype(F32), value)
                padded[side, half * 256 : (half + 1) * 256, e * H : (e + 1) * H] = value.astype(
                    BF16
                )
    copy.wait()
    for dz in range(4):
        value = jnp.zeros((512, 256), F32)
        for side in range(2):
            head = core if side == 0 else 1 - core
            rows = pl.ds(pl.multiple_of(head * 1024, 1024), 1024)
            w = jnp.concatenate(
                [held[idx[2 * dz], rows], held[idx[2 * dz + 1], rows]], axis=1
            )
            value += jnp.dot(padded[side], w, preferred_element_type=F32)
        for s in range(2):
            outs[dz][s] = value[:, s * H : (s + 1) * H].astype(outs[dz].dtype)


def project_out(idx, routes, own, other, blocks):
    return pl.pallas_call(
        out_kernel,
        out_shape=(jax.ShapeDtypeStruct((2, 512, H), F32),)
        + tuple(jax.ShapeDtypeStruct((2, 512, H), BF16) for _ in range(3)),
        in_specs=[SMEM, VMEM, VMEM, VMEM, HBM],
        out_specs=tuple([VMEM] * 4),
        scratch_shapes=[
            pltpu.VMEM((8, 2048, H), BF16),
            pltpu.VMEM((2, 512, 1024), BF16),
            pltpu.SemaphoreType.DMA((1,)),
        ],
        compiler_params=pltpu.CompilerParams(vmem_limit_bytes=20 << 20),
        cost_estimate=pl.CostEstimate(flops=4 << 30, bytes_accessed=6 << 20, transcendentals=0),
        name="project_out",
    )(idx, routes, own, other, *pin([blocks]))


def on_device(
    tokens,
    norm_gain,
    router,
    routes,
    kv_weight,
    query_weight,
    out_weight,
    prefix_cache,
    suffix_lengths,
    prefix_lengths,
):
    xl, y, c = (lax.axis_index(a) for a in WIDE)
    z, xh = (lax.axis_index(a) for a in NARROW)
    first_core = c == 0
    chips = chip_order()
    out_all = lax.all_gather(out_weight, ("xl", "y"), axis=0)

    def table(values):
        return jnp.stack([jnp.asarray(v, jnp.int32) for v in values])

    def head_rows(w, h):
        rows = w.shape[0] // 2
        return lax.dynamic_slice_in_dim(w, h * rows, rows, 0)

    def weights_of(h):
        return jnp.concatenate([head_rows(query_weight, h), head_rows(kv_weight, h)], axis=0)

    w0, w1 = weights_of(c), across_core(weights_of(1 - c))
    step0 = first_step(w0)
    pair = jnp.stack([tokens, across_far(tokens)])
    pair, step0 = tie(pair, step0)
    step1 = first_step(w1)
    blocks = [pair] + [along_z(pair, k) for k in (1, 2, 3)]
    blocks, step1 = tie(blocks, step1)
    gathered = gather_parts(w0, w1, step0, step1)
    other_routes = across_core(routes)
    both_routes = jnp.where(
        first_core,
        jnp.concatenate([routes, other_routes]),
        jnp.concatenate([other_routes, routes]),
    )

    def cache_of(h):
        return lax.dynamic_slice_in_dim(prefix_cache, h * 2 * H, 2 * H, 1)

    cache = jnp.stack([cache_of(c), across_core(cache_of(1 - c))])
    cache_out, step1 = tie(cache, step1)
    caches = [cache, across_x(cache_out)]
    gathered, caches = tie(gathered, caches)

    token_src = [lax.rem(z + 4 - dz, 4) * 2 + (xh ^ s) for dz in range(4) for s in range(2)]
    places = [lax.rem(lax.rem(v, 4) + 4 - y, 4) * 2 + (v // 4 ^ xl) for v in token_src]
    normed = normalise(table(token_src + places), norm_gain.reshape(8, 1, 256), blocks)
    q, kv, gates = project(
        table(chips + [c]), both_routes, router.T, normed, across_core(normed), gathered
    )
    kvs = [kv, across_x(kv)]
    qs = [q] + [along_y(q, k) for k in (1, 2, 3)]

    firsts = [(xl * 4 + lax.rem(y + 4 - k, 4)) * 512 for k in range(4)]
    mine, partner = xl * 4 + y, (1 - xl) * 4 + y
    at = [c] + firsts + [mine * 1536, partner * 1536, mine * 512, partner * 512]
    parts = list(attend(table(at), suffix_lengths, prefix_lengths, qs, caches, kvs))
    for k in range(1, 4):
        parts[k] = along_y(parts[k], 4 - k)
    gate_row = gates.reshape(2, 256, 2).transpose(0, 2, 1).reshape(1, 1024)
    attended = combine(gate_row, parts)

    dests = [lax.rem(z + dz, 4) * 2 + (xh ^ s) for dz in range(4) for s in range(2)]
    sums = project_out(
        table(dests + [c]), both_routes, attended, across_core(attended), out_all
    )
    total = sums[0]
    for k in (1, 2, 3):
        total = total + along_z(sums[k], k).astype(F32)
    total = total[0] + across_far(total[1].astype(BF16)).astype(F32)
    here = lax.dynamic_slice_in_dim(total, c * 256, 256, 0).astype(BF16)
    there = lax.dynamic_slice_in_dim(total, (1 - c) * 256, 256, 0).astype(BF16)
    there = across_core(there)
    return jnp.where(
        first_core,
        jnp.concatenate([here, there], axis=1),
        jnp.concatenate([there, here], axis=1),
    )


def solution(mesh):
    fine = Mesh(mesh.devices.reshape(SIZES), AXES)
    placed = (
        P(WIDE, NARROW),
        P(),
        P(),
        P(WIDE, None),
        P(NARROW, WIDE),
        P(NARROW, WIDE),
        P(NARROW, WIDE),
        P(WIDE, NARROW),
        P(),
        P(),
    )
    return jax.shard_map(
        on_device, mesh=fine, in_specs=placed, out_specs=P(WIDE, NARROW), check_vma=False
    )
```

```python
import functools
import math

import jax
import jax.numpy as jnp
from jax import lax
from jax.experimental import pallas as pl
from jax.experimental.pallas import tpu as pltpu
from jax.sharding import Mesh
from jax.sharding import PartitionSpec as P

H = 128
E = 8
EPS = 1e-06
FLOOR = -1e30
AXES = ("xl", "y", "c", "z", "xh")
SIZES = (2, 4, 2, 4, 2)
WIDE = ("xl", "y", "c")
NARROW = ("z", "xh")
BF16 = jnp.bfloat16
F32 = jnp.float32
SCALE2 = H ** (-0.5) * math.log2(math.e)
CK = 512
R = 512
CHUNKS = 8
TILES = 8
DUMMY = 8
UNROLL = 4

SMEM = pl.BlockSpec(memory_space=pltpu.SMEM)
VMEM = pl.BlockSpec(memory_space=pltpu.VMEM)
HBM = pl.BlockSpec(memory_space=pltpu.HBM)
ANY = pl.BlockSpec(memory_space=pl.ANY)


def along_y(x, k):
    return lax.ppermute(x, "y", [(i, (i + k) % 4) for i in range(4)])


def along_z(x, k):
    return lax.ppermute(x, "z", [(i, (i + k) % 4) for i in range(4)])


def across_x(x):
    return lax.ppermute(x, "xl", [(0, 1), (1, 0)])


def across_far(x):
    return lax.ppermute(x, "xh", [(0, 1), (1, 0)])


def across_core(x):
    return lax.ppermute(x, "c", [(0, 1), (1, 0)])


def tie(a, b):
    return lax.optimization_barrier((a, b))


def first_step(w):
    return along_y(w, 3), along_y(w, 1), across_x(w)


def gather_parts(w0, w1, step0, step1):
    ym0, yp0, a0 = step0
    ym1, yp1, a1 = step1
    far0, far1 = along_y(yp0, 1), along_y(ym1, 3)
    am0, ap0 = along_y(a0, 3), along_y(a0, 1)
    am1, ap1 = along_y(a1, 3), along_y(a1, 1)
    afar0, afar1 = across_x(far0), across_x(far1)
    pairs = [(w0, w1), (a0, a1), (ym0, ym1), (am0, am1), (far0, far1), (afar0, afar1), (yp0, yp1), (ap0, ap1)]
    return [part for pair in pairs for part in pair]


def chip_order():
    xl, y = lax.axis_index("xl"), lax.axis_index("y")
    return [(xl ^ dx) * 4 + lax.rem(y + dy, 4) for dy in range(4) for dx in range(2)]


def pin(arrays):
    return [pltpu.with_memory_space_constraint(a, pltpu.HBM) for a in arrays]


def nt_dot(a, b):
    return lax.dot_general(a, b, (((1,), (1,)), ((), ())), preferred_element_type=F32)


def run(copies):
    for c in copies:
        c.start()
    for c in copies:
        c.wait()


def norm_kernel(idx, gain, b0, b1, b2, b3, normed, held, sem):
    refs = (b0, b1, b2, b3)
    run([pltpu.make_async_copy(r, held.at[i], sem.at[i]) for i, r in enumerate(refs)])
    total = jnp.zeros((256, 1), F32)
    for k in range(8):
        v = held[k // 2, k % 2].astype(F32)
        total = total + jnp.sum(v * v, axis=1, keepdims=True)
    scale = lax.rsqrt(total * (1.0 / 2048) + EPS)
    for k in range(8):
        v = held[k // 2, k % 2].astype(F32) * scale * gain[idx[k]].astype(F32)
        normed[:, pl.ds(pl.multiple_of(idx[8 + k] * 256, 256), 256)] = v.astype(BF16)


def normalise(idx, gain, blocks):
    return pl.pallas_call(
        norm_kernel,
        out_shape=jax.ShapeDtypeStruct((256, 2048), BF16),
        in_specs=[SMEM, VMEM] + [HBM] * 4,
        out_specs=VMEM,
        scratch_shapes=[pltpu.VMEM((4, 2, 256, 256), BF16), pltpu.SemaphoreType.DMA((4,))],
        compiler_params=pltpu.CompilerParams(vmem_limit_bytes=8 << 20),
        cost_estimate=pl.CostEstimate(flops=1 << 24, bytes_accessed=2 << 20, transcendentals=0),
        name="normalise",
    )(idx, gain, *blocks)


GROUPS = ((0, 512), (512, 768))


def project_kernel(idx, routes, router, own, other, *refs):
    blocks = refs[:16]
    q_out, kv_out, gates, xs, held, sel, sem = refs[16:]
    core = idx[8]
    copies = []
    for i, r in enumerate((own, other)):
        at = pl.multiple_of((core if i == 0 else 1 - core) * 256, 256)
        copies.append(pltpu.make_async_copy(r, xs.at[pl.ds(at, 256)], sem.at[32 + i]))
    for g, (start, rows) in enumerate(GROUPS):
        for k in range(16):
            lane = (k // 2) * 256 + H * (core if k % 2 == 0 else 1 - core)
            at = pl.ds(pl.multiple_of(lane, H), H)
            copies.append(
                pltpu.make_async_copy(
                    blocks[k].at[pl.ds(start, rows)],
                    held.at[pl.ds(start, rows), at],
                    sem.at[16 * g + k],
                )
            )
    for c in copies:
        c.start()
    for c in copies[:2]:
        c.wait()
    logits = jnp.zeros((512, E), F32)
    for i in range(8):
        part = router[:, pl.ds(pl.multiple_of(idx[i] * 256, 256), 256)]
        logits += nt_dot(xs[:, i * 256 : (i + 1) * 256], part)
    lane = lax.broadcasted_iota(jnp.int32, (512, E), 1)
    chosen = [
        jnp.sum(jnp.where(routes[:, j : j + 1] == lane, logits, 0.0), axis=1, keepdims=True)
        for j in range(2)
    ]
    top = jnp.maximum(chosen[0], chosen[1])
    e0, e1 = jnp.exp(chosen[0] - top), jnp.exp(chosen[1] - top)
    gates[:, 0:1] = e0 / (e0 + e1)
    gates[:, 1:2] = e1 / (e0 + e1)

    for r in range(5):
        if r == 0:
            for c in copies[2:18]:
                c.wait()
        if r == 2:
            for c in copies[18:]:
                c.wait()
        acc = nt_dot(xs[...], held[r * 256 : (r + 1) * 256])
        if r == 4:
            kv_out[...] = acc.astype(BF16)
            continue
        for j in range(2):
            value = jnp.zeros((512, H), F32) if r == 0 else sel[j]
            for e in range(2):
                hit = routes[:, j : j + 1] == 2 * r + e
                value = jnp.where(hit, acc[:, e * H : (e + 1) * H], value)
            if r < 3:
                sel[j] = value
            else:
                for half in range(2):
                    at = (half * 2 + j) * 256
                    q_out[at : at + 256] = value[half * 256 : (half + 1) * 256].astype(BF16)


def project(idx, routes, router, own, other, blocks):
    return pl.pallas_call(
        project_kernel,
        out_shape=(
            jax.ShapeDtypeStruct((1024, H), BF16),
            jax.ShapeDtypeStruct((512, 2 * H), BF16),
            jax.ShapeDtypeStruct((512, 2), F32),
        ),
        in_specs=[SMEM, VMEM, VMEM] + [HBM] * 18,
        out_specs=(VMEM, VMEM, VMEM),
        scratch_shapes=[
            pltpu.VMEM((512, 2048), BF16),
            pltpu.VMEM((1280, 2048), BF16),
            pltpu.VMEM((2, 512, H), F32),
            pltpu.SemaphoreType.DMA((34,)),
        ],
        compiler_params=pltpu.CompilerParams(vmem_limit_bytes=20 << 20),
        cost_estimate=pl.CostEstimate(flops=6 << 30, bytes_accessed=8 << 20, transcendentals=0),
        name="project",
    )(idx, routes, router, *pin([own, other, *blocks]))


def attend_kernel(idx, ends_s, ends_p, q0, q1, q2, q3, cache0, cache1, kv0, kv1, *refs):
    outs = refs[:4]
    q, keep, limits, top, tot, acc, sa, sb, chunk_of, tile_of, sem = refs[4:]
    core = idx[0]
    copies = [
        pltpu.make_async_copy(r, q.at[pl.ds(1024 * b, 1024)], sem.at[b])
        for b, r in enumerate((q0, q1, q2, q3))
    ]
    for i, r in enumerate((cache0, cache1)):
        for side in range(2):
            at = pl.multiple_of(i * 1536 + 768 * (core if side == 0 else 1 - core), 256)
            copies.append(
                pltpu.make_async_copy(r.at[side], keep.at[pl.ds(at, 768)], sem.at[4 + 2 * i + side])
            )
    for i, r in enumerate((kv0, kv1)):
        copies.append(
            pltpu.make_async_copy(r, keep.at[pl.ds(3072 + 512 * i, 512)], sem.at[8 + i])
        )
    for c in copies:
        c.start()

    se, pe = [ends_s[0]], [ends_p[0]]
    for k in range(1, 4):
        se.append(se[-1] + ends_s[k])
        pe.append(pe[-1] + ends_p[k])

    def allowed_of(token):
        lo, hi, own = 0 * token, 0 * token + pe[0], 0 * token
        for k in range(3):
            later = token >= se[k]
            lo = jnp.where(later, pe[k], lo)
            hi = jnp.where(later, pe[k + 1], hi)
            own = jnp.where(later, se[k], own)
        return lo, hi, own

    for t in range(TILES):
        first = idx[1 + t // 2] + (t % 2) * 256
        token = first + lax.rem(lax.broadcasted_iota(jnp.int32, (1, R), 1), 256)
        lo, hi, own = allowed_of(token)
        limits[t, 0:1] = lo
        limits[t, 1:2] = hi
        limits[t, 2:3] = own
        limits[t, 3:4] = token + 1
    limits[DUMMY] = jnp.zeros((4, R), jnp.int32)
    top[...] = jnp.full(top.shape, FLOOR, F32)
    tot[...] = jnp.zeros(tot.shape, F32)
    acc[...] = jnp.zeros(acc.shape, F32)

    def base_of(i):
        slot = jnp.where(i < 3, idx[5] + i * CK, idx[6] + (i - 3) * CK)
        return jnp.where(i < 6, slot, jnp.where(i == 6, idx[7], idx[8]))

    def collect(want_full, start):
        def visit(n, count):
            i, t = n // TILES, lax.rem(n, TILES)
            base = base_of(i)
            first = idx[1 + t // 2] + lax.rem(t, 2) * 256
            last = first + 255
            lo_a, hi_a, own_a = allowed_of(first)
            lo_b, hi_b, own_b = allowed_of(last)
            pre = i < 6
            lo_first, lo_last = jnp.where(pre, lo_a, own_a), jnp.where(pre, lo_b, own_b)
            hi_first, hi_last = jnp.where(pre, hi_a, first + 1), jnp.where(pre, hi_b, last + 1)
            some = (base + CK > lo_first) & (base < hi_last)
            full = (base >= lo_last) & (base + CK <= hi_first)
            hit = full if want_full else (some & jnp.logical_not(full))

            @pl.when(hit)
            def _():
                chunk_of[count] = i
                tile_of[count] = t

            return count + hit.astype(jnp.int32)

        count = lax.fori_loop(0, CHUNKS * TILES, visit, start)
        rounds = (count + UNROLL - 1) // UNROLL
        for k in range(UNROLL):
            chunk_of[count + k] = 0
            tile_of[count + k] = DUMMY
        return rounds

    full_rounds = collect(True, 0)
    all_rounds = collect(False, full_rounds * UNROLL)
    for c in copies:
        c.wait()
    q[4096:4608] = jnp.zeros((R, H), BF16)

    def scores(n, out):
        keys = keep[pl.ds(pl.multiple_of(chunk_of[n] * CK, CK), CK), :H]
        out[...] = nt_dot(keys, q[pl.ds(pl.multiple_of(tile_of[n] * R, R), R), :])

    def consume(n, s_ref, masked):
        i, t = chunk_of[n], tile_of[n]
        s = s_ref[...]
        if masked:
            pos = base_of(i) + lax.broadcasted_iota(jnp.int32, (CK, R), 0)
            kind = jnp.where(i < 6, 0, 2)
            lo, hi = limits[t, pl.ds(kind, 1)], limits[t, pl.ds(kind + 1, 1)]
            s = jnp.where((pos >= lo) & (pos < hi), s, -jnp.inf)
        old = top[t]
        new = jnp.maximum(old, jnp.max(s, axis=0, keepdims=True))
        p = jnp.exp2(s * SCALE2 - new * SCALE2)
        factor = jnp.exp2((old - new) * SCALE2)
        top[t] = new
        tot[t] = tot[t] * factor + jnp.sum(p, axis=0, keepdims=True)
        values = keep[pl.ds(pl.multiple_of(i * CK, CK), CK), H:]
        acc[t] = acc[t] * factor + lax.dot_general(
            values, p.astype(BF16), (((0,), (0,)), ((), ())), preferred_element_type=F32
        )

    def rounds(masked):
        def body(n, _):
            for k in range(UNROLL):
                cur, nxt = (sa, sb) if k % 2 == 0 else (sb, sa)
                scores(n * UNROLL + k + 1, nxt)
                consume(n * UNROLL + k, cur, masked)
            return 0

        return body

    chunk_of[all_rounds * UNROLL] = 0
    tile_of[all_rounds * UNROLL] = DUMMY
    scores(0, sa)
    lax.fori_loop(0, full_rounds, rounds(False), 0)
    lax.fori_loop(full_rounds, all_rounds, rounds(True), 0)

    for t in range(TILES):
        total = tot[t]
        safe = jnp.where(total > 0.0, total, 1.0)
        cols = slice((t % 2) * R, (t % 2 + 1) * R)
        out = outs[t // 2]
        out[0:H, cols] = (acc[t] / safe).astype(BF16)
        lse = jnp.where(total > 0.0, top[t] * SCALE2 + jnp.log2(safe), FLOOR)
        high = lse.astype(BF16).astype(F32)
        mid = (lse - high).astype(BF16).astype(F32)
        low = lse - high - mid
        row = lax.broadcasted_iota(jnp.int32, (16, R), 0)
        packed = jnp.where(row == 0, high, jnp.where(row == 1, mid, jnp.where(row == 2, low, 0.0)))
        out[H : H + 16, cols] = packed.astype(BF16)


def attend(idx, suffix_lengths, prefix_lengths, qs, caches, kvs):
    return pl.pallas_call(
        attend_kernel,
        out_shape=tuple(jax.ShapeDtypeStruct((H + 16, 1024), BF16) for _ in range(4)),
        in_specs=[SMEM] * 3 + [HBM] * 8,
        out_specs=tuple([VMEM] * 4),
        scratch_shapes=[
            pltpu.VMEM((9 * R, H), BF16),
            pltpu.VMEM((CHUNKS * CK, 2 * H), BF16),
            pltpu.VMEM((TILES + 1, 4, R), jnp.int32),
            pltpu.VMEM((TILES + 1, 1, R), F32),
            pltpu.VMEM((TILES + 1, 1, R), F32),
            pltpu.VMEM((TILES + 1, H, R), F32),
            pltpu.VMEM((CK, R), F32),
            pltpu.VMEM((CK, R), F32),
            pltpu.SMEM((CHUNKS * TILES + 4 * UNROLL,), jnp.int32),
            pltpu.SMEM((CHUNKS * TILES + 4 * UNROLL,), jnp.int32),
            pltpu.SemaphoreType.DMA((10,)),
        ],
        compiler_params=pltpu.CompilerParams(vmem_limit_bytes=20 << 20),
        cost_estimate=pl.CostEstimate(
            flops=12 << 30, bytes_accessed=6 << 20, transcendentals=10 << 20
        ),
        name="attend",
    )(idx, suffix_lengths, prefix_lengths, *pin([*qs, *caches, *kvs]))


def combine_kernel(gates, p0, p1, p2, p3, out):
    parts = (p0, p1, p2, p3)
    lses = []
    for p in parts:
        rows = p[H : H + 16].astype(F32)
        lses.append(rows[0:1] + rows[1:2] + rows[2:3])
    high = jnp.maximum(jnp.maximum(lses[0], lses[1]), jnp.maximum(lses[2], lses[3]))
    share = [jnp.exp2(v - high) for v in lses]
    norm = gates[...] / (share[0] + share[1] + share[2] + share[3])
    for at in range(0, 1024, 256):
        cols = slice(at, at + 256)
        total = jnp.zeros((H, 256), F32)
        for p, s in zip(parts, share):
            total += p[0:H, cols].astype(F32) * s[:, cols]
        out[cols] = jnp.transpose(total * norm[:, cols]).astype(BF16)


def combine(gates, parts):
    return pl.pallas_call(
        combine_kernel,
        out_shape=jax.ShapeDtypeStruct((1024, H), BF16),
        in_specs=[VMEM] * 5,
        out_specs=VMEM,
        compiler_params=pltpu.CompilerParams(vmem_limit_bytes=8 << 20),
        cost_estimate=pl.CostEstimate(flops=1 << 22, bytes_accessed=2 << 20, transcendentals=0),
        name="combine",
    )(gates, *parts)


def out_kernel(idx, routes, own, other, *refs):
    blocks = refs[:8]
    outs = refs[8:12]
    held, padded, sem = refs[12:]
    core = idx[8]
    copies = [
        pltpu.make_async_copy(r, held.at[idx[k]], sem.at[k]) for k, r in enumerate(blocks)
    ]
    for c in copies:
        c.start()
    for side, source in enumerate((own, other)):
        for half in range(2):
            for e in range(E):
                value = jnp.zeros((256, H), F32)
                for j in range(2):
                    hit = routes[half * 256 : (half + 1) * 256, j : j + 1] == e
                    at = (half * 2 + j) * 256
                    value = jnp.where(hit, source[at : at + 256].astype(F32), value)
                padded[side, half * 256 : (half + 1) * 256, e * H : (e + 1) * H] = value.astype(
                    BF16
                )
    for c in copies:
        c.wait()
    for dz in range(4):
        value = jnp.zeros((512, 256), F32)
        for side in range(2):
            head = core if side == 0 else 1 - core
            rows = pl.ds(pl.multiple_of(head * 1024, 1024), 1024)
            w = jnp.concatenate(
                [held[idx[9 + 2 * dz], rows], held[idx[10 + 2 * dz], rows]], axis=1
            )
            value += jnp.dot(padded[side], w, preferred_element_type=F32)
        for s in range(2):
            outs[dz][s] = value[:, s * H : (s + 1) * H].astype(outs[dz].dtype)


def project_out(idx, routes, own, other, blocks):
    return pl.pallas_call(
        out_kernel,
        out_shape=(jax.ShapeDtypeStruct((2, 512, H), F32),)
        + tuple(jax.ShapeDtypeStruct((2, 512, H), BF16) for _ in range(3)),
        in_specs=[SMEM, VMEM, VMEM, VMEM] + [HBM] * 8,
        out_specs=tuple([VMEM] * 4),
        scratch_shapes=[
            pltpu.VMEM((8, 2048, H), BF16),
            pltpu.VMEM((2, 512, 1024), BF16),
            pltpu.SemaphoreType.DMA((8,)),
        ],
        compiler_params=pltpu.CompilerParams(vmem_limit_bytes=20 << 20),
        cost_estimate=pl.CostEstimate(flops=4 << 30, bytes_accessed=6 << 20, transcendentals=0),
        name="project_out",
    )(idx, routes, own, other, *pin(blocks))


def on_device(
    tokens,
    norm_gain,
    router,
    routes,
    kv_weight,
    query_weight,
    out_weight,
    prefix_cache,
    suffix_lengths,
    prefix_lengths,
):
    xl, y, c = (lax.axis_index(a) for a in WIDE)
    z, xh = (lax.axis_index(a) for a in NARROW)
    first_core = c == 0
    chips = chip_order()

    def table(values):
        return jnp.stack([jnp.asarray(v, jnp.int32) for v in values])

    def head_rows(w, h):
        rows = w.shape[0] // 2
        return lax.dynamic_slice_in_dim(w, h * rows, rows, 0)

    def weights_of(h):
        return jnp.concatenate([head_rows(query_weight, h), head_rows(kv_weight, h)], axis=0)

    w0, w1 = weights_of(c), across_core(weights_of(1 - c))
    step0 = first_step(w0)
    pair = jnp.stack([tokens, across_far(tokens)])
    pair, step0 = tie(pair, step0)
    step1 = first_step(w1)
    blocks = [pair] + [along_z(pair, k) for k in (1, 2, 3)]
    blocks, step1 = tie(blocks, step1)
    gathered = gather_parts(w0, w1, step0, step1)
    other_routes = across_core(routes)
    both_routes = jnp.where(
        first_core,
        jnp.concatenate([routes, other_routes]),
        jnp.concatenate([other_routes, routes]),
    )

    def cache_of(h):
        return lax.dynamic_slice_in_dim(prefix_cache, h * 2 * H, 2 * H, 1)

    cache = jnp.stack([cache_of(c), across_core(cache_of(1 - c))])
    cache_out, step1 = tie(cache, step1)
    caches = [cache, across_x(cache_out)]
    gathered, caches = tie(gathered, caches)

    token_src = [lax.rem(z + 4 - dz, 4) * 2 + (xh ^ s) for dz in range(4) for s in range(2)]
    places = [lax.rem(lax.rem(v, 4) + 4 - y, 4) * 2 + (v // 4 ^ xl) for v in token_src]
    normed = normalise(table(token_src + places), norm_gain.reshape(8, 1, 256), blocks)
    out_early, gathered[7] = tie(out_weight, gathered[7])
    o_ym, o_yp, o_a = along_y(out_early, 3), along_y(out_early, 1), across_x(out_early)
    q, kv, gates = project(
        table(chips + [c]), both_routes, router.T, normed, across_core(normed), gathered
    )
    kvs = [kv, across_x(kv)]
    q_out, o_a, o_ym, o_yp = lax.optimization_barrier((q, o_a, o_ym, o_yp))
    qs = [q] + [along_y(q_out, k) for k in (1, 2, 3)]
    out_late, o_a_late, kvs[1] = lax.optimization_barrier((out_weight, o_a, kvs[1]))
    o_far, o_am, o_ap = along_y(out_late, 2), along_y(o_a_late, 3), along_y(o_a_late, 1)

    firsts = [(xl * 4 + lax.rem(y + 4 - k, 4)) * 512 for k in range(4)]
    mine, partner = xl * 4 + y, (1 - xl) * 4 + y
    at = [c] + firsts + [mine * 1536, partner * 1536, mine * 512, partner * 512]
    parts = list(attend(table(at), suffix_lengths, prefix_lengths, qs, caches, kvs))
    parts[1:], o_far, o_am, o_ap = lax.optimization_barrier((parts[1:], o_far, o_am, o_ap))
    for k in range(1, 4):
        parts[k] = along_y(parts[k], 4 - k)
    out_blocks = [out_weight, o_a, o_ym, o_am, o_far, across_x(o_far), o_yp, o_ap]
    gate_row = gates.reshape(2, 256, 2).transpose(0, 2, 1).reshape(1, 1024)
    attended = combine(gate_row, parts)

    dests = [lax.rem(z + dz, 4) * 2 + (xh ^ s) for dz in range(4) for s in range(2)]
    sums = project_out(
        table(chips + [c] + dests), both_routes, attended, across_core(attended), out_blocks
    )
    total = sums[0]
    for k in (1, 2, 3):
        total = total + along_z(sums[k], k).astype(F32)
    total = total[0] + across_far(total[1].astype(BF16)).astype(F32)
    here = lax.dynamic_slice_in_dim(total, c * 256, 256, 0).astype(BF16)
    there = lax.dynamic_slice_in_dim(total, (1 - c) * 256, 256, 0).astype(BF16)
    there = across_core(there)
    return jnp.where(
        first_core,
        jnp.concatenate([here, there], axis=1),
        jnp.concatenate([there, here], axis=1),
    )


def solution(mesh):
    fine = Mesh(mesh.devices.reshape(SIZES), AXES)
    placed = (
        P(WIDE, NARROW),
        P(),
        P(),
        P(WIDE, None),
        P(NARROW, WIDE),
        P(NARROW, WIDE),
        P(NARROW, WIDE),
        P(WIDE, NARROW),
        P(),
        P(),
    )
    return jax.shard_map(
        on_device, mesh=fine, in_specs=placed, out_specs=P(WIDE, NARROW), check_vma=False
    )
```

```python
import functools
import math

import jax
import jax.numpy as jnp
from jax import lax
from jax.experimental import pallas as pl
from jax.experimental.pallas import tpu as pltpu
from jax.sharding import Mesh
from jax.sharding import PartitionSpec as P

H = 128
E = 8
EPS = 1e-06
FLOOR = -1e30
AXES = ("xl", "y", "c", "z", "xh")
SIZES = (2, 4, 2, 4, 2)
WIDE = ("xl", "y", "c")
NARROW = ("z", "xh")
BF16 = jnp.bfloat16
F32 = jnp.float32
SCALE2 = H ** (-0.5) * math.log2(math.e)
CK = 512
R = 512
CHUNKS = 8
TILES = 8
DUMMY = 8
UNROLL = 4

SMEM = pl.BlockSpec(memory_space=pltpu.SMEM)
VMEM = pl.BlockSpec(memory_space=pltpu.VMEM)
HBM = pl.BlockSpec(memory_space=pltpu.HBM)
ANY = pl.BlockSpec(memory_space=pl.ANY)


def along_y(x, k):
    return lax.ppermute(x, "y", [(i, (i + k) % 4) for i in range(4)])


def across_x(x):
    return lax.ppermute(x, "xl", [(0, 1), (1, 0)])


def across_core(x):
    return lax.ppermute(x, "c", [(0, 1), (1, 0)])


def tie(a, b):
    return lax.optimization_barrier((a, b))


def chip_order():
    xl, y = lax.axis_index("xl"), lax.axis_index("y")
    return [(xl ^ dx) * 4 + lax.rem(y + dy, 4) for dy in range(4) for dx in range(2)]


def pin(arrays):
    return [pltpu.with_memory_space_constraint(a, pltpu.HBM) for a in arrays]


def nt_dot(a, b):
    return lax.dot_general(a, b, (((1,), (1,)), ((), ())), preferred_element_type=F32)


def run(copies):
    for c in copies:
        c.start()
    for c in copies:
        c.wait()


def norm_kernel(idx, gain, blocks, normed, held, sem):
    run([pltpu.make_async_copy(blocks, held, sem.at[0])])
    total = jnp.zeros((256, 1), F32)
    for k in range(8):
        v = held[k].astype(F32)
        total = total + jnp.sum(v * v, axis=1, keepdims=True)
    scale = lax.rsqrt(total * (1.0 / 2048) + EPS)
    for k in range(8):
        v = held[k].astype(F32) * scale * gain[k].astype(F32)
        normed[:, pl.ds(pl.multiple_of(idx[k] * 256, 256), 256)] = v.astype(BF16)


def normalise(idx, gain, blocks):
    return pl.pallas_call(
        norm_kernel,
        out_shape=jax.ShapeDtypeStruct((256, 2048), BF16),
        in_specs=[SMEM, VMEM, ANY],
        out_specs=VMEM,
        scratch_shapes=[pltpu.VMEM((8, 256, 256), BF16), pltpu.SemaphoreType.DMA((1,))],
        compiler_params=pltpu.CompilerParams(vmem_limit_bytes=8 << 20),
        cost_estimate=pl.CostEstimate(flops=1 << 24, bytes_accessed=2 << 20, transcendentals=0),
        name="normalise",
    )(idx, gain, blocks)


GROUPS = ((0, 512), (512, 768))


def project_kernel(idx, routes, router, own, other, *refs):
    blocks = refs[:8]
    q_out, kv_out, gates, xs, held, sel, sem = refs[8:]
    core = idx[8]
    copies = []
    for i, r in enumerate((own, other)):
        at = pl.multiple_of((core if i == 0 else 1 - core) * 256, 256)
        copies.append(pltpu.make_async_copy(r, xs.at[pl.ds(at, 256)], sem.at[32 + i]))
    for g, (start, rows) in enumerate(GROUPS):
        for k in range(16):
            lane = (k // 2) * 256 + H * (core if k % 2 == 0 else 1 - core)
            at = pl.ds(pl.multiple_of(lane, H), H)
            copies.append(
                pltpu.make_async_copy(
                    blocks[k // 2].at[k % 2, pl.ds(start, rows)],
                    held.at[pl.ds(start, rows), at],
                    sem.at[16 * g + k],
                )
            )
    for c in copies:
        c.start()
    for c in copies[:2]:
        c.wait()
    logits = jnp.zeros((512, E), F32)
    for i in range(8):
        part = router[:, pl.ds(pl.multiple_of(idx[i] * 256, 256), 256)]
        logits += nt_dot(xs[:, i * 256 : (i + 1) * 256], part)
    lane = lax.broadcasted_iota(jnp.int32, (512, E), 1)
    chosen = [
        jnp.sum(jnp.where(routes[:, j : j + 1] == lane, logits, 0.0), axis=1, keepdims=True)
        for j in range(2)
    ]
    top = jnp.maximum(chosen[0], chosen[1])
    e0, e1 = jnp.exp(chosen[0] - top), jnp.exp(chosen[1] - top)
    gates[:, 0:1] = e0 / (e0 + e1)
    gates[:, 1:2] = e1 / (e0 + e1)

    for r in range(5):
        if r == 0:
            for c in copies[2:18]:
                c.wait()
        if r == 2:
            for c in copies[18:]:
                c.wait()
        acc = nt_dot(xs[...], held[r * 256 : (r + 1) * 256])
        if r == 4:
            kv_out[...] = acc.astype(BF16)
            continue
        for j in range(2):
            value = jnp.zeros((512, H), F32) if r == 0 else sel[j]
            for e in range(2):
                hit = routes[:, j : j + 1] == 2 * r + e
                value = jnp.where(hit, acc[:, e * H : (e + 1) * H], value)
            if r < 3:
                sel[j] = value
            else:
                for half in range(2):
                    at = (half * 2 + j) * 256
                    q_out[at : at + 256] = value[half * 256 : (half + 1) * 256].astype(BF16)


def project(idx, routes, router, own, other, blocks):
    return pl.pallas_call(
        project_kernel,
        out_shape=(
            jax.ShapeDtypeStruct((1024, H), BF16),
            jax.ShapeDtypeStruct((512, 2 * H), BF16),
            jax.ShapeDtypeStruct((512, 2), F32),
        ),
        in_specs=[SMEM, VMEM, VMEM] + [HBM] * 10,
        out_specs=(VMEM, VMEM, VMEM),
        scratch_shapes=[
            pltpu.VMEM((512, 2048), BF16),
            pltpu.VMEM((1280, 2048), BF16),
            pltpu.VMEM((2, 512, H), F32),
            pltpu.SemaphoreType.DMA((34,)),
        ],
        compiler_params=pltpu.CompilerParams(vmem_limit_bytes=20 << 20),
        cost_estimate=pl.CostEstimate(flops=6 << 30, bytes_accessed=8 << 20, transcendentals=0),
        name="project",
    )(idx, routes, router, *pin([own, other, *blocks]))


def attend_kernel(idx, ends_s, ends_p, q0, q1, q2, q3, cache0, cache1, kv0, kv1, *refs):
    outs = refs[:4]
    q, keep, limits, top, tot, acc, sa, sb, chunk_of, tile_of, sem = refs[4:]
    core = idx[0]
    copies = [
        pltpu.make_async_copy(r, q.at[pl.ds(1024 * b, 1024)], sem.at[b])
        for b, r in enumerate((q0, q1, q2, q3))
    ]
    for i, r in enumerate((cache0, cache1)):
        for side in range(2):
            at = pl.multiple_of(i * 1536 + 768 * (core if side == 0 else 1 - core), 256)
            copies.append(
                pltpu.make_async_copy(r.at[side], keep.at[pl.ds(at, 768)], sem.at[4 + 2 * i + side])
            )
    for i, r in enumerate((kv0, kv1)):
        copies.append(
            pltpu.make_async_copy(r, keep.at[pl.ds(3072 + 512 * i, 512)], sem.at[8 + i])
        )
    for c in copies:
        c.start()

    se, pe = [ends_s[0]], [ends_p[0]]
    for k in range(1, 4):
        se.append(se[-1] + ends_s[k])
        pe.append(pe[-1] + ends_p[k])

    def allowed_of(token):
        lo, hi, own = 0 * token, 0 * token + pe[0], 0 * token
        for k in range(3):
            later = token >= se[k]
            lo = jnp.where(later, pe[k], lo)
            hi = jnp.where(later, pe[k + 1], hi)
            own = jnp.where(later, se[k], own)
        return lo, hi, own

    for t in range(TILES):
        first = idx[1 + t // 2] + (t % 2) * 256
        token = first + lax.rem(lax.broadcasted_iota(jnp.int32, (1, R), 1), 256)
        lo, hi, own = allowed_of(token)
        limits[t, 0:1] = lo
        limits[t, 1:2] = hi
        limits[t, 2:3] = own
        limits[t, 3:4] = token + 1
    limits[DUMMY] = jnp.zeros((4, R), jnp.int32)
    top[...] = jnp.full(top.shape, FLOOR, F32)
    tot[...] = jnp.zeros(tot.shape, F32)
    acc[...] = jnp.zeros(acc.shape, F32)

    def base_of(i):
        slot = jnp.where(i < 3, idx[5] + i * CK, idx[6] + (i - 3) * CK)
        return jnp.where(i < 6, slot, jnp.where(i == 6, idx[7], idx[8]))

    def collect(want_full, start):
        def visit(n, count):
            i, t = n // TILES, lax.rem(n, TILES)
            base = base_of(i)
            first = idx[1 + t // 2] + lax.rem(t, 2) * 256
            last = first + 255
            lo_a, hi_a, own_a = allowed_of(first)
            lo_b, hi_b, own_b = allowed_of(last)
            pre = i < 6
            lo_first, lo_last = jnp.where(pre, lo_a, own_a), jnp.where(pre, lo_b, own_b)
            hi_first, hi_last = jnp.where(pre, hi_a, first + 1), jnp.where(pre, hi_b, last + 1)
            some = (base + CK > lo_first) & (base < hi_last)
            full = (base >= lo_last) & (base + CK <= hi_first)
            hit = full if want_full else (some & jnp.logical_not(full))

            @pl.when(hit)
            def _():
                chunk_of[count] = i
                tile_of[count] = t

            return count + hit.astype(jnp.int32)

        count = lax.fori_loop(0, CHUNKS * TILES, visit, start)
        rounds = (count + UNROLL - 1) // UNROLL
        for k in range(UNROLL):
            chunk_of[count + k] = 0
            tile_of[count + k] = DUMMY
        return rounds

    full_rounds = collect(True, 0)
    all_rounds = collect(False, full_rounds * UNROLL)
    for c in copies:
        c.wait()
    q[4096:4608] = jnp.zeros((R, H), BF16)

    def scores(n, out):
        keys = keep[pl.ds(pl.multiple_of(chunk_of[n] * CK, CK), CK), :H]
        out[...] = nt_dot(keys, q[pl.ds(pl.multiple_of(tile_of[n] * R, R), R), :])

    def consume(n, s_ref, masked):
        i, t = chunk_of[n], tile_of[n]
        s = s_ref[...]
        if masked:
            pos = base_of(i) + lax.broadcasted_iota(jnp.int32, (CK, R), 0)
            kind = jnp.where(i < 6, 0, 2)
            lo, hi = limits[t, pl.ds(kind, 1)], limits[t, pl.ds(kind + 1, 1)]
            s = jnp.where((pos >= lo) & (pos < hi), s, -jnp.inf)
        old = top[t]
        new = jnp.maximum(old, jnp.max(s, axis=0, keepdims=True))
        p = jnp.exp2(s * SCALE2 - new * SCALE2)
        factor = jnp.exp2((old - new) * SCALE2)
        top[t] = new
        tot[t] = tot[t] * factor + jnp.sum(p, axis=0, keepdims=True)
        values = keep[pl.ds(pl.multiple_of(i * CK, CK), CK), H:]
        acc[t] = acc[t] * factor + lax.dot_general(
            values, p.astype(BF16), (((0,), (0,)), ((), ())), preferred_element_type=F32
        )

    def rounds(masked):
        def body(n, _):
            for k in range(UNROLL):
                cur, nxt = (sa, sb) if k % 2 == 0 else (sb, sa)
                scores(n * UNROLL + k + 1, nxt)
                consume(n * UNROLL + k, cur, masked)
            return 0

        return body

    chunk_of[all_rounds * UNROLL] = 0
    tile_of[all_rounds * UNROLL] = DUMMY
    scores(0, sa)
    lax.fori_loop(0, full_rounds, rounds(False), 0)
    lax.fori_loop(full_rounds, all_rounds, rounds(True), 0)

    for t in range(TILES):
        total = tot[t]
        safe = jnp.where(total > 0.0, total, 1.0)
        cols = slice((t % 2) * R, (t % 2 + 1) * R)
        out = outs[t // 2]
        out[0:H, cols] = (acc[t] / safe).astype(BF16)
        lse = jnp.where(total > 0.0, top[t] * SCALE2 + jnp.log2(safe), FLOOR)
        high = lse.astype(BF16).astype(F32)
        mid = (lse - high).astype(BF16).astype(F32)
        low = lse - high - mid
        row = lax.broadcasted_iota(jnp.int32, (16, R), 0)
        packed = jnp.where(row == 0, high, jnp.where(row == 1, mid, jnp.where(row == 2, low, 0.0)))
        out[H : H + 16, cols] = packed.astype(BF16)


def attend(idx, suffix_lengths, prefix_lengths, qs, caches, kvs):
    return pl.pallas_call(
        attend_kernel,
        out_shape=tuple(jax.ShapeDtypeStruct((H + 16, 1024), BF16) for _ in range(4)),
        in_specs=[SMEM] * 3 + [HBM] * 8,
        out_specs=tuple([VMEM] * 4),
        scratch_shapes=[
            pltpu.VMEM((9 * R, H), BF16),
            pltpu.VMEM((CHUNKS * CK, 2 * H), BF16),
            pltpu.VMEM((TILES + 1, 4, R), jnp.int32),
            pltpu.VMEM((TILES + 1, 1, R), F32),
            pltpu.VMEM((TILES + 1, 1, R), F32),
            pltpu.VMEM((TILES + 1, H, R), F32),
            pltpu.VMEM((CK, R), F32),
            pltpu.VMEM((CK, R), F32),
            pltpu.SMEM((CHUNKS * TILES + 4 * UNROLL,), jnp.int32),
            pltpu.SMEM((CHUNKS * TILES + 4 * UNROLL,), jnp.int32),
            pltpu.SemaphoreType.DMA((10,)),
        ],
        compiler_params=pltpu.CompilerParams(vmem_limit_bytes=20 << 20),
        cost_estimate=pl.CostEstimate(
            flops=12 << 30, bytes_accessed=6 << 20, transcendentals=10 << 20
        ),
        name="attend",
    )(idx, suffix_lengths, prefix_lengths, *pin([*qs, *caches, *kvs]))


def combine_kernel(gates, p0, p1, p2, p3, out):
    parts = (p0, p1, p2, p3)
    lses = []
    for p in parts:
        rows = p[H : H + 16].astype(F32)
        lses.append(rows[0:1] + rows[1:2] + rows[2:3])
    high = jnp.maximum(jnp.maximum(lses[0], lses[1]), jnp.maximum(lses[2], lses[3]))
    share = [jnp.exp2(v - high) for v in lses]
    norm = gates[...] / (share[0] + share[1] + share[2] + share[3])
    for at in range(0, 1024, 256):
        cols = slice(at, at + 256)
        total = jnp.zeros((H, 256), F32)
        for p, s in zip(parts, share):
            total += p[0:H, cols].astype(F32) * s[:, cols]
        out[cols] = jnp.transpose(total * norm[:, cols]).astype(BF16)


def combine(gates, parts):
    return pl.pallas_call(
        combine_kernel,
        out_shape=jax.ShapeDtypeStruct((1024, H), BF16),
        in_specs=[VMEM] * 5,
        out_specs=VMEM,
        compiler_params=pltpu.CompilerParams(vmem_limit_bytes=8 << 20),
        cost_estimate=pl.CostEstimate(flops=1 << 22, bytes_accessed=2 << 20, transcendentals=0),
        name="combine",
    )(gates, *parts)


def out_kernel(idx, routes, own, other, *refs):
    blocks = refs[:8]
    out, held, padded, sem = refs[8:]
    core = idx[8]
    copies = [
        pltpu.make_async_copy(r, held.at[idx[k]], sem.at[k]) for k, r in enumerate(blocks)
    ]
    for c in copies:
        c.start()
    for side, source in enumerate((own, other)):
        for half in range(2):
            for e in range(E):
                value = jnp.zeros((256, H), F32)
                for j in range(2):
                    hit = routes[half * 256 : (half + 1) * 256, j : j + 1] == e
                    at = (half * 2 + j) * 256
                    value = jnp.where(hit, source[at : at + 256].astype(F32), value)
                padded[side, half * 256 : (half + 1) * 256, e * H : (e + 1) * H] = value.astype(
                    BF16
                )
    for c in copies:
        c.wait()
    for k in range(0, 8, 2):
        value = jnp.zeros((512, 256), F32)
        for side in range(2):
            head = core if side == 0 else 1 - core
            rows = pl.ds(pl.multiple_of(head * 1024, 1024), 1024)
            w = jnp.concatenate([held[k, rows], held[k + 1, rows]], axis=1)
            value += jnp.dot(padded[side], w, preferred_element_type=F32)
        for s in range(2):
            out[k + s] = value[:, s * H : (s + 1) * H].astype(BF16)


def project_out(idx, routes, own, other, blocks):
    return pl.pallas_call(
        out_kernel,
        out_shape=jax.ShapeDtypeStruct((8, 512, H), BF16),
        in_specs=[SMEM, VMEM, VMEM, VMEM] + [HBM] * 8,
        out_specs=VMEM,
        scratch_shapes=[
            pltpu.VMEM((8, 2048, H), BF16),
            pltpu.VMEM((2, 512, 1024), BF16),
            pltpu.SemaphoreType.DMA((8,)),
        ],
        compiler_params=pltpu.CompilerParams(vmem_limit_bytes=20 << 20),
        cost_estimate=pl.CostEstimate(flops=4 << 30, bytes_accessed=6 << 20, transcendentals=0),
        name="project_out",
    )(idx, routes, own, other, *pin(blocks))


def on_device(
    tokens,
    norm_gain,
    router,
    routes,
    kv_weight,
    query_weight,
    out_weight,
    prefix_cache,
    suffix_lengths,
    prefix_lengths,
):
    xl, y, c = (lax.axis_index(a) for a in WIDE)
    first_core = c == 0
    chips = chip_order()

    def table(values):
        return jnp.stack([jnp.asarray(v, jnp.int32) for v in values])

    def head_rows(w, h):
        rows = w.shape[0] // 2
        return lax.dynamic_slice_in_dim(w, h * rows, rows, 0)

    def weights_of(h):
        return jnp.concatenate([head_rows(query_weight, h), head_rows(kv_weight, h)], axis=0)

    w = jnp.stack([weights_of(c), across_core(weights_of(1 - c))])
    other_routes = across_core(routes)
    both_routes = jnp.where(
        first_core,
        jnp.concatenate([routes, other_routes]),
        jnp.concatenate([other_routes, routes]),
    )

    def cache_of(h):
        return lax.dynamic_slice_in_dim(prefix_cache, h * 2 * H, 2 * H, 1)

    cache = jnp.stack([cache_of(c), across_core(cache_of(1 - c))])
    tokens, w = tie(tokens, w)
    copies = jnp.broadcast_to(tokens[None], (8,) + tokens.shape)
    blocks = lax.all_to_all(copies, NARROW, 0, 0, tiled=True)
    far, ym, yp, a = along_y(w, 2), along_y(w, 3), along_y(w, 1), across_x(w)
    caches = [cache, across_x(cache)]
    far, ym, yp, a, blocks, caches = lax.optimization_barrier((far, ym, yp, a, blocks, caches))
    am, ap, afar = along_y(a, 3), along_y(a, 1), across_x(far)
    gathered = [w, a, ym, am, far, afar, yp, ap]

    places = [(k % 4 - y + 4) % 4 * 2 + (k // 4 ^ xl) for k in range(8)]
    normed = normalise(table(places), norm_gain.reshape(8, 1, 256), blocks)
    out_early, am, ap = lax.optimization_barrier((out_weight, am, ap))
    gathered[3], gathered[7] = am, ap
    o_ym, o_yp, o_a = along_y(out_early, 3), along_y(out_early, 1), across_x(out_early)
    q, kv, gates = project(
        table(chips + [c]), both_routes, router.T, normed, across_core(normed), gathered
    )
    kvs = [kv, across_x(kv)]
    q_out, o_ym, o_yp = lax.optimization_barrier((q, o_ym, o_yp))
    qs = [q] + [along_y(q_out, k) for k in (1, 2, 3)]
    out_late, o_a_late, kvs[1] = lax.optimization_barrier((out_weight, o_a, kvs[1]))
    o_far, o_am, o_ap = along_y(out_late, 2), along_y(o_a_late, 3), along_y(o_a_late, 1)

    firsts = [(xl * 4 + lax.rem(y + 4 - k, 4)) * 512 for k in range(4)]
    mine, partner = xl * 4 + y, (1 - xl) * 4 + y
    at = [c] + firsts + [mine * 1536, partner * 1536, mine * 512, partner * 512]
    parts = list(attend(table(at), suffix_lengths, prefix_lengths, qs, caches, kvs))
    parts[1:], o_far, o_am, o_ap = lax.optimization_barrier((parts[1:], o_far, o_am, o_ap))
    for k in range(1, 4):
        parts[k] = along_y(parts[k], 4 - k)
    out_blocks = [out_weight, o_a, o_ym, o_am, o_far, across_x(o_far), o_yp, o_ap]
    gate_row = gates.reshape(2, 256, 2).transpose(0, 2, 1).reshape(1, 1024)
    attended = combine(gate_row, parts)

    sums = project_out(
        table(chips + [c]), both_routes, attended, across_core(attended), out_blocks
    )
    sums = lax.all_to_all(sums, NARROW, 0, 0, tiled=True)
    total = jnp.sum(sums.astype(F32), axis=0)
    here = lax.dynamic_slice_in_dim(total, c * 256, 256, 0).astype(BF16)
    there = lax.dynamic_slice_in_dim(total, (1 - c) * 256, 256, 0).astype(BF16)
    there = across_core(there)
    return jnp.where(
        first_core,
        jnp.concatenate([here, there], axis=1),
        jnp.concatenate([there, here], axis=1),
    )


def solution(mesh):
    fine = Mesh(mesh.devices.reshape(SIZES), AXES)
    placed = (
        P(WIDE, NARROW),
        P(),
        P(),
        P(WIDE, None),
        P(NARROW, WIDE),
        P(NARROW, WIDE),
        P(NARROW, WIDE),
        P(WIDE, NARROW),
        P(),
        P(),
    )
    return jax.shard_map(
        on_device, mesh=fine, in_specs=placed, out_specs=P(WIDE, NARROW), check_vma=False
    )
```

```python
import functools
import math

import jax
import jax.numpy as jnp
from jax import lax
from jax.experimental import pallas as pl
from jax.experimental.pallas import tpu as pltpu
from jax.sharding import Mesh
from jax.sharding import PartitionSpec as P

H = 128
E = 8
EPS = 1e-06
FLOOR = -1e30
AXES = ("xl", "y", "c", "z", "xh")
SIZES = (2, 4, 2, 4, 2)
WIDE = ("xl", "y", "c")
NARROW = ("z", "xh")
BF16 = jnp.bfloat16
F32 = jnp.float32
SCALE2 = H ** (-0.5) * math.log2(math.e)
CK = 512
R = 512
CHUNKS = 8
TILES = 8
DUMMY = 8
UNROLL = 4

SMEM = pl.BlockSpec(memory_space=pltpu.SMEM)
VMEM = pl.BlockSpec(memory_space=pltpu.VMEM)
HBM = pl.BlockSpec(memory_space=pltpu.HBM)
ANY = pl.BlockSpec(memory_space=pl.ANY)


def along_y(x, k):
    return lax.ppermute(x, "y", [(i, (i + k) % 4) for i in range(4)])


def across_x(x):
    return lax.ppermute(x, "xl", [(0, 1), (1, 0)])


def across_core(x):
    return lax.ppermute(x, "c", [(0, 1), (1, 0)])


def tie(a, b):
    return lax.optimization_barrier((a, b))


def chip_order():
    xl, y = lax.axis_index("xl"), lax.axis_index("y")
    return [(xl ^ dx) * 4 + lax.rem(y + dy, 4) for dy in range(4) for dx in range(2)]


def pin(arrays):
    return [pltpu.with_memory_space_constraint(a, pltpu.HBM) for a in arrays]


def nt_dot(a, b):
    return lax.dot_general(a, b, (((1,), (1,)), ((), ())), preferred_element_type=F32)


def run(copies):
    for c in copies:
        c.start()
    for c in copies:
        c.wait()


def norm_kernel(idx, gain, blocks, normed, held, sem):
    run([pltpu.make_async_copy(blocks, held, sem.at[0])])
    total = jnp.zeros((256, 1), F32)
    for k in range(8):
        v = held[k].astype(F32)
        total = total + jnp.sum(v * v, axis=1, keepdims=True)
    scale = lax.rsqrt(total * (1.0 / 2048) + EPS)
    for k in range(8):
        v = held[k].astype(F32) * scale * gain[k].astype(F32)
        normed[:, pl.ds(pl.multiple_of(idx[k] * 256, 256), 256)] = v.astype(BF16)


def normalise(idx, gain, blocks):
    return pl.pallas_call(
        norm_kernel,
        out_shape=jax.ShapeDtypeStruct((256, 2048), BF16),
        in_specs=[SMEM, VMEM, ANY],
        out_specs=VMEM,
        scratch_shapes=[pltpu.VMEM((8, 256, 256), BF16), pltpu.SemaphoreType.DMA((1,))],
        compiler_params=pltpu.CompilerParams(vmem_limit_bytes=8 << 20),
        cost_estimate=pl.CostEstimate(flops=1 << 24, bytes_accessed=2 << 20, transcendentals=0),
        name="normalise",
    )(idx, gain, blocks)


GROUPS = ((0, 512), (512, 768))


def project_kernel(idx, routes, router, own, other, *refs):
    blocks = refs[:8]
    q_out, kv_out, gates, xs, held, sel, sem = refs[8:]
    core = idx[8]
    copies = []
    for i, r in enumerate((own, other)):
        at = pl.multiple_of((core if i == 0 else 1 - core) * 256, 256)
        copies.append(pltpu.make_async_copy(r, xs.at[pl.ds(at, 256)], sem.at[32 + i]))
    for g, (start, rows) in enumerate(GROUPS):
        for k in range(16):
            lane = (k // 2) * 256 + H * (core if k % 2 == 0 else 1 - core)
            at = pl.ds(pl.multiple_of(lane, H), H)
            copies.append(
                pltpu.make_async_copy(
                    blocks[k // 2].at[k % 2, pl.ds(start, rows)],
                    held.at[pl.ds(start, rows), at],
                    sem.at[16 * g + k],
                )
            )
    for c in copies:
        c.start()
    for c in copies[:2]:
        c.wait()
    logits = jnp.zeros((512, E), F32)
    for i in range(8):
        part = router[:, pl.ds(pl.multiple_of(idx[i] * 256, 256), 256)]
        logits += nt_dot(xs[:, i * 256 : (i + 1) * 256], part)
    lane = lax.broadcasted_iota(jnp.int32, (512, E), 1)
    chosen = [
        jnp.sum(jnp.where(routes[:, j : j + 1] == lane, logits, 0.0), axis=1, keepdims=True)
        for j in range(2)
    ]
    top = jnp.maximum(chosen[0], chosen[1])
    e0, e1 = jnp.exp(chosen[0] - top), jnp.exp(chosen[1] - top)
    gates[:, 0:1] = e0 / (e0 + e1)
    gates[:, 1:2] = e1 / (e0 + e1)

    for r in range(5):
        if r == 0:
            for c in copies[2:18]:
                c.wait()
        if r == 2:
            for c in copies[18:]:
                c.wait()
        acc = nt_dot(xs[...], held[r * 256 : (r + 1) * 256])
        if r == 4:
            kv_out[...] = acc.astype(BF16)
            continue
        for j in range(2):
            value = jnp.zeros((512, H), F32) if r == 0 else sel[j]
            for e in range(2):
                hit = routes[:, j : j + 1] == 2 * r + e
                value = jnp.where(hit, acc[:, e * H : (e + 1) * H], value)
            if r < 3:
                sel[j] = value
            else:
                for half in range(2):
                    at = (half * 2 + j) * 256
                    q_out[at : at + 256] = value[half * 256 : (half + 1) * 256].astype(BF16)


def project(idx, routes, router, own, other, blocks):
    return pl.pallas_call(
        project_kernel,
        out_shape=(
            jax.ShapeDtypeStruct((1024, H), BF16),
            jax.ShapeDtypeStruct((512, 2 * H), BF16),
            jax.ShapeDtypeStruct((512, 2), F32),
        ),
        in_specs=[SMEM, VMEM, VMEM] + [HBM] * 10,
        out_specs=(VMEM, VMEM, VMEM),
        scratch_shapes=[
            pltpu.VMEM((512, 2048), BF16),
            pltpu.VMEM((1280, 2048), BF16),
            pltpu.VMEM((2, 512, H), F32),
            pltpu.SemaphoreType.DMA((34,)),
        ],
        compiler_params=pltpu.CompilerParams(vmem_limit_bytes=20 << 20),
        cost_estimate=pl.CostEstimate(flops=6 << 30, bytes_accessed=8 << 20, transcendentals=0),
        name="project",
    )(idx, routes, router, *pin([own, other, *blocks]))


def attend_kernel(idx, ends_s, ends_p, q0, q1, q2, q3, cache0, cache1, kv0, kv1, *refs):
    outs = refs[:4]
    q, keep, limits, top, tot, acc, sa, sb, chunk_of, tile_of, sem = refs[4:]
    core = idx[0]
    copies = [
        pltpu.make_async_copy(r, q.at[pl.ds(1024 * b, 1024)], sem.at[b])
        for b, r in enumerate((q0, q1, q2, q3))
    ]
    for i, r in enumerate((cache0, cache1)):
        for side in range(2):
            at = pl.multiple_of(i * 1536 + 768 * (core if side == 0 else 1 - core), 256)
            copies.append(
                pltpu.make_async_copy(r.at[side], keep.at[pl.ds(at, 768)], sem.at[4 + 2 * i + side])
            )
    for i, r in enumerate((kv0, kv1)):
        copies.append(
            pltpu.make_async_copy(r, keep.at[pl.ds(3072 + 512 * i, 512)], sem.at[8 + i])
        )
    for c in copies:
        c.start()

    se, pe = [ends_s[0]], [ends_p[0]]
    for k in range(1, 4):
        se.append(se[-1] + ends_s[k])
        pe.append(pe[-1] + ends_p[k])

    def allowed_of(token):
        lo, hi, own = 0 * token, 0 * token + pe[0], 0 * token
        for k in range(3):
            later = token >= se[k]
            lo = jnp.where(later, pe[k], lo)
            hi = jnp.where(later, pe[k + 1], hi)
            own = jnp.where(later, se[k], own)
        return lo, hi, own

    for t in range(TILES):
        first = idx[1 + t // 2] + (t % 2) * 256
        token = first + lax.rem(lax.broadcasted_iota(jnp.int32, (1, R), 1), 256)
        lo, hi, own = allowed_of(token)
        limits[t, 0:1] = lo
        limits[t, 1:2] = hi
        limits[t, 2:3] = own
        limits[t, 3:4] = token + 1
    limits[DUMMY] = jnp.zeros((4, R), jnp.int32)
    top[...] = jnp.full(top.shape, FLOOR, F32)
    tot[...] = jnp.zeros(tot.shape, F32)
    acc[...] = jnp.zeros(acc.shape, F32)

    def base_of(i):
        slot = jnp.where(i < 3, idx[5] + i * CK, idx[6] + (i - 3) * CK)
        return jnp.where(i < 6, slot, jnp.where(i == 6, idx[7], idx[8]))

    def collect(want_full, start):
        def visit(n, count):
            i, t = n // TILES, lax.rem(n, TILES)
            base = base_of(i)
            first = idx[1 + t // 2] + lax.rem(t, 2) * 256
            last = first + 255
            lo_a, hi_a, own_a = allowed_of(first)
            lo_b, hi_b, own_b = allowed_of(last)
            pre = i < 6
            lo_first, lo_last = jnp.where(pre, lo_a, own_a), jnp.where(pre, lo_b, own_b)
            hi_first, hi_last = jnp.where(pre, hi_a, first + 1), jnp.where(pre, hi_b, last + 1)
            some = (base + CK > lo_first) & (base < hi_last)
            full = (base >= lo_last) & (base + CK <= hi_first)
            hit = full if want_full else (some & jnp.logical_not(full))

            @pl.when(hit)
            def _():
                chunk_of[count] = i
                tile_of[count] = t

            return count + hit.astype(jnp.int32)

        count = lax.fori_loop(0, CHUNKS * TILES, visit, start)
        rounds = (count + UNROLL - 1) // UNROLL
        for k in range(UNROLL):
            chunk_of[count + k] = 0
            tile_of[count + k] = DUMMY
        return rounds

    full_rounds = collect(True, 0)
    all_rounds = collect(False, full_rounds * UNROLL)
    for c in copies:
        c.wait()
    q[4096:4608] = jnp.zeros((R, H), BF16)

    def scores(n, out):
        keys = keep[pl.ds(pl.multiple_of(chunk_of[n] * CK, CK), CK), :H]
        out[...] = nt_dot(keys, q[pl.ds(pl.multiple_of(tile_of[n] * R, R), R), :])

    def consume(n, s_ref, masked):
        i, t = chunk_of[n], tile_of[n]
        s = s_ref[...]
        if masked:
            pos = base_of(i) + lax.broadcasted_iota(jnp.int32, (CK, R), 0)
            kind = jnp.where(i < 6, 0, 2)
            lo, hi = limits[t, pl.ds(kind, 1)], limits[t, pl.ds(kind + 1, 1)]
            s = jnp.where((pos >= lo) & (pos < hi), s, -jnp.inf)
        old = top[t]
        new = jnp.maximum(old, jnp.max(s, axis=0, keepdims=True))
        p = jnp.exp2(s * SCALE2 - new * SCALE2)
        factor = jnp.exp2((old - new) * SCALE2)
        top[t] = new
        tot[t] = tot[t] * factor + jnp.sum(p, axis=0, keepdims=True)
        values = keep[pl.ds(pl.multiple_of(i * CK, CK), CK), H:]
        acc[t] = acc[t] * factor + lax.dot_general(
            values, p.astype(BF16), (((0,), (0,)), ((), ())), preferred_element_type=F32
        )

    def rounds(masked):
        def body(n, _):
            for k in range(UNROLL):
                cur, nxt = (sa, sb) if k % 2 == 0 else (sb, sa)
                scores(n * UNROLL + k + 1, nxt)
                consume(n * UNROLL + k, cur, masked)
            return 0

        return body

    chunk_of[all_rounds * UNROLL] = 0
    tile_of[all_rounds * UNROLL] = DUMMY
    scores(0, sa)
    lax.fori_loop(0, full_rounds, rounds(False), 0)
    lax.fori_loop(full_rounds, all_rounds, rounds(True), 0)

    for t in range(TILES):
        total = tot[t]
        safe = jnp.where(total > 0.0, total, 1.0)
        cols = slice((t % 2) * R, (t % 2 + 1) * R)
        out = outs[t // 2]
        out[0:H, cols] = (acc[t] / safe).astype(BF16)
        lse = jnp.where(total > 0.0, top[t] * SCALE2 + jnp.log2(safe), FLOOR)
        high = lse.astype(BF16).astype(F32)
        mid = (lse - high).astype(BF16).astype(F32)
        low = lse - high - mid
        row = lax.broadcasted_iota(jnp.int32, (16, R), 0)
        packed = jnp.where(row == 0, high, jnp.where(row == 1, mid, jnp.where(row == 2, low, 0.0)))
        out[H : H + 16, cols] = packed.astype(BF16)


def attend(idx, suffix_lengths, prefix_lengths, qs, caches, kvs):
    return pl.pallas_call(
        attend_kernel,
        out_shape=tuple(jax.ShapeDtypeStruct((H + 16, 1024), BF16) for _ in range(4)),
        in_specs=[SMEM] * 3 + [HBM] * 8,
        out_specs=tuple([VMEM] * 4),
        scratch_shapes=[
            pltpu.VMEM((9 * R, H), BF16),
            pltpu.VMEM((CHUNKS * CK, 2 * H), BF16),
            pltpu.VMEM((TILES + 1, 4, R), jnp.int32),
            pltpu.VMEM((TILES + 1, 1, R), F32),
            pltpu.VMEM((TILES + 1, 1, R), F32),
            pltpu.VMEM((TILES + 1, H, R), F32),
            pltpu.VMEM((CK, R), F32),
            pltpu.VMEM((CK, R), F32),
            pltpu.SMEM((CHUNKS * TILES + 4 * UNROLL,), jnp.int32),
            pltpu.SMEM((CHUNKS * TILES + 4 * UNROLL,), jnp.int32),
            pltpu.SemaphoreType.DMA((10,)),
        ],
        compiler_params=pltpu.CompilerParams(vmem_limit_bytes=20 << 20),
        cost_estimate=pl.CostEstimate(
            flops=12 << 30, bytes_accessed=6 << 20, transcendentals=10 << 20
        ),
        name="attend",
    )(idx, suffix_lengths, prefix_lengths, *pin([*qs, *caches, *kvs]))


def combine_kernel(gates, p0, p1, p2, p3, out):
    parts = (p0, p1, p2, p3)
    lses = []
    for p in parts:
        rows = p[H : H + 16].astype(F32)
        lses.append(rows[0:1] + rows[1:2] + rows[2:3])
    high = jnp.maximum(jnp.maximum(lses[0], lses[1]), jnp.maximum(lses[2], lses[3]))
    share = [jnp.exp2(v - high) for v in lses]
    norm = gates[...] / (share[0] + share[1] + share[2] + share[3])
    for at in range(0, 1024, 256):
        cols = slice(at, at + 256)
        total = jnp.zeros((H, 256), F32)
        for p, s in zip(parts, share):
            total += p[0:H, cols].astype(F32) * s[:, cols]
        out[cols] = jnp.transpose(total * norm[:, cols]).astype(BF16)


def combine(gates, parts):
    return pl.pallas_call(
        combine_kernel,
        out_shape=jax.ShapeDtypeStruct((1024, H), BF16),
        in_specs=[VMEM] * 5,
        out_specs=VMEM,
        compiler_params=pltpu.CompilerParams(vmem_limit_bytes=8 << 20),
        cost_estimate=pl.CostEstimate(flops=1 << 22, bytes_accessed=2 << 20, transcendentals=0),
        name="combine",
    )(gates, *parts)


def out_kernel(idx, routes, own, other, blocks, out, held, padded, sem):
    core = idx[0]
    copies = [
        pltpu.make_async_copy(blocks.at[pl.ds(2 * k, 2)], held.at[pl.ds(2 * k, 2)], sem.at[k])
        for k in range(4)
    ]
    for c in copies:
        c.start()
    for side, source in enumerate((own, other)):
        for half in range(2):
            for e in range(E):
                value = jnp.zeros((256, H), F32)
                for j in range(2):
                    hit = routes[half * 256 : (half + 1) * 256, j : j + 1] == e
                    at = (half * 2 + j) * 256
                    value = jnp.where(hit, source[at : at + 256].astype(F32), value)
                padded[side, half * 256 : (half + 1) * 256, e * H : (e + 1) * H] = value.astype(
                    BF16
                )
    for k in range(0, 8, 2):
        copies[k // 2].wait()
        value = jnp.zeros((512, 256), F32)
        for side in range(2):
            head = core if side == 0 else 1 - core
            rows = pl.ds(pl.multiple_of(head * 1024, 1024), 1024)
            w = jnp.concatenate([held[k, rows], held[k + 1, rows]], axis=1)
            value += jnp.dot(padded[side], w, preferred_element_type=F32)
        for s in range(2):
            out[k + s] = value[:, s * H : (s + 1) * H].astype(BF16)


def project_out(idx, routes, own, other, blocks):
    return pl.pallas_call(
        out_kernel,
        out_shape=jax.ShapeDtypeStruct((8, 512, H), BF16),
        in_specs=[SMEM, VMEM, VMEM, VMEM, HBM],
        out_specs=VMEM,
        scratch_shapes=[
            pltpu.VMEM((8, 2048, H), BF16),
            pltpu.VMEM((2, 512, 1024), BF16),
            pltpu.SemaphoreType.DMA((4,)),
        ],
        compiler_params=pltpu.CompilerParams(vmem_limit_bytes=20 << 20),
        cost_estimate=pl.CostEstimate(flops=4 << 30, bytes_accessed=6 << 20, transcendentals=0),
        name="project_out",
    )(idx, routes, own, other, *pin([blocks]))


def on_device(
    tokens,
    norm_gain,
    router,
    routes,
    kv_weight,
    query_weight,
    out_weight,
    prefix_cache,
    suffix_lengths,
    prefix_lengths,
):
    xl, y, c = (lax.axis_index(a) for a in WIDE)
    first_core = c == 0
    chips = chip_order()
    blocks = lax.all_gather(tokens, NARROW, axis=0)

    def table(values):
        return jnp.stack([jnp.asarray(v, jnp.int32) for v in values])

    def head_rows(w, h):
        rows = w.shape[0] // 2
        return lax.dynamic_slice_in_dim(w, h * rows, rows, 0)

    def weights_of(h):
        return jnp.concatenate([head_rows(query_weight, h), head_rows(kv_weight, h)], axis=0)

    w = jnp.stack([weights_of(c), across_core(weights_of(1 - c))])
    other_routes = across_core(routes)
    both_routes = jnp.where(
        first_core,
        jnp.concatenate([routes, other_routes]),
        jnp.concatenate([other_routes, routes]),
    )

    def cache_of(h):
        return lax.dynamic_slice_in_dim(prefix_cache, h * 2 * H, 2 * H, 1)

    cache = jnp.stack([cache_of(c), across_core(cache_of(1 - c))])
    far, ym, yp, a = along_y(w, 2), along_y(w, 3), along_y(w, 1), across_x(w)
    caches = [cache, across_x(cache)]
    far, ym, yp, a, caches = lax.optimization_barrier((far, ym, yp, a, caches))
    am, ap, afar = along_y(a, 3), along_y(a, 1), across_x(far)
    gathered = [w, a, ym, am, far, afar, yp, ap]

    places = [(k % 4 - y + 4) % 4 * 2 + (k // 4 ^ xl) for k in range(8)]
    normed = normalise(table(places), norm_gain.reshape(8, 1, 256), blocks)
    q, kv, gates = project(
        table(chips + [c]), both_routes, router.T, normed, across_core(normed), gathered
    )
    late, q = tie(out_weight, q)
    out_all = lax.all_gather(late, ("xl", "y"), axis=0)
    kvs = [kv, across_x(kv)]
    qs = [q] + [along_y(q, k) for k in (1, 2, 3)]

    firsts = [(xl * 4 + lax.rem(y + 4 - k, 4)) * 512 for k in range(4)]
    mine, partner = xl * 4 + y, (1 - xl) * 4 + y
    at = [c] + firsts + [mine * 1536, partner * 1536, mine * 512, partner * 512]
    parts = list(attend(table(at), suffix_lengths, prefix_lengths, qs, caches, kvs))
    for k in range(1, 4):
        parts[k] = along_y(parts[k], 4 - k)
    gate_row = gates.reshape(2, 256, 2).transpose(0, 2, 1).reshape(1, 1024)
    attended = combine(gate_row, parts)

    sums = project_out(
        table([c]), both_routes, attended, across_core(attended), out_all
    )
    sums = lax.all_to_all(sums, NARROW, 0, 0, tiled=True)
    total = jnp.sum(sums.astype(F32), axis=0)
    here = lax.dynamic_slice_in_dim(total, c * 256, 256, 0).astype(BF16)
    there = lax.dynamic_slice_in_dim(total, (1 - c) * 256, 256, 0).astype(BF16)
    there = across_core(there)
    return jnp.where(
        first_core,
        jnp.concatenate([here, there], axis=1),
        jnp.concatenate([there, here], axis=1),
    )


def solution(mesh):
    fine = Mesh(mesh.devices.reshape(SIZES), AXES)
    placed = (
        P(WIDE, NARROW),
        P(),
        P(),
        P(WIDE, None),
        P(NARROW, WIDE),
        P(NARROW, WIDE),
        P(NARROW, WIDE),
        P(WIDE, NARROW),
        P(),
        P(),
    )
    return jax.shard_map(
        on_device, mesh=fine, in_specs=placed, out_specs=P(WIDE, NARROW), check_vma=False
    )
```

```python
import functools
import math

import jax
import jax.numpy as jnp
from jax import lax
from jax.experimental import pallas as pl
from jax.experimental.pallas import tpu as pltpu
from jax.sharding import Mesh
from jax.sharding import PartitionSpec as P

H = 128
E = 8
EPS = 1e-06
FLOOR = -1e30
AXES = ("xl", "y", "c", "z", "xh")
SIZES = (2, 4, 2, 4, 2)
WIDE = ("xl", "y", "c")
NARROW = ("z", "xh")
BF16 = jnp.bfloat16
F32 = jnp.float32
SCALE2 = H ** (-0.5) * math.log2(math.e)
CK = 512
R = 512
CHUNKS = 8
TILES = 8
DUMMY = 8
UNROLL = 4

SMEM = pl.BlockSpec(memory_space=pltpu.SMEM)
VMEM = pl.BlockSpec(memory_space=pltpu.VMEM)
HBM = pl.BlockSpec(memory_space=pltpu.HBM)
ANY = pl.BlockSpec(memory_space=pl.ANY)


def along_y(x, k):
    return lax.ppermute(x, "y", [(i, (i + k) % 4) for i in range(4)])


def across_x(x):
    return lax.ppermute(x, "xl", [(0, 1), (1, 0)])


def across_far(x):
    return lax.ppermute(x, "xh", [(0, 1), (1, 0)])


def along_z(x, k):
    return lax.ppermute(x, "z", [(i, (i + k) % 4) for i in range(4)])


def across_core(x):
    return lax.ppermute(x, "c", [(0, 1), (1, 0)])


def tie(a, b):
    return lax.optimization_barrier((a, b))


def chip_order():
    xl, y = lax.axis_index("xl"), lax.axis_index("y")
    return [(xl ^ dx) * 4 + lax.rem(y + dy, 4) for dy in range(4) for dx in range(2)]


def pin(arrays):
    return [pltpu.with_memory_space_constraint(a, pltpu.HBM) for a in arrays]


def nt_dot(a, b):
    return lax.dot_general(a, b, (((1,), (1,)), ((), ())), preferred_element_type=F32)


def run(copies):
    for c in copies:
        c.start()
    for c in copies:
        c.wait()


def norm_kernel(idx, gain, b0, b1, b2, b3, normed, held, sem):
    refs = (b0, b1, b2, b3)
    run([pltpu.make_async_copy(r, held.at[i], sem.at[i]) for i, r in enumerate(refs)])
    total = jnp.zeros((256, 1), F32)
    for k in range(8):
        v = held[k // 2, k % 2].astype(F32)
        total = total + jnp.sum(v * v, axis=1, keepdims=True)
    scale = lax.rsqrt(total * (1.0 / 2048) + EPS)
    for k in range(8):
        v = held[k // 2, k % 2].astype(F32) * scale * gain[idx[k]].astype(F32)
        normed[:, pl.ds(pl.multiple_of(idx[8 + k] * 256, 256), 256)] = v.astype(BF16)


def normalise(idx, gain, blocks):
    return pl.pallas_call(
        norm_kernel,
        out_shape=jax.ShapeDtypeStruct((256, 2048), BF16),
        in_specs=[SMEM, VMEM] + [ANY] * 4,
        out_specs=VMEM,
        scratch_shapes=[pltpu.VMEM((4, 2, 256, 256), BF16), pltpu.SemaphoreType.DMA((4,))],
        compiler_params=pltpu.CompilerParams(vmem_limit_bytes=8 << 20),
        cost_estimate=pl.CostEstimate(flops=1 << 24, bytes_accessed=2 << 20, transcendentals=0),
        name="normalise",
    )(idx, gain, *blocks)


GROUPS = ((0, 512), (512, 768))


def project_kernel(idx, routes, router, own, other, *refs):
    blocks = refs[:8]
    q_out, kv_out, gates, xs, held, sel, sem = refs[8:]
    core = idx[8]
    copies = []
    for i, r in enumerate((own, other)):
        at = pl.multiple_of((core if i == 0 else 1 - core) * 256, 256)
        copies.append(pltpu.make_async_copy(r, xs.at[pl.ds(at, 256)], sem.at[32 + i]))
    for g, (start, rows) in enumerate(GROUPS):
        for k in range(16):
            lane = (k // 2) * 256 + H * (core if k % 2 == 0 else 1 - core)
            at = pl.ds(pl.multiple_of(lane, H), H)
            copies.append(
                pltpu.make_async_copy(
                    blocks[k // 2].at[k % 2, pl.ds(start, rows)],
                    held.at[pl.ds(start, rows), at],
                    sem.at[16 * g + k],
                )
            )
    for c in copies:
        c.start()
    for c in copies[:2]:
        c.wait()
    logits = jnp.zeros((512, E), F32)
    for i in range(8):
        part = router[:, pl.ds(pl.multiple_of(idx[i] * 256, 256), 256)]
        logits += nt_dot(xs[:, i * 256 : (i + 1) * 256], part)
    lane = lax.broadcasted_iota(jnp.int32, (512, E), 1)
    chosen = [
        jnp.sum(jnp.where(routes[:, j : j + 1] == lane, logits, 0.0), axis=1, keepdims=True)
        for j in range(2)
    ]
    top = jnp.maximum(chosen[0], chosen[1])
    e0, e1 = jnp.exp(chosen[0] - top), jnp.exp(chosen[1] - top)
    gates[:, 0:1] = e0 / (e0 + e1)
    gates[:, 1:2] = e1 / (e0 + e1)

    for r in range(5):
        if r == 0:
            for c in copies[2:18]:
                c.wait()
        if r == 2:
            for c in copies[18:]:
                c.wait()
        acc = nt_dot(xs[...], held[r * 256 : (r + 1) * 256])
        if r == 4:
            kv_out[...] = acc.astype(BF16)
            continue
        for j in range(2):
            value = jnp.zeros((512, H), F32) if r == 0 else sel[j]
            for e in range(2):
                hit = routes[:, j : j + 1] == 2 * r + e
                value = jnp.where(hit, acc[:, e * H : (e + 1) * H], value)
            if r < 3:
                sel[j] = value
            else:
                for half in range(2):
                    at = (half * 2 + j) * 256
                    q_out[at : at + 256] = value[half * 256 : (half + 1) * 256].astype(BF16)


def project(idx, routes, router, own, other, blocks):
    return pl.pallas_call(
        project_kernel,
        out_shape=(
            jax.ShapeDtypeStruct((1024, H), BF16),
            jax.ShapeDtypeStruct((512, 2 * H), BF16),
            jax.ShapeDtypeStruct((512, 2), F32),
        ),
        in_specs=[SMEM, VMEM, VMEM] + [HBM] * 10,
        out_specs=(VMEM, VMEM, VMEM),
        scratch_shapes=[
            pltpu.VMEM((512, 2048), BF16),
            pltpu.VMEM((1280, 2048), BF16),
            pltpu.VMEM((2, 512, H), F32),
            pltpu.SemaphoreType.DMA((34,)),
        ],
        compiler_params=pltpu.CompilerParams(vmem_limit_bytes=20 << 20),
        cost_estimate=pl.CostEstimate(flops=6 << 30, bytes_accessed=8 << 20, transcendentals=0),
        name="project",
    )(idx, routes, router, *pin([own, other, *blocks]))


def attend_kernel(idx, ends_s, ends_p, q0, q1, q2, q3, cache0, cache1, kv0, kv1, *refs):
    outs = refs[:4]
    q, keep, limits, top, tot, acc, sa, sb, chunk_of, tile_of, sem = refs[4:]
    core = idx[0]
    copies = [
        pltpu.make_async_copy(r, q.at[pl.ds(1024 * b, 1024)], sem.at[b])
        for b, r in enumerate((q0, q1, q2, q3))
    ]
    for i, r in enumerate((cache0, cache1)):
        for side in range(2):
            at = pl.multiple_of(i * 1536 + 768 * (core if side == 0 else 1 - core), 256)
            copies.append(
                pltpu.make_async_copy(r.at[side], keep.at[pl.ds(at, 768)], sem.at[4 + 2 * i + side])
            )
    for i, r in enumerate((kv0, kv1)):
        copies.append(
            pltpu.make_async_copy(r, keep.at[pl.ds(3072 + 512 * i, 512)], sem.at[8 + i])
        )
    for c in copies:
        c.start()

    se, pe = [ends_s[0]], [ends_p[0]]
    for k in range(1, 4):
        se.append(se[-1] + ends_s[k])
        pe.append(pe[-1] + ends_p[k])

    def allowed_of(token):
        lo, hi, own = 0 * token, 0 * token + pe[0], 0 * token
        for k in range(3):
            later = token >= se[k]
            lo = jnp.where(later, pe[k], lo)
            hi = jnp.where(later, pe[k + 1], hi)
            own = jnp.where(later, se[k], own)
        return lo, hi, own

    for t in range(TILES):
        first = idx[1 + t // 2] + (t % 2) * 256
        token = first + lax.rem(lax.broadcasted_iota(jnp.int32, (1, R), 1), 256)
        lo, hi, own = allowed_of(token)
        limits[t, 0:1] = lo
        limits[t, 1:2] = hi
        limits[t, 2:3] = own
        limits[t, 3:4] = token + 1
    limits[DUMMY] = jnp.zeros((4, R), jnp.int32)
    top[...] = jnp.full(top.shape, FLOOR, F32)
    tot[...] = jnp.zeros(tot.shape, F32)
    acc[...] = jnp.zeros(acc.shape, F32)

    def base_of(i):
        slot = jnp.where(i < 3, idx[5] + i * CK, idx[6] + (i - 3) * CK)
        return jnp.where(i < 6, slot, jnp.where(i == 6, idx[7], idx[8]))

    def collect(want_full, start):
        def visit(n, count):
            i, t = n // TILES, lax.rem(n, TILES)
            base = base_of(i)
            first = idx[1 + t // 2] + lax.rem(t, 2) * 256
            last = first + 255
            lo_a, hi_a, own_a = allowed_of(first)
            lo_b, hi_b, own_b = allowed_of(last)
            pre = i < 6
            lo_first, lo_last = jnp.where(pre, lo_a, own_a), jnp.where(pre, lo_b, own_b)
            hi_first, hi_last = jnp.where(pre, hi_a, first + 1), jnp.where(pre, hi_b, last + 1)
            some = (base + CK > lo_first) & (base < hi_last)
            full = (base >= lo_last) & (base + CK <= hi_first)
            hit = full if want_full else (some & jnp.logical_not(full))

            @pl.when(hit)
            def _():
                chunk_of[count] = i
                tile_of[count] = t

            return count + hit.astype(jnp.int32)

        count = lax.fori_loop(0, CHUNKS * TILES, visit, start)
        rounds = (count + UNROLL - 1) // UNROLL
        for k in range(UNROLL):
            chunk_of[count + k] = 0
            tile_of[count + k] = DUMMY
        return rounds

    full_rounds = collect(True, 0)
    all_rounds = collect(False, full_rounds * UNROLL)
    for c in copies:
        c.wait()
    q[4096:4608] = jnp.zeros((R, H), BF16)

    def scores(n, out):
        keys = keep[pl.ds(pl.multiple_of(chunk_of[n] * CK, CK), CK), :H]
        out[...] = nt_dot(keys, q[pl.ds(pl.multiple_of(tile_of[n] * R, R), R), :])

    def consume(n, s_ref, masked):
        i, t = chunk_of[n], tile_of[n]
        s = s_ref[...]
        if masked:
            pos = base_of(i) + lax.broadcasted_iota(jnp.int32, (CK, R), 0)
            kind = jnp.where(i < 6, 0, 2)
            lo, hi = limits[t, pl.ds(kind, 1)], limits[t, pl.ds(kind + 1, 1)]
            s = jnp.where((pos >= lo) & (pos < hi), s, -jnp.inf)
        old = top[t]
        new = jnp.maximum(old, jnp.max(s, axis=0, keepdims=True))
        p = jnp.exp2(s * SCALE2 - new * SCALE2)
        factor = jnp.exp2((old - new) * SCALE2)
        top[t] = new
        tot[t] = tot[t] * factor + jnp.sum(p, axis=0, keepdims=True)
        values = keep[pl.ds(pl.multiple_of(i * CK, CK), CK), H:]
        acc[t] = acc[t] * factor + lax.dot_general(
            values, p.astype(BF16), (((0,), (0,)), ((), ())), preferred_element_type=F32
        )

    def rounds(masked):
        def body(n, _):
            for k in range(UNROLL):
                cur, nxt = (sa, sb) if k % 2 == 0 else (sb, sa)
                scores(n * UNROLL + k + 1, nxt)
                consume(n * UNROLL + k, cur, masked)
            return 0

        return body

    chunk_of[all_rounds * UNROLL] = 0
    tile_of[all_rounds * UNROLL] = DUMMY
    scores(0, sa)
    lax.fori_loop(0, full_rounds, rounds(False), 0)
    lax.fori_loop(full_rounds, all_rounds, rounds(True), 0)

    for t in range(TILES):
        total = tot[t]
        safe = jnp.where(total > 0.0, total, 1.0)
        cols = slice((t % 2) * R, (t % 2 + 1) * R)
        out = outs[t // 2]
        out[0:H, cols] = (acc[t] / safe).astype(BF16)
        lse = jnp.where(total > 0.0, top[t] * SCALE2 + jnp.log2(safe), FLOOR)
        high = lse.astype(BF16).astype(F32)
        mid = (lse - high).astype(BF16).astype(F32)
        low = lse - high - mid
        row = lax.broadcasted_iota(jnp.int32, (16, R), 0)
        packed = jnp.where(row == 0, high, jnp.where(row == 1, mid, jnp.where(row == 2, low, 0.0)))
        out[H : H + 16, cols] = packed.astype(BF16)


def attend(idx, suffix_lengths, prefix_lengths, qs, caches, kvs):
    return pl.pallas_call(
        attend_kernel,
        out_shape=tuple(jax.ShapeDtypeStruct((H + 16, 1024), BF16) for _ in range(4)),
        in_specs=[SMEM] * 3 + [HBM] * 8,
        out_specs=tuple([VMEM] * 4),
        scratch_shapes=[
            pltpu.VMEM((9 * R, H), BF16),
            pltpu.VMEM((CHUNKS * CK, 2 * H), BF16),
            pltpu.VMEM((TILES + 1, 4, R), jnp.int32),
            pltpu.VMEM((TILES + 1, 1, R), F32),
            pltpu.VMEM((TILES + 1, 1, R), F32),
            pltpu.VMEM((TILES + 1, H, R), F32),
            pltpu.VMEM((CK, R), F32),
            pltpu.VMEM((CK, R), F32),
            pltpu.SMEM((CHUNKS * TILES + 4 * UNROLL,), jnp.int32),
            pltpu.SMEM((CHUNKS * TILES + 4 * UNROLL,), jnp.int32),
            pltpu.SemaphoreType.DMA((10,)),
        ],
        compiler_params=pltpu.CompilerParams(vmem_limit_bytes=20 << 20),
        cost_estimate=pl.CostEstimate(
            flops=12 << 30, bytes_accessed=6 << 20, transcendentals=10 << 20
        ),
        name="attend",
    )(idx, suffix_lengths, prefix_lengths, *pin([*qs, *caches, *kvs]))


def combine_kernel(gates, p0, p1, p2, p3, out):
    parts = (p0, p1, p2, p3)
    lses = []
    for p in parts:
        rows = p[H : H + 16].astype(F32)
        lses.append(rows[0:1] + rows[1:2] + rows[2:3])
    high = jnp.maximum(jnp.maximum(lses[0], lses[1]), jnp.maximum(lses[2], lses[3]))
    share = [jnp.exp2(v - high) for v in lses]
    norm = gates[...] / (share[0] + share[1] + share[2] + share[3])
    for at in range(0, 1024, 256):
        cols = slice(at, at + 256)
        total = jnp.zeros((H, 256), F32)
        for p, s in zip(parts, share):
            total += p[0:H, cols].astype(F32) * s[:, cols]
        out[cols] = jnp.transpose(total * norm[:, cols]).astype(BF16)


def combine(gates, parts):
    return pl.pallas_call(
        combine_kernel,
        out_shape=jax.ShapeDtypeStruct((1024, H), BF16),
        in_specs=[VMEM] * 5,
        out_specs=VMEM,
        compiler_params=pltpu.CompilerParams(vmem_limit_bytes=8 << 20),
        cost_estimate=pl.CostEstimate(flops=1 << 22, bytes_accessed=2 << 20, transcendentals=0),
        name="combine",
    )(gates, *parts)


def out_kernel(idx, routes, own, other, *refs):
    blocks = refs[:8]
    out, held, padded, sem = refs[8:]
    core = idx[8]
    copies = [
        pltpu.make_async_copy(r, held.at[idx[k]], sem.at[k]) for k, r in enumerate(blocks)
    ]
    for c in copies:
        c.start()
    for side, source in enumerate((own, other)):
        for half in range(2):
            for e in range(E):
                value = jnp.zeros((256, H), F32)
                for j in range(2):
                    hit = routes[half * 256 : (half + 1) * 256, j : j + 1] == e
                    at = (half * 2 + j) * 256
                    value = jnp.where(hit, source[at : at + 256].astype(F32), value)
                padded[side, half * 256 : (half + 1) * 256, e * H : (e + 1) * H] = value.astype(
                    BF16
                )
    for c in copies:
        c.wait()
    for k in range(0, 8, 2):
        value = jnp.zeros((512, 256), F32)
        for side in range(2):
            head = core if side == 0 else 1 - core
            rows = pl.ds(pl.multiple_of(head * 1024, 1024), 1024)
            w = jnp.concatenate([held[k, rows], held[k + 1, rows]], axis=1)
            value += jnp.dot(padded[side], w, preferred_element_type=F32)
        for s in range(2):
            out[k + s] = value[:, s * H : (s + 1) * H].astype(BF16)


def project_out(idx, routes, own, other, blocks):
    return pl.pallas_call(
        out_kernel,
        out_shape=jax.ShapeDtypeStruct((8, 512, H), BF16),
        in_specs=[SMEM, VMEM, VMEM, VMEM] + [HBM] * 8,
        out_specs=VMEM,
        scratch_shapes=[
            pltpu.VMEM((8, 2048, H), BF16),
            pltpu.VMEM((2, 512, 1024), BF16),
            pltpu.SemaphoreType.DMA((8,)),
        ],
        compiler_params=pltpu.CompilerParams(vmem_limit_bytes=20 << 20),
        cost_estimate=pl.CostEstimate(flops=4 << 30, bytes_accessed=6 << 20, transcendentals=0),
        name="project_out",
    )(idx, routes, own, other, *pin(blocks))


def on_device(
    tokens,
    norm_gain,
    router,
    routes,
    kv_weight,
    query_weight,
    out_weight,
    prefix_cache,
    suffix_lengths,
    prefix_lengths,
):
    xl, y, c = (lax.axis_index(a) for a in WIDE)
    first_core = c == 0
    chips = chip_order()

    def table(values):
        return jnp.stack([jnp.asarray(v, jnp.int32) for v in values])

    def head_rows(w, h):
        rows = w.shape[0] // 2
        return lax.dynamic_slice_in_dim(w, h * rows, rows, 0)

    def weights_of(h):
        return jnp.concatenate([head_rows(query_weight, h), head_rows(kv_weight, h)], axis=0)

    w = jnp.stack([weights_of(c), across_core(weights_of(1 - c))])
    other_routes = across_core(routes)
    both_routes = jnp.where(
        first_core,
        jnp.concatenate([routes, other_routes]),
        jnp.concatenate([other_routes, routes]),
    )

    def cache_of(h):
        return lax.dynamic_slice_in_dim(prefix_cache, h * 2 * H, 2 * H, 1)

    cache = jnp.stack([cache_of(c), across_core(cache_of(1 - c))])
    pair = jnp.stack([tokens, across_far(tokens)])
    far, ym, yp, a = along_y(w, 2), along_y(w, 3), along_y(w, 1), across_x(w)
    caches = [cache, across_x(cache)]
    far, ym, yp, a, pair, caches = lax.optimization_barrier((far, ym, yp, a, pair, caches))
    blocks = [pair] + [along_z(pair, k) for k in (1, 2, 3)]
    am, ap, afar = along_y(a, 3), along_y(a, 1), across_x(far)
    blocks, am, ap, afar = lax.optimization_barrier((blocks, am, ap, afar))
    gathered = [w, a, ym, am, far, afar, yp, ap]

    z, xh = (lax.axis_index(a) for a in NARROW)
    token_src = [lax.rem(z + 4 - dz, 4) * 2 + (xh ^ s) for dz in range(4) for s in range(2)]
    places = [lax.rem(lax.rem(v, 4) + 4 - y, 4) * 2 + (v // 4 ^ xl) for v in token_src]
    normed = normalise(table(token_src + places), norm_gain.reshape(8, 1, 256), blocks)
    out_early, am, ap = lax.optimization_barrier((out_weight, am, ap))
    gathered[3], gathered[7] = am, ap
    o_ym, o_yp, o_a = along_y(out_early, 3), along_y(out_early, 1), across_x(out_early)
    q, kv, gates = project(
        table(chips + [c]), both_routes, router.T, normed, across_core(normed), gathered
    )
    kvs = [kv, across_x(kv)]
    qs = [q] + [along_y(q, k) for k in (1, 2, 3)]
    qs[0], o_ym, o_yp = lax.optimization_barrier((q, o_ym, o_yp))
    out_late, o_a_late, kvs[1] = lax.optimization_barrier((out_weight, o_a, kvs[1]))
    o_far, o_am, o_ap = along_y(out_late, 2), along_y(o_a_late, 3), along_y(o_a_late, 1)

    firsts = [(xl * 4 + lax.rem(y + 4 - k, 4)) * 512 for k in range(4)]
    mine, partner = xl * 4 + y, (1 - xl) * 4 + y
    at = [c] + firsts + [mine * 1536, partner * 1536, mine * 512, partner * 512]
    parts = list(attend(table(at), suffix_lengths, prefix_lengths, qs, caches, kvs))
    parts[1:], o_far, o_am, o_ap = lax.optimization_barrier((parts[1:], o_far, o_am, o_ap))
    for k in range(1, 4):
        parts[k] = along_y(parts[k], 4 - k)
    out_blocks = [out_weight, o_a, o_ym, o_am, o_far, across_x(o_far), o_yp, o_ap]
    gate_row = gates.reshape(2, 256, 2).transpose(0, 2, 1).reshape(1, 1024)
    attended = combine(gate_row, parts)

    sums = project_out(
        table(chips + [c]), both_routes, attended, across_core(attended), out_blocks
    )
    sums = lax.all_to_all(sums, NARROW, 0, 0, tiled=True)
    total = jnp.sum(sums.astype(F32), axis=0)
    here = lax.dynamic_slice_in_dim(total, c * 256, 256, 0).astype(BF16)
    there = lax.dynamic_slice_in_dim(total, (1 - c) * 256, 256, 0).astype(BF16)
    there = across_core(there)
    return jnp.where(
        first_core,
        jnp.concatenate([here, there], axis=1),
        jnp.concatenate([there, here], axis=1),
    )


def solution(mesh):
    fine = Mesh(mesh.devices.reshape(SIZES), AXES)
    placed = (
        P(WIDE, NARROW),
        P(),
        P(),
        P(WIDE, None),
        P(NARROW, WIDE),
        P(NARROW, WIDE),
        P(NARROW, WIDE),
        P(WIDE, NARROW),
        P(),
        P(),
    )
    return jax.shard_map(
        on_device, mesh=fine, in_specs=placed, out_specs=P(WIDE, NARROW), check_vma=False
    )
```

```python
import functools
import math

import jax
import jax.numpy as jnp
from jax import lax
from jax.experimental import pallas as pl
from jax.experimental.pallas import tpu as pltpu
from jax.sharding import Mesh
from jax.sharding import PartitionSpec as P

H = 128
E = 8
EPS = 1e-06
FLOOR = -1e30
AXES = ("xl", "y", "c", "z", "xh")
SIZES = (2, 4, 2, 4, 2)
WIDE = ("xl", "y", "c")
NARROW = ("z", "xh")
BF16 = jnp.bfloat16
F32 = jnp.float32
SCALE2 = H ** (-0.5) * math.log2(math.e)
CK = 512
R = 512
CHUNKS = 8
UNROLL = 4

SMEM = pl.BlockSpec(memory_space=pltpu.SMEM)
VMEM = pl.BlockSpec(memory_space=pltpu.VMEM)
HBM = pl.BlockSpec(memory_space=pltpu.HBM)
ANY = pl.BlockSpec(memory_space=pl.ANY)


def along_y(x, k):
    return lax.ppermute(x, "y", [(i, (i + k) % 4) for i in range(4)])


def across_x(x):
    return lax.ppermute(x, "xl", [(0, 1), (1, 0)])


def across_far(x):
    return lax.ppermute(x, "xh", [(0, 1), (1, 0)])


def across_core(x):
    return lax.ppermute(x, "c", [(0, 1), (1, 0)])


def tie(a, b):
    return lax.optimization_barrier((a, b))


def chip_order():
    xl, y = lax.axis_index("xl"), lax.axis_index("y")
    return [(xl ^ dx) * 4 + lax.rem(y + dy, 4) for dy in range(4) for dx in range(2)]


def pin(arrays):
    return [pltpu.with_memory_space_constraint(a, pltpu.HBM) for a in arrays]


def nt_dot(a, b):
    return lax.dot_general(a, b, (((1,), (1,)), ((), ())), preferred_element_type=F32)


def run(copies):
    for c in copies:
        c.start()
    for c in copies:
        c.wait()


def norm_kernel(idx, gain, blocks, normed, held, sem):
    run([pltpu.make_async_copy(blocks, held, sem.at[0])])
    total = jnp.zeros((256, 1), F32)
    for k in range(8):
        v = held[k // 2, k % 2].astype(F32)
        total = total + jnp.sum(v * v, axis=1, keepdims=True)
    scale = lax.rsqrt(total * (1.0 / 2048) + EPS)
    for k in range(8):
        v = held[k // 2, k % 2].astype(F32) * scale * gain[idx[k]].astype(F32)
        normed[:, pl.ds(pl.multiple_of(idx[8 + k] * 256, 256), 256)] = v.astype(BF16)


def normalise(idx, gain, blocks):
    return pl.pallas_call(
        norm_kernel,
        out_shape=jax.ShapeDtypeStruct((256, 2048), BF16),
        in_specs=[SMEM, VMEM, ANY],
        out_specs=VMEM,
        scratch_shapes=[pltpu.VMEM((4, 2, 256, 256), BF16), pltpu.SemaphoreType.DMA((1,))],
        compiler_params=pltpu.CompilerParams(vmem_limit_bytes=8 << 20),
        cost_estimate=pl.CostEstimate(flops=1 << 24, bytes_accessed=2 << 20, transcendentals=0),
        name="normalise",
    )(idx, gain, blocks)


GROUPS = ((0, 512), (512, 768))


def project_kernel(idx, routes, router, own, other, *refs):
    blocks = refs[:8]
    q_out, kv_out, gates, xs, held, sel, sem = refs[8:]
    core = idx[8]
    copies = []
    for i, r in enumerate((own, other)):
        at = pl.multiple_of((core if i == 0 else 1 - core) * 256, 256)
        copies.append(pltpu.make_async_copy(r, xs.at[pl.ds(at, 256)], sem.at[32 + i]))
    for g, (start, rows) in enumerate(GROUPS):
        for k in range(16):
            lane = (k // 2) * 256 + H * (core if k % 2 == 0 else 1 - core)
            at = pl.ds(pl.multiple_of(lane, H), H)
            copies.append(
                pltpu.make_async_copy(
                    blocks[k // 2].at[k % 2, pl.ds(start, rows)],
                    held.at[pl.ds(start, rows), at],
                    sem.at[16 * g + k],
                )
            )
    for c in copies:
        c.start()
    for c in copies[:2]:
        c.wait()
    logits = jnp.zeros((512, E), F32)
    for i in range(8):
        part = router[:, pl.ds(pl.multiple_of(idx[i] * 256, 256), 256)]
        logits += nt_dot(xs[:, i * 256 : (i + 1) * 256], part)
    lane = lax.broadcasted_iota(jnp.int32, (512, E), 1)
    chosen = [
        jnp.sum(jnp.where(routes[:, j : j + 1] == lane, logits, 0.0), axis=1, keepdims=True)
        for j in range(2)
    ]
    top = jnp.maximum(chosen[0], chosen[1])
    e0, e1 = jnp.exp(chosen[0] - top), jnp.exp(chosen[1] - top)
    gates[:, 0:1] = e0 / (e0 + e1)
    gates[:, 1:2] = e1 / (e0 + e1)

    wanted = [jnp.broadcast_to(routes[:, j : j + 1], (512, H)) for j in range(2)]
    for r in range(5):
        if r == 0:
            for c in copies[2:18]:
                c.wait()
        if r == 2:
            for c in copies[18:]:
                c.wait()
        acc = nt_dot(xs[...], held[r * 256 : (r + 1) * 256])
        if r == 4:
            kv_out[...] = acc.astype(BF16)
            continue
        for j in range(2):
            value = jnp.zeros((512, H), F32) if r == 0 else sel[j]
            for e in range(2):
                value = jnp.where(wanted[j] == 2 * r + e, acc[:, e * H : (e + 1) * H], value)
            if r < 3:
                sel[j] = value
            else:
                for half in range(2):
                    at = (half * 2 + j) * 256
                    q_out[at : at + 256] = value[half * 256 : (half + 1) * 256].astype(BF16)


def project(idx, routes, router, own, other, blocks):
    return pl.pallas_call(
        project_kernel,
        out_shape=(
            jax.ShapeDtypeStruct((1024, H), BF16),
            jax.ShapeDtypeStruct((512, 2 * H), BF16),
            jax.ShapeDtypeStruct((512, 2), F32),
        ),
        in_specs=[SMEM, VMEM, VMEM] + [HBM] * 10,
        out_specs=(VMEM, VMEM, VMEM),
        scratch_shapes=[
            pltpu.VMEM((512, 2048), BF16),
            pltpu.VMEM((1280, 2048), BF16),
            pltpu.VMEM((2, 512, H), F32),
            pltpu.SemaphoreType.DMA((34,)),
        ],
        compiler_params=pltpu.CompilerParams(vmem_limit_bytes=20 << 20),
        cost_estimate=pl.CostEstimate(flops=6 << 30, bytes_accessed=8 << 20, transcendentals=0),
        name="project",
    )(idx, routes, router, *pin([own, other, *blocks]))


def attend_kernel(count, idx, ends_s, ends_p, *refs):
    queries, (cache0, cache1, kv0, kv1) = refs[:count], refs[count : count + 4]
    outs = refs[count + 4 : 2 * count + 4]
    q, keep, limits, top, tot, acc, sa, sb, chunk_of, tile_of, sem = refs[2 * count + 4 :]
    tiles = 2 * count
    core = idx[0]
    copies = [
        pltpu.make_async_copy(r, q.at[pl.ds(1024 * b, 1024)], sem.at[b])
        for b, r in enumerate(queries)
    ]
    for i, r in enumerate((cache0, cache1)):
        for side in range(2):
            at = pl.multiple_of(i * 1536 + 768 * (core if side == 0 else 1 - core), 256)
            copies.append(
                pltpu.make_async_copy(r.at[side], keep.at[pl.ds(at, 768)], sem.at[count + 2 * i + side])
            )
    for i, r in enumerate((kv0, kv1)):
        copies.append(
            pltpu.make_async_copy(r, keep.at[pl.ds(3072 + 512 * i, 512)], sem.at[count + 4 + i])
        )
    for c in copies:
        c.start()

    se, pe = [ends_s[0]], [ends_p[0]]
    for k in range(1, 4):
        se.append(se[-1] + ends_s[k])
        pe.append(pe[-1] + ends_p[k])

    def allowed_of(token):
        lo, hi, own = 0 * token, 0 * token + pe[0], 0 * token
        for k in range(3):
            later = token >= se[k]
            lo = jnp.where(later, pe[k], lo)
            hi = jnp.where(later, pe[k + 1], hi)
            own = jnp.where(later, se[k], own)
        return lo, hi, own

    for t in range(tiles):
        first = idx[5 + t // 2] + (t % 2) * 256
        token = first + lax.rem(lax.broadcasted_iota(jnp.int32, (1, R), 1), 256)
        lo, hi, own = allowed_of(token)
        limits[t, 0:1] = lo
        limits[t, 1:2] = hi
        limits[t, 2:3] = own
        limits[t, 3:4] = token + 1
    limits[tiles] = jnp.zeros((4, R), jnp.int32)
    top[...] = jnp.full(top.shape, FLOOR, F32)
    tot[...] = jnp.zeros(tot.shape, F32)
    acc[...] = jnp.zeros(acc.shape, F32)

    def base_of(i):
        slot = jnp.where(i < 3, idx[1] + i * CK, idx[2] + (i - 3) * CK)
        return jnp.where(i < 6, slot, jnp.where(i == 6, idx[3], idx[4]))

    def collect(want_full, start):
        def visit(n, count):
            i, t = n // tiles, lax.rem(n, tiles)
            base = base_of(i)
            first = idx[5 + t // 2] + lax.rem(t, 2) * 256
            last = first + 255
            lo_a, hi_a, own_a = allowed_of(first)
            lo_b, hi_b, own_b = allowed_of(last)
            pre = i < 6
            lo_first, lo_last = jnp.where(pre, lo_a, own_a), jnp.where(pre, lo_b, own_b)
            hi_first, hi_last = jnp.where(pre, hi_a, first + 1), jnp.where(pre, hi_b, last + 1)
            some = (base + CK > lo_first) & (base < hi_last)
            full = (base >= lo_last) & (base + CK <= hi_first)
            hit = full if want_full else (some & jnp.logical_not(full))

            @pl.when(hit)
            def _():
                chunk_of[count] = i
                tile_of[count] = t

            return count + hit.astype(jnp.int32)

        count = lax.fori_loop(0, CHUNKS * tiles, visit, start)
        rounds = (count + UNROLL - 1) // UNROLL
        for k in range(UNROLL):
            chunk_of[count + k] = 0
            tile_of[count + k] = tiles
        return rounds

    full_rounds = collect(True, 0)
    all_rounds = collect(False, full_rounds * UNROLL)
    for c in copies:
        c.wait()
    q[tiles * R : (tiles + 1) * R] = jnp.zeros((R, H), BF16)

    def scores(n, out):
        keys = keep[pl.ds(pl.multiple_of(chunk_of[n] * CK, CK), CK), :H]
        out[...] = nt_dot(keys, q[pl.ds(pl.multiple_of(tile_of[n] * R, R), R), :])

    def consume(n, s_ref, masked):
        i, t = chunk_of[n], tile_of[n]
        s = s_ref[...]
        if masked:
            pos = base_of(i) + lax.broadcasted_iota(jnp.int32, (CK, R), 0)
            kind = jnp.where(i < 6, 0, 2)
            lo, hi = limits[t, pl.ds(kind, 1)], limits[t, pl.ds(kind + 1, 1)]
            s = jnp.where((pos >= lo) & (pos < hi), s, -jnp.inf)
        old = top[t]
        new = jnp.maximum(old, jnp.max(s, axis=0, keepdims=True))
        p = jnp.exp2(s * SCALE2 - new * SCALE2)
        factor = jnp.exp2((old - new) * SCALE2)
        top[t] = new
        tot[t] = tot[t] * factor + jnp.sum(p, axis=0, keepdims=True)
        values = keep[pl.ds(pl.multiple_of(i * CK, CK), CK), H:]
        acc[t] = acc[t] * factor + lax.dot_general(
            values, p.astype(BF16), (((0,), (0,)), ((), ())), preferred_element_type=F32
        )

    def rounds(masked):
        def body(n, _):
            for k in range(UNROLL):
                cur, nxt = (sa, sb) if k % 2 == 0 else (sb, sa)
                scores(n * UNROLL + k + 1, nxt)
                consume(n * UNROLL + k, cur, masked)
            return 0

        return body

    chunk_of[all_rounds * UNROLL] = 0
    tile_of[all_rounds * UNROLL] = tiles
    scores(0, sa)
    lax.fori_loop(0, full_rounds, rounds(False), 0)
    lax.fori_loop(full_rounds, all_rounds, rounds(True), 0)

    for t in range(tiles):
        total = tot[t]
        safe = jnp.where(total > 0.0, total, 1.0)
        cols = slice((t % 2) * R, (t % 2 + 1) * R)
        out = outs[t // 2]
        out[0:H, cols] = (acc[t] / safe).astype(BF16)
        lse = jnp.where(total > 0.0, top[t] * SCALE2 + jnp.log2(safe), FLOOR)
        high = lse.astype(BF16).astype(F32)
        mid = (lse - high).astype(BF16).astype(F32)
        low = lse - high - mid
        row = lax.broadcasted_iota(jnp.int32, (16, R), 0)
        packed = jnp.where(row == 0, high, jnp.where(row == 1, mid, jnp.where(row == 2, low, 0.0)))
        out[H : H + 16, cols] = packed.astype(BF16)


def attend(idx, suffix_lengths, prefix_lengths, qs, caches, kvs):
    count, tiles = len(qs), 2 * len(qs)
    return pl.pallas_call(
        functools.partial(attend_kernel, count),
        out_shape=tuple(jax.ShapeDtypeStruct((H + 16, 1024), BF16) for _ in range(count)),
        in_specs=[SMEM] * 3 + [HBM] * (count + 4),
        out_specs=tuple([VMEM] * count),
        scratch_shapes=[
            pltpu.VMEM(((tiles + 1) * R, H), BF16),
            pltpu.VMEM((CHUNKS * CK, 2 * H), BF16),
            pltpu.VMEM((tiles + 1, 4, R), jnp.int32),
            pltpu.VMEM((tiles + 1, 1, R), F32),
            pltpu.VMEM((tiles + 1, 1, R), F32),
            pltpu.VMEM((tiles + 1, H, R), F32),
            pltpu.VMEM((CK, R), F32),
            pltpu.VMEM((CK, R), F32),
            pltpu.SMEM((CHUNKS * tiles + 4 * UNROLL,), jnp.int32),
            pltpu.SMEM((CHUNKS * tiles + 4 * UNROLL,), jnp.int32),
            pltpu.SemaphoreType.DMA((count + 6,)),
        ],
        compiler_params=pltpu.CompilerParams(vmem_limit_bytes=20 << 20),
        cost_estimate=pl.CostEstimate(
            flops=count * (3 << 30), bytes_accessed=4 << 20, transcendentals=count << 21
        ),
        name="attend",
    )(idx, suffix_lengths, prefix_lengths, *pin([*qs, *caches, *kvs]))


def combine_kernel(gates, p0, p1, p2, p3, out):
    parts = (p0, p1, p2, p3)
    lses = []
    for p in parts:
        rows = p[H : H + 16].astype(F32)
        lses.append(rows[0:1] + rows[1:2] + rows[2:3])
    high = jnp.maximum(jnp.maximum(lses[0], lses[1]), jnp.maximum(lses[2], lses[3]))
    share = [jnp.exp2(v - high) for v in lses]
    norm = gates[...] / (share[0] + share[1] + share[2] + share[3])
    for at in range(0, 1024, 256):
        cols = slice(at, at + 256)
        total = jnp.zeros((H, 256), F32)
        for p, s in zip(parts, share):
            total += p[0:H, cols].astype(F32) * s[:, cols]
        out[cols] = jnp.transpose(total * norm[:, cols]).astype(BF16)


def combine(gates, parts):
    return pl.pallas_call(
        combine_kernel,
        out_shape=jax.ShapeDtypeStruct((1024, H), BF16),
        in_specs=[VMEM] * 5,
        out_specs=VMEM,
        compiler_params=pltpu.CompilerParams(vmem_limit_bytes=8 << 20),
        cost_estimate=pl.CostEstimate(flops=1 << 22, bytes_accessed=2 << 20, transcendentals=0),
        name="combine",
    )(gates, *parts)


def out_kernel(idx, routes, own, other, *refs):
    blocks = refs[:8]
    out, held, padded, sem = refs[8:]
    core = idx[8]
    copies = [
        pltpu.make_async_copy(r, held.at[idx[k]], sem.at[k]) for k, r in enumerate(blocks)
    ]
    for c in copies:
        c.start()
    for half in range(2):
        rows = slice(half * 256, (half + 1) * 256)
        wanted = [jnp.broadcast_to(routes[rows, j : j + 1], (256, H)) for j in range(2)]
        for side, source in enumerate((own, other)):
            head = core if side == 0 else 1 - core
            first = source[half * 512 : half * 512 + 256].astype(F32)
            second = source[half * 512 + 256 : half * 512 + 512].astype(F32)
            for e in range(E):
                value = jnp.where(wanted[1] == e, second, 0.0)
                value = jnp.where(wanted[0] == e, first, value).astype(BF16)
                padded[rows, pl.ds(pl.multiple_of((head * E + e) * H, H), H)] = value
    for c in copies:
        c.wait()
    for k in range(0, 8, 2):
        w = jnp.concatenate([held[k], held[k + 1]], axis=1)
        value = jnp.dot(padded[...], w, preferred_element_type=F32)
        for s in range(2):
            out[k + s] = value[:, s * H : (s + 1) * H].astype(BF16)


def project_out(idx, routes, own, other, blocks):
    return pl.pallas_call(
        out_kernel,
        out_shape=jax.ShapeDtypeStruct((8, 512, H), BF16),
        in_specs=[SMEM, VMEM, VMEM, VMEM] + [HBM] * 8,
        out_specs=VMEM,
        scratch_shapes=[
            pltpu.VMEM((8, 2048, H), BF16),
            pltpu.VMEM((512, 2048), BF16),
            pltpu.SemaphoreType.DMA((8,)),
        ],
        compiler_params=pltpu.CompilerParams(vmem_limit_bytes=20 << 20),
        cost_estimate=pl.CostEstimate(flops=4 << 30, bytes_accessed=6 << 20, transcendentals=0),
        name="project_out",
    )(idx, routes, own, other, *pin(blocks))


def on_device(
    tokens,
    norm_gain,
    router,
    routes,
    kv_weight,
    query_weight,
    out_weight,
    prefix_cache,
    suffix_lengths,
    prefix_lengths,
):
    xl, y, c = (lax.axis_index(a) for a in WIDE)
    first_core = c == 0
    chips = chip_order()

    def table(values):
        return jnp.stack([jnp.asarray(v, jnp.int32) for v in values])

    def head_rows(w, h):
        rows = w.shape[0] // 2
        return lax.dynamic_slice_in_dim(w, h * rows, rows, 0)

    def weights_of(h):
        return jnp.concatenate([head_rows(query_weight, h), head_rows(kv_weight, h)], axis=0)

    w = jnp.stack([weights_of(c), across_core(weights_of(1 - c))])
    other_routes = across_core(routes)
    both_routes = jnp.where(
        first_core,
        jnp.concatenate([routes, other_routes]),
        jnp.concatenate([other_routes, routes]),
    )

    def cache_of(h):
        return lax.dynamic_slice_in_dim(prefix_cache, h * 2 * H, 2 * H, 1)

    cache = jnp.stack([cache_of(c), across_core(cache_of(1 - c))])
    pair = jnp.stack([tokens, across_far(tokens)])
    far, ym, yp, a = along_y(w, 2), along_y(w, 3), along_y(w, 1), across_x(w)
    caches = [cache, across_x(cache)]
    copies = jnp.broadcast_to(pair[None], (4,) + pair.shape)
    far, ym, yp, a, copies, caches = lax.optimization_barrier((far, ym, yp, a, copies, caches))
    blocks = lax.all_to_all(copies, "z", 0, 0, tiled=True)
    am, ap, afar = along_y(a, 3), along_y(a, 1), across_x(far)
    blocks, am, ap, afar = lax.optimization_barrier((blocks, am, ap, afar))
    gathered = [w, a, ym, am, far, afar, yp, ap]

    xh = lax.axis_index("xh")
    token_src = [k * 2 + (xh ^ s) for k in range(4) for s in range(2)]
    places = [lax.rem(lax.rem(v, 4) + 4 - y, 4) * 2 + (v // 4 ^ xl) for v in token_src]
    normed = normalise(table(token_src + places), norm_gain.reshape(8, 1, 256), blocks)
    out_early, am, ap = lax.optimization_barrier((out_weight, am, ap))
    gathered[3], gathered[7] = am, ap
    o_ym, o_yp, o_a = along_y(out_early, 3), along_y(out_early, 1), across_x(out_early)
    q, kv, gates = project(
        table(chips + [c]), both_routes, router.T, normed, across_core(normed), gathered
    )
    kvs = [kv, across_x(kv)]
    qs = [q] + [along_y(q, k) for k in (1, 2, 3)]
    qs[0], o_ym, o_yp = lax.optimization_barrier((q, o_ym, o_yp))
    out_late, o_a_late, kvs[1] = lax.optimization_barrier((out_weight, o_a, kvs[1]))
    o_far, o_am, o_ap = along_y(out_late, 2), along_y(o_a_late, 3), along_y(o_a_late, 1)

    firsts = [(xl * 4 + lax.rem(y + 4 - k, 4)) * 512 for k in range(4)]
    mine, partner = xl * 4 + y, (1 - xl) * 4 + y
    at = [c, mine * 1536, partner * 1536, mine * 512, partner * 512]
    lengths = (suffix_lengths, prefix_lengths)
    parts = list(attend(table(at + firsts[:1]), *lengths, qs[:1], caches, kvs))
    parts += list(attend(table(at + firsts[1:]), *lengths, qs[1:], caches, kvs))
    parts[1:], o_far, o_am, o_ap = lax.optimization_barrier((parts[1:], o_far, o_am, o_ap))
    for k in range(1, 4):
        parts[k] = along_y(parts[k], 4 - k)
    out_blocks = [out_weight, o_a, o_ym, o_am, o_far, across_x(o_far), o_yp, o_ap]
    gate_row = gates.reshape(2, 256, 2).transpose(0, 2, 1).reshape(1, 1024)
    attended = combine(gate_row, parts)

    sums = project_out(
        table(chips + [c]), both_routes, attended, across_core(attended), out_blocks
    )
    sums = lax.all_to_all(sums, NARROW, 0, 0, tiled=True)
    total = jnp.sum(sums.astype(F32), axis=0)
    here = lax.dynamic_slice_in_dim(total, c * 256, 256, 0).astype(BF16)
    there = lax.dynamic_slice_in_dim(total, (1 - c) * 256, 256, 0).astype(BF16)
    there = across_core(there)
    return jnp.where(
        first_core,
        jnp.concatenate([here, there], axis=1),
        jnp.concatenate([there, here], axis=1),
    )


def solution(mesh):
    fine = Mesh(mesh.devices.reshape(SIZES), AXES)
    placed = (
        P(WIDE, NARROW),
        P(),
        P(),
        P(WIDE, None),
        P(NARROW, WIDE),
        P(NARROW, WIDE),
        P(NARROW, WIDE),
        P(WIDE, NARROW),
        P(),
        P(),
    )
    return jax.shard_map(
        on_device, mesh=fine, in_specs=placed, out_specs=P(WIDE, NARROW), check_vma=False
    )
```

```python
import functools
import math

import jax
import jax.numpy as jnp
from jax import lax
from jax.experimental import pallas as pl
from jax.experimental.pallas import tpu as pltpu
from jax.sharding import Mesh
from jax.sharding import PartitionSpec as P

H = 128
E = 8
EPS = 1e-06
FLOOR = -1e30
AXES = ("xl", "y", "c", "z", "xh")
SIZES = (2, 4, 2, 4, 2)
WIDE = ("xl", "y", "c")
NARROW = ("z", "xh")
BF16 = jnp.bfloat16
F32 = jnp.float32
SCALE2 = H ** (-0.5) * math.log2(math.e)
CK = 512
R = 512
CHUNKS = 8
UNROLL = 4

SMEM = pl.BlockSpec(memory_space=pltpu.SMEM)
VMEM = pl.BlockSpec(memory_space=pltpu.VMEM)
HBM = pl.BlockSpec(memory_space=pltpu.HBM)
ANY = pl.BlockSpec(memory_space=pl.ANY)


def along_y(x, k):
    return lax.ppermute(x, "y", [(i, (i + k) % 4) for i in range(4)])


def across_x(x):
    return lax.ppermute(x, "xl", [(0, 1), (1, 0)])


def across_far(x):
    return lax.ppermute(x, "xh", [(0, 1), (1, 0)])


def across_core(x):
    return lax.ppermute(x, "c", [(0, 1), (1, 0)])


def tie(a, b):
    return lax.optimization_barrier((a, b))


def chip_order():
    xl, y = lax.axis_index("xl"), lax.axis_index("y")
    return [(xl ^ dx) * 4 + lax.rem(y + dy, 4) for dy in range(4) for dx in range(2)]


def pin(arrays):
    return [pltpu.with_memory_space_constraint(a, pltpu.HBM) for a in arrays]


def nt_dot(a, b):
    return lax.dot_general(a, b, (((1,), (1,)), ((), ())), preferred_element_type=F32)


def run(copies):
    for c in copies:
        c.start()
    for c in copies:
        c.wait()


def norm_kernel(idx, gain, b0, b1, normed, held, sem):
    run([pltpu.make_async_copy(r, held.at[i], sem.at[i]) for i, r in enumerate((b0, b1))])
    total = jnp.zeros((256, 1), F32)
    for k in range(8):
        v = held[k // 4, k % 4].astype(F32)
        total = total + jnp.sum(v * v, axis=1, keepdims=True)
    scale = lax.rsqrt(total * (1.0 / 2048) + EPS)
    for k in range(8):
        v = held[k // 4, k % 4].astype(F32) * scale * gain[idx[k]].astype(F32)
        normed[:, pl.ds(pl.multiple_of(idx[8 + k] * 256, 256), 256)] = v.astype(BF16)


def normalise(idx, gain, blocks):
    return pl.pallas_call(
        norm_kernel,
        out_shape=jax.ShapeDtypeStruct((256, 2048), BF16),
        in_specs=[SMEM, VMEM, ANY, ANY],
        out_specs=VMEM,
        scratch_shapes=[pltpu.VMEM((2, 4, 256, 256), BF16), pltpu.SemaphoreType.DMA((2,))],
        compiler_params=pltpu.CompilerParams(vmem_limit_bytes=8 << 20),
        cost_estimate=pl.CostEstimate(flops=1 << 24, bytes_accessed=2 << 20, transcendentals=0),
        name="normalise",
    )(idx, gain, *blocks)


GROUPS = ((0, 512), (512, 768))


def project_kernel(idx, routes, router, own, other, *refs):
    blocks = refs[:8]
    q_out, kv_out, gates, xs, held, sel, sem = refs[8:]
    core = idx[8]
    copies = []
    for i, r in enumerate((own, other)):
        at = pl.multiple_of((core if i == 0 else 1 - core) * 256, 256)
        copies.append(pltpu.make_async_copy(r, xs.at[pl.ds(at, 256)], sem.at[32 + i]))
    for g, (start, rows) in enumerate(GROUPS):
        for k in range(16):
            lane = (k // 2) * 256 + H * (core if k % 2 == 0 else 1 - core)
            at = pl.ds(pl.multiple_of(lane, H), H)
            copies.append(
                pltpu.make_async_copy(
                    blocks[k // 2].at[k % 2, pl.ds(start, rows)],
                    held.at[pl.ds(start, rows), at],
                    sem.at[16 * g + k],
                )
            )
    for c in copies:
        c.start()
    for c in copies[:2]:
        c.wait()
    logits = jnp.zeros((512, E), F32)
    for i in range(8):
        part = router[:, pl.ds(pl.multiple_of(idx[i] * 256, 256), 256)]
        logits += nt_dot(xs[:, i * 256 : (i + 1) * 256], part)
    lane = lax.broadcasted_iota(jnp.int32, (512, E), 1)
    chosen = [
        jnp.sum(jnp.where(routes[:, j : j + 1] == lane, logits, 0.0), axis=1, keepdims=True)
        for j in range(2)
    ]
    top = jnp.maximum(chosen[0], chosen[1])
    e0, e1 = jnp.exp(chosen[0] - top), jnp.exp(chosen[1] - top)
    gates[:, 0:1] = e0 / (e0 + e1)
    gates[:, 1:2] = e1 / (e0 + e1)

    wanted = [jnp.broadcast_to(routes[:, j : j + 1], (512, H)) for j in range(2)]
    for r in range(5):
        if r == 0:
            for c in copies[2:18]:
                c.wait()
        if r == 2:
            for c in copies[18:]:
                c.wait()
        acc = nt_dot(xs[...], held[r * 256 : (r + 1) * 256])
        if r == 4:
            kv_out[...] = acc.astype(BF16)
            continue
        for j in range(2):
            value = jnp.zeros((512, H), F32) if r == 0 else sel[j]
            for e in range(2):
                value = jnp.where(wanted[j] == 2 * r + e, acc[:, e * H : (e + 1) * H], value)
            if r < 3:
                sel[j] = value
            else:
                for half in range(2):
                    at = (half * 2 + j) * 256
                    q_out[at : at + 256] = value[half * 256 : (half + 1) * 256].astype(BF16)


def project(idx, routes, router, own, other, blocks):
    return pl.pallas_call(
        project_kernel,
        out_shape=(
            jax.ShapeDtypeStruct((1024, H), BF16),
            jax.ShapeDtypeStruct((512, 2 * H), BF16),
            jax.ShapeDtypeStruct((512, 2), F32),
        ),
        in_specs=[SMEM, VMEM, VMEM] + [HBM] * 10,
        out_specs=(VMEM, VMEM, VMEM),
        scratch_shapes=[
            pltpu.VMEM((512, 2048), BF16),
            pltpu.VMEM((1280, 2048), BF16),
            pltpu.VMEM((2, 512, H), F32),
            pltpu.SemaphoreType.DMA((34,)),
        ],
        compiler_params=pltpu.CompilerParams(vmem_limit_bytes=20 << 20),
        cost_estimate=pl.CostEstimate(flops=6 << 30, bytes_accessed=8 << 20, transcendentals=0),
        name="project",
    )(idx, routes, router, *pin([own, other, *blocks]))


def attend_kernel(count, idx, ends_s, ends_p, *refs):
    queries, (cache0, cache1, kv0, kv1) = refs[:count], refs[count : count + 4]
    outs = refs[count + 4 : 2 * count + 4]
    q, keep, limits, top, tot, acc, sa, sb, chunk_of, tile_of, sem = refs[2 * count + 4 :]
    tiles = 2 * count
    core = idx[0]
    copies = [
        pltpu.make_async_copy(r, q.at[pl.ds(1024 * b, 1024)], sem.at[b])
        for b, r in enumerate(queries)
    ]
    for i, r in enumerate((cache0, cache1)):
        for side in range(2):
            at = pl.multiple_of(i * 1536 + 768 * (core if side == 0 else 1 - core), 256)
            copies.append(
                pltpu.make_async_copy(r.at[side], keep.at[pl.ds(at, 768)], sem.at[count + 2 * i + side])
            )
    for i, r in enumerate((kv0, kv1)):
        copies.append(
            pltpu.make_async_copy(r, keep.at[pl.ds(3072 + 512 * i, 512)], sem.at[count + 4 + i])
        )
    for c in copies:
        c.start()

    se, pe = [ends_s[0]], [ends_p[0]]
    for k in range(1, 4):
        se.append(se[-1] + ends_s[k])
        pe.append(pe[-1] + ends_p[k])

    def allowed_of(token):
        lo, hi, own = 0 * token, 0 * token + pe[0], 0 * token
        for k in range(3):
            later = token >= se[k]
            lo = jnp.where(later, pe[k], lo)
            hi = jnp.where(later, pe[k + 1], hi)
            own = jnp.where(later, se[k], own)
        return lo, hi, own

    for t in range(tiles):
        first = idx[5 + t // 2] + (t % 2) * 256
        token = first + lax.rem(lax.broadcasted_iota(jnp.int32, (1, R), 1), 256)
        lo, hi, own = allowed_of(token)
        limits[t, 0:1] = lo
        limits[t, 1:2] = hi
        limits[t, 2:3] = own
        limits[t, 3:4] = token + 1
    limits[tiles] = jnp.zeros((4, R), jnp.int32)
    top[...] = jnp.full(top.shape, FLOOR, F32)
    tot[...] = jnp.zeros(tot.shape, F32)
    acc[...] = jnp.zeros(acc.shape, F32)

    def base_of(i):
        slot = jnp.where(i < 3, idx[1] + i * CK, idx[2] + (i - 3) * CK)
        return jnp.where(i < 6, slot, jnp.where(i == 6, idx[3], idx[4]))

    def collect(want_full, start):
        def visit(n, count):
            i, t = n // tiles, lax.rem(n, tiles)
            base = base_of(i)
            first = idx[5 + t // 2] + lax.rem(t, 2) * 256
            last = first + 255
            lo_a, hi_a, own_a = allowed_of(first)
            lo_b, hi_b, own_b = allowed_of(last)
            pre = i < 6
            lo_first, lo_last = jnp.where(pre, lo_a, own_a), jnp.where(pre, lo_b, own_b)
            hi_first, hi_last = jnp.where(pre, hi_a, first + 1), jnp.where(pre, hi_b, last + 1)
            some = (base + CK > lo_first) & (base < hi_last)
            full = (base >= lo_last) & (base + CK <= hi_first)
            hit = full if want_full else (some & jnp.logical_not(full))

            @pl.when(hit)
            def _():
                chunk_of[count] = i
                tile_of[count] = t

            return count + hit.astype(jnp.int32)

        count = lax.fori_loop(0, CHUNKS * tiles, visit, start)
        rounds = (count + UNROLL - 1) // UNROLL
        for k in range(UNROLL):
            chunk_of[count + k] = 0
            tile_of[count + k] = tiles
        return rounds

    full_rounds = collect(True, 0)
    all_rounds = collect(False, full_rounds * UNROLL)
    for c in copies:
        c.wait()
    q[tiles * R : (tiles + 1) * R] = jnp.zeros((R, H), BF16)

    def scores(n, out):
        keys = keep[pl.ds(pl.multiple_of(chunk_of[n] * CK, CK), CK), :H]
        out[...] = nt_dot(keys, q[pl.ds(pl.multiple_of(tile_of[n] * R, R), R), :])

    def consume(n, s_ref, masked):
        i, t = chunk_of[n], tile_of[n]
        s = s_ref[...]
        if masked:
            pos = base_of(i) + lax.broadcasted_iota(jnp.int32, (CK, R), 0)
            kind = jnp.where(i < 6, 0, 2)
            lo, hi = limits[t, pl.ds(kind, 1)], limits[t, pl.ds(kind + 1, 1)]
            s = jnp.where((pos >= lo) & (pos < hi), s, -jnp.inf)
        old = top[t]
        new = jnp.maximum(old, jnp.max(s, axis=0, keepdims=True))
        p = jnp.exp2(s * SCALE2 - new * SCALE2)
        factor = jnp.exp2((old - new) * SCALE2)
        top[t] = new
        tot[t] = tot[t] * factor + jnp.sum(p, axis=0, keepdims=True)
        values = keep[pl.ds(pl.multiple_of(i * CK, CK), CK), H:]
        acc[t] = acc[t] * factor + lax.dot_general(
            values, p.astype(BF16), (((0,), (0,)), ((), ())), preferred_element_type=F32
        )

    def rounds(masked):
        def body(n, _):
            for k in range(UNROLL):
                cur, nxt = (sa, sb) if k % 2 == 0 else (sb, sa)
                scores(n * UNROLL + k + 1, nxt)
                consume(n * UNROLL + k, cur, masked)
            return 0

        return body

    chunk_of[all_rounds * UNROLL] = 0
    tile_of[all_rounds * UNROLL] = tiles
    scores(0, sa)
    lax.fori_loop(0, full_rounds, rounds(False), 0)
    lax.fori_loop(full_rounds, all_rounds, rounds(True), 0)

    for t in range(tiles):
        total = tot[t]
        safe = jnp.where(total > 0.0, total, 1.0)
        cols = slice((t % 2) * R, (t % 2 + 1) * R)
        out = outs[t // 2]
        out[0:H, cols] = (acc[t] / safe).astype(BF16)
        lse = jnp.where(total > 0.0, top[t] * SCALE2 + jnp.log2(safe), FLOOR)
        high = lse.astype(BF16).astype(F32)
        mid = (lse - high).astype(BF16).astype(F32)
        low = lse - high - mid
        row = lax.broadcasted_iota(jnp.int32, (16, R), 0)
        packed = jnp.where(row == 0, high, jnp.where(row == 1, mid, jnp.where(row == 2, low, 0.0)))
        out[H : H + 16, cols] = packed.astype(BF16)


def attend(idx, suffix_lengths, prefix_lengths, qs, caches, kvs):
    count, tiles = len(qs), 2 * len(qs)
    return pl.pallas_call(
        functools.partial(attend_kernel, count),
        out_shape=tuple(jax.ShapeDtypeStruct((H + 16, 1024), BF16) for _ in range(count)),
        in_specs=[SMEM] * 3 + [HBM] * (count + 4),
        out_specs=tuple([VMEM] * count),
        scratch_shapes=[
            pltpu.VMEM(((tiles + 1) * R, H), BF16),
            pltpu.VMEM((CHUNKS * CK, 2 * H), BF16),
            pltpu.VMEM((tiles + 1, 4, R), jnp.int32),
            pltpu.VMEM((tiles + 1, 1, R), F32),
            pltpu.VMEM((tiles + 1, 1, R), F32),
            pltpu.VMEM((tiles + 1, H, R), F32),
            pltpu.VMEM((CK, R), F32),
            pltpu.VMEM((CK, R), F32),
            pltpu.SMEM((CHUNKS * tiles + 4 * UNROLL,), jnp.int32),
            pltpu.SMEM((CHUNKS * tiles + 4 * UNROLL,), jnp.int32),
            pltpu.SemaphoreType.DMA((count + 6,)),
        ],
        compiler_params=pltpu.CompilerParams(vmem_limit_bytes=20 << 20),
        cost_estimate=pl.CostEstimate(
            flops=count * (3 << 30), bytes_accessed=4 << 20, transcendentals=count << 21
        ),
        name="attend",
    )(idx, suffix_lengths, prefix_lengths, *pin([*qs, *caches, *kvs]))


def combine_kernel(gates, p0, p1, p2, p3, out):
    parts = (p0, p1, p2, p3)
    lses = []
    for p in parts:
        rows = p[H : H + 16].astype(F32)
        lses.append(rows[0:1] + rows[1:2] + rows[2:3])
    high = jnp.maximum(jnp.maximum(lses[0], lses[1]), jnp.maximum(lses[2], lses[3]))
    share = [jnp.exp2(v - high) for v in lses]
    norm = gates[...] / (share[0] + share[1] + share[2] + share[3])
    for at in range(0, 1024, 256):
        cols = slice(at, at + 256)
        total = jnp.zeros((H, 256), F32)
        for p, s in zip(parts, share):
            total += p[0:H, cols].astype(F32) * s[:, cols]
        out[cols] = jnp.transpose(total * norm[:, cols]).astype(BF16)


def combine(gates, parts):
    return pl.pallas_call(
        combine_kernel,
        out_shape=jax.ShapeDtypeStruct((1024, H), BF16),
        in_specs=[VMEM] * 5,
        out_specs=VMEM,
        compiler_params=pltpu.CompilerParams(vmem_limit_bytes=8 << 20),
        cost_estimate=pl.CostEstimate(flops=1 << 22, bytes_accessed=2 << 20, transcendentals=0),
        name="combine",
    )(gates, *parts)


def out_kernel(idx, routes, own, other, *refs):
    blocks = refs[:10]
    out, held, padded, sem = refs[10:]
    core = idx[8]
    copies = []
    for k, slot in enumerate((0, 1, 2, 3, 6, 7)):
        copies.append(pltpu.make_async_copy(blocks[k], held.at[idx[slot]], sem.at[k]))
    for k in range(6, 10):
        target = held.at[idx[4 + (k - 6) // 2], pl.ds((k % 2) * 1024, 1024)]
        copies.append(pltpu.make_async_copy(blocks[k], target, sem.at[k]))
    for c in copies:
        c.start()
    for half in range(2):
        rows = slice(half * 256, (half + 1) * 256)
        wanted = [jnp.broadcast_to(routes[rows, j : j + 1], (256, H)) for j in range(2)]
        for side, source in enumerate((own, other)):
            head = core if side == 0 else 1 - core
            first = source[half * 512 : half * 512 + 256].astype(F32)
            second = source[half * 512 + 256 : half * 512 + 512].astype(F32)
            for e in range(E):
                value = jnp.where(wanted[1] == e, second, 0.0)
                value = jnp.where(wanted[0] == e, first, value).astype(BF16)
                padded[rows, pl.ds(pl.multiple_of((head * E + e) * H, H), H)] = value
    for c in copies:
        c.wait()
    for k in range(0, 8, 2):
        w = jnp.concatenate([held[k], held[k + 1]], axis=1)
        value = jnp.dot(padded[...], w, preferred_element_type=F32)
        for s in range(2):
            out[k + s] = value[:, s * H : (s + 1) * H].astype(BF16)


def project_out(idx, routes, own, other, blocks):
    return pl.pallas_call(
        out_kernel,
        out_shape=jax.ShapeDtypeStruct((8, 512, H), BF16),
        in_specs=[SMEM, VMEM, VMEM, VMEM] + [HBM] * 10,
        out_specs=VMEM,
        scratch_shapes=[
            pltpu.VMEM((8, 2048, H), BF16),
            pltpu.VMEM((512, 2048), BF16),
            pltpu.SemaphoreType.DMA((10,)),
        ],
        compiler_params=pltpu.CompilerParams(vmem_limit_bytes=20 << 20),
        cost_estimate=pl.CostEstimate(flops=4 << 30, bytes_accessed=6 << 20, transcendentals=0),
        name="project_out",
    )(idx, routes, own, other, *pin(blocks))


def on_device(
    tokens,
    norm_gain,
    router,
    routes,
    kv_weight,
    query_weight,
    out_weight,
    prefix_cache,
    suffix_lengths,
    prefix_lengths,
):
    xl, y, c = (lax.axis_index(a) for a in WIDE)
    first_core = c == 0
    chips = chip_order()

    def table(values):
        return jnp.stack([jnp.asarray(v, jnp.int32) for v in values])

    def head_rows(w, h):
        rows = w.shape[0] // 2
        return lax.dynamic_slice_in_dim(w, h * rows, rows, 0)

    def weights_of(h):
        return jnp.concatenate([head_rows(query_weight, h), head_rows(kv_weight, h)], axis=0)

    w = jnp.stack([weights_of(c), across_core(weights_of(1 - c))])
    other_routes = across_core(routes)
    both_routes = jnp.where(
        first_core,
        jnp.concatenate([routes, other_routes]),
        jnp.concatenate([other_routes, routes]),
    )

    def cache_of(h):
        return lax.dynamic_slice_in_dim(prefix_cache, h * 2 * H, 2 * H, 1)

    cache = jnp.stack([cache_of(c), across_core(cache_of(1 - c))])
    half_row = across_far(tokens)
    far, ym, yp, a = along_y(w, 2), along_y(w, 3), along_y(w, 1), across_x(w)
    caches = [cache, across_x(cache)]
    blocks = [lax.all_gather(v, "z", axis=0) for v in (tokens, half_row)]
    xh = lax.axis_index("xh")
    token_src = [k * 2 + (xh ^ s) for s in range(2) for k in range(4)]
    places = [lax.rem(lax.rem(v, 4) + 4 - y, 4) * 2 + (v // 4 ^ xl) for v in token_src]
    normed = normalise(table(token_src + places), norm_gain.reshape(8, 1, 256), blocks)
    far, ym, yp, a, normed, caches, both_routes = lax.optimization_barrier(
        (far, ym, yp, a, normed, caches, both_routes)
    )
    am, ap, afar = along_y(a, 3), along_y(a, 1), across_x(far)
    other_normed = across_core(normed)
    gathered = [w, a, ym, am, far, afar, yp, ap]

    out_early, am, ap = lax.optimization_barrier((out_weight, am, ap))
    gathered[3], gathered[7] = am, ap
    o_ym, o_yp, o_a = along_y(out_early, 3), along_y(out_early, 1), across_x(out_early)
    q, kv, gates = project(
        table(chips + [c]), both_routes, router.T, normed, other_normed, gathered
    )
    kvs = [kv, across_x(kv)]
    qs = [q] + [along_y(q, k) for k in (1, 2, 3)]
    qs[0], o_ym, o_yp = lax.optimization_barrier((q, o_ym, o_yp))
    o_a_late, up, down, kvs[1] = lax.optimization_barrier((o_a, o_yp[:1024], o_ym[1024:], kvs[1]))
    far0, far1 = along_y(up, 1), along_y(down, 3)
    o_am, o_ap = along_y(o_a_late, 3), along_y(o_a_late, 1)

    firsts = [(xl * 4 + lax.rem(y + 4 - k, 4)) * 512 for k in range(4)]
    mine, partner = xl * 4 + y, (1 - xl) * 4 + y
    at = [c, mine * 1536, partner * 1536, mine * 512, partner * 512]
    lengths = (suffix_lengths, prefix_lengths)
    parts = list(attend(table(at + firsts[:1]), *lengths, qs[:1], caches, kvs))
    parts += list(attend(table(at + firsts[1:]), *lengths, qs[1:], caches, kvs))
    parts[1:], far0, far1, o_am, o_ap = lax.optimization_barrier(
        (parts[1:], far0, far1, o_am, o_ap)
    )
    for k in range(1, 4):
        parts[k] = along_y(parts[k], 4 - k)
    out_blocks = [out_weight, o_a, o_ym, o_am, o_yp, o_ap]
    out_blocks += [far0, far1, across_x(far0), across_x(far1)]
    gate_row = gates.reshape(2, 256, 2).transpose(0, 2, 1).reshape(1, 1024)
    attended = combine(gate_row, parts)

    sums = project_out(
        table(chips + [c]), both_routes, attended, across_core(attended), out_blocks
    )
    sums = lax.all_to_all(sums, NARROW, 0, 0, tiled=True)
    total = jnp.sum(sums.astype(F32), axis=0)
    here = lax.dynamic_slice_in_dim(total, c * 256, 256, 0).astype(BF16)
    there = lax.dynamic_slice_in_dim(total, (1 - c) * 256, 256, 0).astype(BF16)
    there = across_core(there)
    return jnp.where(
        first_core,
        jnp.concatenate([here, there], axis=1),
        jnp.concatenate([there, here], axis=1),
    )


def solution(mesh):
    fine = Mesh(mesh.devices.reshape(SIZES), AXES)
    placed = (
        P(WIDE, NARROW),
        P(),
        P(),
        P(WIDE, None),
        P(NARROW, WIDE),
        P(NARROW, WIDE),
        P(NARROW, WIDE),
        P(WIDE, NARROW),
        P(),
        P(),
    )
    return jax.shard_map(
        on_device, mesh=fine, in_specs=placed, out_specs=P(WIDE, NARROW), check_vma=False
    )
```

```python
import functools
import math

import jax
import jax.numpy as jnp
from jax import lax
from jax.experimental import pallas as pl
from jax.experimental.pallas import tpu as pltpu
from jax.sharding import Mesh
from jax.sharding import PartitionSpec as P

H = 128
E = 8
EPS = 1e-06
FLOOR = -1e30
AXES = ("xl", "y", "c", "z", "xh")
SIZES = (2, 4, 2, 4, 2)
WIDE = ("xl", "y", "c")
NARROW = ("z", "xh")
BF16 = jnp.bfloat16
F32 = jnp.float32
SCALE2 = H ** (-0.5) * math.log2(math.e)
CK = 512
R = 512
CHUNKS = 8
UNROLL = 4

SMEM = pl.BlockSpec(memory_space=pltpu.SMEM)
VMEM = pl.BlockSpec(memory_space=pltpu.VMEM)
HBM = pl.BlockSpec(memory_space=pltpu.HBM)
ANY = pl.BlockSpec(memory_space=pl.ANY)


def along_y(x, k):
    return lax.ppermute(x, "y", [(i, (i + k) % 4) for i in range(4)])


def across_x(x):
    return lax.ppermute(x, "xl", [(0, 1), (1, 0)])


def across_far(x):
    return lax.ppermute(x, "xh", [(0, 1), (1, 0)])


def across_core(x):
    return lax.ppermute(x, "c", [(0, 1), (1, 0)])


def tie(a, b):
    return lax.optimization_barrier((a, b))


def chip_order():
    xl, y = lax.axis_index("xl"), lax.axis_index("y")
    return [(xl ^ dx) * 4 + lax.rem(y + dy, 4) for dy in range(4) for dx in range(2)]


def pin(arrays):
    return [pltpu.with_memory_space_constraint(a, pltpu.HBM) for a in arrays]


def nt_dot(a, b):
    return lax.dot_general(a, b, (((1,), (1,)), ((), ())), preferred_element_type=F32)


def run(copies):
    for c in copies:
        c.start()
    for c in copies:
        c.wait()


def norm_kernel(idx, gain, b0, b1, normed, held, sem):
    run([pltpu.make_async_copy(r, held.at[i], sem.at[i]) for i, r in enumerate((b0, b1))])
    total = jnp.zeros((256, 1), F32)
    for k in range(8):
        v = held[k // 4, k % 4].astype(F32)
        total = total + jnp.sum(v * v, axis=1, keepdims=True)
    scale = lax.rsqrt(total * (1.0 / 2048) + EPS)
    for k in range(8):
        v = held[k // 4, k % 4].astype(F32) * scale * gain[idx[k]].astype(F32)
        normed[:, pl.ds(pl.multiple_of(idx[8 + k] * 256, 256), 256)] = v.astype(BF16)


def normalise(idx, gain, blocks):
    return pl.pallas_call(
        norm_kernel,
        out_shape=jax.ShapeDtypeStruct((256, 2048), BF16),
        in_specs=[SMEM, VMEM, ANY, ANY],
        out_specs=VMEM,
        scratch_shapes=[pltpu.VMEM((2, 4, 256, 256), BF16), pltpu.SemaphoreType.DMA((2,))],
        compiler_params=pltpu.CompilerParams(vmem_limit_bytes=8 << 20),
        cost_estimate=pl.CostEstimate(flops=1 << 24, bytes_accessed=2 << 20, transcendentals=0),
        name="normalise",
    )(idx, gain, *blocks)


GROUPS = ((0, 512), (512, 768))


def project_kernel(idx, routes, router, own, other, *refs):
    blocks = refs[:8]
    q_out, kv_out, gates, xs, held, sel, sem = refs[8:]
    core = idx[8]
    copies = []
    for i, r in enumerate((own, other)):
        at = pl.multiple_of((core if i == 0 else 1 - core) * 256, 256)
        copies.append(pltpu.make_async_copy(r, xs.at[pl.ds(at, 256)], sem.at[32 + i]))
    for g, (start, rows) in enumerate(GROUPS):
        for k in range(16):
            lane = (k // 2) * 256 + H * (core if k % 2 == 0 else 1 - core)
            at = pl.ds(pl.multiple_of(lane, H), H)
            copies.append(
                pltpu.make_async_copy(
                    blocks[k // 2].at[k % 2, pl.ds(start, rows)],
                    held.at[pl.ds(start, rows), at],
                    sem.at[16 * g + k],
                )
            )
    for c in copies:
        c.start()
    for c in copies[:2]:
        c.wait()
    logits = jnp.zeros((512, E), F32)
    for i in range(8):
        part = router[:, pl.ds(pl.multiple_of(idx[i] * 256, 256), 256)]
        logits += nt_dot(xs[:, i * 256 : (i + 1) * 256], part)
    lane = lax.broadcasted_iota(jnp.int32, (512, E), 1)
    chosen = [
        jnp.sum(jnp.where(routes[:, j : j + 1] == lane, logits, 0.0), axis=1, keepdims=True)
        for j in range(2)
    ]
    top = jnp.maximum(chosen[0], chosen[1])
    e0, e1 = jnp.exp(chosen[0] - top), jnp.exp(chosen[1] - top)
    gates[:, 0:1] = e0 / (e0 + e1)
    gates[:, 1:2] = e1 / (e0 + e1)

    wanted = [jnp.broadcast_to(routes[:, j : j + 1], (512, H)) for j in range(2)]
    for r in range(5):
        if r == 0:
            for c in copies[2:18]:
                c.wait()
        if r == 2:
            for c in copies[18:]:
                c.wait()
        acc = nt_dot(xs[...], held[r * 256 : (r + 1) * 256])
        if r == 4:
            kv_out[...] = acc.astype(BF16)
            continue
        for j in range(2):
            value = jnp.zeros((512, H), F32) if r == 0 else sel[j]
            for e in range(2):
                value = jnp.where(wanted[j] == 2 * r + e, acc[:, e * H : (e + 1) * H], value)
            if r < 3:
                sel[j] = value
            else:
                for half in range(2):
                    at = (half * 2 + j) * 256
                    q_out[at : at + 256] = value[half * 256 : (half + 1) * 256].astype(BF16)


def project(idx, routes, router, own, other, blocks):
    return pl.pallas_call(
        project_kernel,
        out_shape=(
            jax.ShapeDtypeStruct((1024, H), BF16),
            jax.ShapeDtypeStruct((512, 2 * H), BF16),
            jax.ShapeDtypeStruct((512, 2), F32),
        ),
        in_specs=[SMEM, VMEM, VMEM] + [HBM] * 10,
        out_specs=(VMEM, VMEM, VMEM),
        scratch_shapes=[
            pltpu.VMEM((512, 2048), BF16),
            pltpu.VMEM((1280, 2048), BF16),
            pltpu.VMEM((2, 512, H), F32),
            pltpu.SemaphoreType.DMA((34,)),
        ],
        compiler_params=pltpu.CompilerParams(vmem_limit_bytes=20 << 20),
        cost_estimate=pl.CostEstimate(flops=6 << 30, bytes_accessed=8 << 20, transcendentals=0),
        name="project",
    )(idx, routes, router, *pin([own, other, *blocks]))


def attend_kernel(count, idx, ends_s, ends_p, *refs):
    queries, (cache0, cache1, kv0, kv1) = refs[:count], refs[count : count + 4]
    outs = refs[count + 4 : 2 * count + 4]
    q, keep, limits, top, tot, acc, sa, sb, chunk_of, tile_of, sem = refs[2 * count + 4 :]
    tiles = 2 * count
    core = idx[0]
    copies = [
        pltpu.make_async_copy(r, q.at[pl.ds(1024 * b, 1024)], sem.at[b])
        for b, r in enumerate(queries)
    ]
    for i, r in enumerate((cache0, cache1)):
        for side in range(2):
            at = pl.multiple_of(i * 1536 + 768 * (core if side == 0 else 1 - core), 256)
            copies.append(
                pltpu.make_async_copy(r.at[side], keep.at[pl.ds(at, 768)], sem.at[count + 2 * i + side])
            )
    for i, r in enumerate((kv0, kv1)):
        copies.append(
            pltpu.make_async_copy(r, keep.at[pl.ds(3072 + 512 * i, 512)], sem.at[count + 4 + i])
        )
    for c in copies:
        c.start()

    se, pe = [ends_s[0]], [ends_p[0]]
    for k in range(1, 4):
        se.append(se[-1] + ends_s[k])
        pe.append(pe[-1] + ends_p[k])

    def allowed_of(token):
        lo, hi, own = 0 * token, 0 * token + pe[0], 0 * token
        for k in range(3):
            later = token >= se[k]
            lo = jnp.where(later, pe[k], lo)
            hi = jnp.where(later, pe[k + 1], hi)
            own = jnp.where(later, se[k], own)
        return lo, hi, own

    for t in range(tiles):
        first = idx[5 + t // 2] + (t % 2) * 256
        token = first + lax.rem(lax.broadcasted_iota(jnp.int32, (1, R), 1), 256)
        lo, hi, own = allowed_of(token)
        limits[t, 0:1] = lo
        limits[t, 1:2] = hi
        limits[t, 2:3] = own
        limits[t, 3:4] = token + 1
    limits[tiles] = jnp.zeros((4, R), jnp.int32)
    top[...] = jnp.full(top.shape, FLOOR, F32)
    tot[...] = jnp.zeros(tot.shape, F32)
    acc[...] = jnp.zeros(acc.shape, F32)

    def base_of(i):
        slot = jnp.where(i < 3, idx[1] + i * CK, idx[2] + (i - 3) * CK)
        return jnp.where(i < 6, slot, jnp.where(i == 6, idx[3], idx[4]))

    def collect(want_full, start):
        def visit(n, count):
            i, t = n // tiles, lax.rem(n, tiles)
            base = base_of(i)
            first = idx[5 + t // 2] + lax.rem(t, 2) * 256
            last = first + 255
            lo_a, hi_a, own_a = allowed_of(first)
            lo_b, hi_b, own_b = allowed_of(last)
            pre = i < 6
            lo_first, lo_last = jnp.where(pre, lo_a, own_a), jnp.where(pre, lo_b, own_b)
            hi_first, hi_last = jnp.where(pre, hi_a, first + 1), jnp.where(pre, hi_b, last + 1)
            some = (base + CK > lo_first) & (base < hi_last)
            full = (base >= lo_last) & (base + CK <= hi_first)
            hit = full if want_full else (some & jnp.logical_not(full))

            @pl.when(hit)
            def _():
                chunk_of[count] = i
                tile_of[count] = t

            return count + hit.astype(jnp.int32)

        count = lax.fori_loop(0, CHUNKS * tiles, visit, start)
        rounds = (count + UNROLL - 1) // UNROLL
        for k in range(UNROLL):
            chunk_of[count + k] = 0
            tile_of[count + k] = tiles
        return rounds

    full_rounds = collect(True, 0)
    all_rounds = collect(False, full_rounds * UNROLL)
    for c in copies:
        c.wait()
    q[tiles * R : (tiles + 1) * R] = jnp.zeros((R, H), BF16)

    def scores(n, out):
        keys = keep[pl.ds(pl.multiple_of(chunk_of[n] * CK, CK), CK), :H]
        out[...] = nt_dot(keys, q[pl.ds(pl.multiple_of(tile_of[n] * R, R), R), :])

    def consume(n, s_ref, masked):
        i, t = chunk_of[n], tile_of[n]
        s = s_ref[...]
        if masked:
            pos = base_of(i) + lax.broadcasted_iota(jnp.int32, (CK, R), 0)
            kind = jnp.where(i < 6, 0, 2)
            lo, hi = limits[t, pl.ds(kind, 1)], limits[t, pl.ds(kind + 1, 1)]
            s = jnp.where((pos >= lo) & (pos < hi), s, -jnp.inf)
        old = top[t]
        new = jnp.maximum(old, jnp.max(s, axis=0, keepdims=True))
        p = jnp.exp2(s * SCALE2 - new * SCALE2)
        factor = jnp.exp2((old - new) * SCALE2)
        top[t] = new
        tot[t] = tot[t] * factor + jnp.sum(p, axis=0, keepdims=True)
        values = keep[pl.ds(pl.multiple_of(i * CK, CK), CK), H:]
        acc[t] = acc[t] * factor + lax.dot_general(
            values, p.astype(BF16), (((0,), (0,)), ((), ())), preferred_element_type=F32
        )

    def rounds(masked):
        def body(n, _):
            for k in range(UNROLL):
                cur, nxt = (sa, sb) if k % 2 == 0 else (sb, sa)
                scores(n * UNROLL + k + 1, nxt)
                consume(n * UNROLL + k, cur, masked)
            return 0

        return body

    chunk_of[all_rounds * UNROLL] = 0
    tile_of[all_rounds * UNROLL] = tiles
    scores(0, sa)
    lax.fori_loop(0, full_rounds, rounds(False), 0)
    lax.fori_loop(full_rounds, all_rounds, rounds(True), 0)

    for t in range(tiles):
        total = tot[t]
        safe = jnp.where(total > 0.0, total, 1.0)
        cols = slice((t % 2) * R, (t % 2 + 1) * R)
        out = outs[t // 2]
        out[0:H, cols] = (acc[t] / safe).astype(BF16)
        lse = jnp.where(total > 0.0, top[t] * SCALE2 + jnp.log2(safe), FLOOR)
        high = lse.astype(BF16).astype(F32)
        mid = (lse - high).astype(BF16).astype(F32)
        low = lse - high - mid
        row = lax.broadcasted_iota(jnp.int32, (16, R), 0)
        packed = jnp.where(row == 0, high, jnp.where(row == 1, mid, jnp.where(row == 2, low, 0.0)))
        out[H : H + 16, cols] = packed.astype(BF16)


def attend(idx, suffix_lengths, prefix_lengths, qs, caches, kvs):
    count, tiles = len(qs), 2 * len(qs)
    return pl.pallas_call(
        functools.partial(attend_kernel, count),
        out_shape=tuple(jax.ShapeDtypeStruct((H + 16, 1024), BF16) for _ in range(count)),
        in_specs=[SMEM] * 3 + [HBM] * (count + 4),
        out_specs=tuple([VMEM] * count),
        scratch_shapes=[
            pltpu.VMEM(((tiles + 1) * R, H), BF16),
            pltpu.VMEM((CHUNKS * CK, 2 * H), BF16),
            pltpu.VMEM((tiles + 1, 4, R), jnp.int32),
            pltpu.VMEM((tiles + 1, 1, R), F32),
            pltpu.VMEM((tiles + 1, 1, R), F32),
            pltpu.VMEM((tiles + 1, H, R), F32),
            pltpu.VMEM((CK, R), F32),
            pltpu.VMEM((CK, R), F32),
            pltpu.SMEM((CHUNKS * tiles + 4 * UNROLL,), jnp.int32),
            pltpu.SMEM((CHUNKS * tiles + 4 * UNROLL,), jnp.int32),
            pltpu.SemaphoreType.DMA((count + 6,)),
        ],
        compiler_params=pltpu.CompilerParams(vmem_limit_bytes=20 << 20),
        cost_estimate=pl.CostEstimate(
            flops=count * (3 << 30), bytes_accessed=4 << 20, transcendentals=count << 21
        ),
        name="attend",
    )(idx, suffix_lengths, prefix_lengths, *pin([*qs, *caches, *kvs]))


def combine_kernel(gates, p0, p1, p2, p3, out):
    parts = (p0, p1, p2, p3)
    lses = []
    for p in parts:
        rows = p[H : H + 16].astype(F32)
        lses.append(rows[0:1] + rows[1:2] + rows[2:3])
    high = jnp.maximum(jnp.maximum(lses[0], lses[1]), jnp.maximum(lses[2], lses[3]))
    share = [jnp.exp2(v - high) for v in lses]
    norm = gates[...] / (share[0] + share[1] + share[2] + share[3])
    for at in range(0, 1024, 256):
        cols = slice(at, at + 256)
        total = jnp.zeros((H, 256), F32)
        for p, s in zip(parts, share):
            total += p[0:H, cols].astype(F32) * s[:, cols]
        out[cols] = jnp.transpose(total * norm[:, cols]).astype(BF16)


def combine(gates, parts):
    return pl.pallas_call(
        combine_kernel,
        out_shape=jax.ShapeDtypeStruct((1024, H), BF16),
        in_specs=[VMEM] * 5,
        out_specs=VMEM,
        compiler_params=pltpu.CompilerParams(vmem_limit_bytes=8 << 20),
        cost_estimate=pl.CostEstimate(flops=1 << 22, bytes_accessed=2 << 20, transcendentals=0),
        name="combine",
    )(gates, *parts)


def out_kernel(idx, routes, own, other, *refs):
    blocks = refs[:10]
    out, held, padded, sem = refs[10:]
    core = idx[8]
    copies = []
    for k, slot in enumerate((0, 1, 2, 3, 6, 7)):
        copies.append(pltpu.make_async_copy(blocks[k], held.at[idx[slot]], sem.at[k]))
    for k in range(6, 10):
        target = held.at[idx[4 + (k - 6) // 2], pl.ds((k % 2) * 1024, 1024)]
        copies.append(pltpu.make_async_copy(blocks[k], target, sem.at[k]))
    for c in copies:
        c.start()
    for half in range(2):
        rows = slice(half * 256, (half + 1) * 256)
        wanted = [jnp.broadcast_to(routes[rows, j : j + 1], (256, H)) for j in range(2)]
        for side, source in enumerate((own, other)):
            head = core if side == 0 else 1 - core
            first = source[half * 512 : half * 512 + 256].astype(F32)
            second = source[half * 512 + 256 : half * 512 + 512].astype(F32)
            for e in range(E):
                value = jnp.where(wanted[1] == e, second, 0.0)
                value = jnp.where(wanted[0] == e, first, value).astype(BF16)
                padded[rows, pl.ds(pl.multiple_of((head * E + e) * H, H), H)] = value
    for c in copies:
        c.wait()
    for k in range(0, 8, 2):
        w = jnp.concatenate([held[k], held[k + 1]], axis=1)
        value = jnp.dot(padded[...], w, preferred_element_type=F32)
        for s in range(2):
            out[k + s] = value[:, s * H : (s + 1) * H].astype(BF16)


def project_out(idx, routes, own, other, blocks):
    return pl.pallas_call(
        out_kernel,
        out_shape=jax.ShapeDtypeStruct((8, 512, H), BF16),
        in_specs=[SMEM, VMEM, VMEM, VMEM] + [HBM] * 10,
        out_specs=VMEM,
        scratch_shapes=[
            pltpu.VMEM((8, 2048, H), BF16),
            pltpu.VMEM((512, 2048), BF16),
            pltpu.SemaphoreType.DMA((10,)),
        ],
        compiler_params=pltpu.CompilerParams(vmem_limit_bytes=20 << 20),
        cost_estimate=pl.CostEstimate(flops=4 << 30, bytes_accessed=6 << 20, transcendentals=0),
        name="project_out",
    )(idx, routes, own, other, *pin(blocks))


def on_device(
    tokens,
    norm_gain,
    router,
    routes,
    kv_weight,
    query_weight,
    out_weight,
    prefix_cache,
    suffix_lengths,
    prefix_lengths,
):
    xl, y, c = (lax.axis_index(a) for a in WIDE)
    first_core = c == 0
    chips = chip_order()

    def table(values):
        return jnp.stack([jnp.asarray(v, jnp.int32) for v in values])

    def head_rows(w, h):
        rows = w.shape[0] // 2
        return lax.dynamic_slice_in_dim(w, h * rows, rows, 0)

    def weights_of(h):
        return jnp.concatenate([head_rows(query_weight, h), head_rows(kv_weight, h)], axis=0)

    w = jnp.stack([weights_of(c), across_core(weights_of(1 - c))])
    other_routes = across_core(routes)
    both_routes = jnp.where(
        first_core,
        jnp.concatenate([routes, other_routes]),
        jnp.concatenate([other_routes, routes]),
    )

    def cache_of(h):
        return lax.dynamic_slice_in_dim(prefix_cache, h * 2 * H, 2 * H, 1)

    cache = jnp.stack([cache_of(c), across_core(cache_of(1 - c))])
    half_row = across_far(tokens)
    far, ym, yp, a = along_y(w, 2), along_y(w, 3), along_y(w, 1), across_x(w)
    caches = [cache, across_x(cache)]
    blocks = [lax.all_gather(v, "z", axis=0) for v in (tokens, half_row)]
    xh = lax.axis_index("xh")
    token_src = [k * 2 + (xh ^ s) for s in range(2) for k in range(4)]
    places = [lax.rem(lax.rem(v, 4) + 4 - y, 4) * 2 + (v // 4 ^ xl) for v in token_src]
    normed = normalise(table(token_src + places), norm_gain.reshape(8, 1, 256), blocks)
    far, ym, yp, a, normed, caches, both_routes = lax.optimization_barrier(
        (far, ym, yp, a, normed, caches, both_routes)
    )
    am, ap, afar = along_y(a, 3), along_y(a, 1), across_x(far)
    other_normed = across_core(normed)
    gathered = [w, a, ym, am, far, afar, yp, ap]

    out_early, am, ap = lax.optimization_barrier((out_weight, am, ap))
    gathered[3], gathered[7] = am, ap
    o_ym, o_yp, o_a = along_y(out_early, 3), along_y(out_early, 1), across_x(out_early)
    q, kv, gates = project(
        table(chips + [c]), both_routes, router.T, normed, other_normed, gathered
    )
    kvs = [kv, across_x(kv)]
    qs = [q] + [along_y(q, k) for k in (1, 2, 3)]
    qs[0], o_ym, o_yp = lax.optimization_barrier((q, o_ym, o_yp))
    o_a, up, down, kvs[1] = lax.optimization_barrier((o_a, o_yp[:1024], o_ym[1024:], kvs[1]))
    far0, far1 = along_y(up, 1), along_y(down, 3)
    o_am, o_ap = across_x(o_ym), across_x(o_yp)

    firsts = [(xl * 4 + lax.rem(y + 4 - k, 4)) * 512 for k in range(4)]
    mine, partner = xl * 4 + y, (1 - xl) * 4 + y
    at = [c, mine * 1536, partner * 1536, mine * 512, partner * 512]
    lengths = (suffix_lengths, prefix_lengths)
    parts = list(attend(table(at + firsts[:1]), *lengths, qs[:1], caches, kvs))
    parts += list(attend(table(at + firsts[1:]), *lengths, qs[1:], caches, kvs))
    parts[1:], far0, far1, o_am, o_ap = lax.optimization_barrier(
        (parts[1:], far0, far1, o_am, o_ap)
    )
    for k in range(1, 4):
        parts[k] = along_y(parts[k], 4 - k)
    afar0, afar1 = across_x(far0), across_x(far1)
    parts, afar0, afar1 = lax.optimization_barrier((parts, afar0, afar1))
    out_blocks = [out_weight, o_a, o_ym, o_am, o_yp, o_ap, far0, far1, afar0, afar1]
    gate_row = gates.reshape(2, 256, 2).transpose(0, 2, 1).reshape(1, 1024)
    attended = combine(gate_row, parts)

    sums = project_out(
        table(chips + [c]), both_routes, attended, across_core(attended), out_blocks
    )
    sums = lax.all_to_all(sums, NARROW, 0, 0, tiled=True)
    total = jnp.sum(sums.astype(F32), axis=0)
    here = lax.dynamic_slice_in_dim(total, c * 256, 256, 0).astype(BF16)
    there = lax.dynamic_slice_in_dim(total, (1 - c) * 256, 256, 0).astype(BF16)
    there = across_core(there)
    return jnp.where(
        first_core,
        jnp.concatenate([here, there], axis=1),
        jnp.concatenate([there, here], axis=1),
    )


def solution(mesh):
    fine = Mesh(mesh.devices.reshape(SIZES), AXES)
    placed = (
        P(WIDE, NARROW),
        P(),
        P(),
        P(WIDE, None),
        P(NARROW, WIDE),
        P(NARROW, WIDE),
        P(NARROW, WIDE),
        P(WIDE, NARROW),
        P(),
        P(),
    )
    return jax.shard_map(
        on_device, mesh=fine, in_specs=placed, out_specs=P(WIDE, NARROW), check_vma=False
    )
```

```python
import functools
import math

import jax
import jax.numpy as jnp
from jax import lax
from jax.experimental import pallas as pl
from jax.experimental.pallas import tpu as pltpu
from jax.sharding import Mesh
from jax.sharding import PartitionSpec as P

H = 128
E = 8
EPS = 1e-06
FLOOR = -1e30
AXES = ("xl", "y", "c", "z", "xh")
SIZES = (2, 4, 2, 4, 2)
WIDE = ("xl", "y", "c")
NARROW = ("z", "xh")
BF16 = jnp.bfloat16
F32 = jnp.float32
SCALE2 = H ** (-0.5) * math.log2(math.e)
CK = 512
R = 512
CHUNKS = 8
UNROLL = 4

SMEM = pl.BlockSpec(memory_space=pltpu.SMEM)
VMEM = pl.BlockSpec(memory_space=pltpu.VMEM)
HBM = pl.BlockSpec(memory_space=pltpu.HBM)
ANY = pl.BlockSpec(memory_space=pl.ANY)


def along_y(x, k):
    return lax.ppermute(x, "y", [(i, (i + k) % 4) for i in range(4)])


def across_x(x):
    return lax.ppermute(x, "xl", [(0, 1), (1, 0)])


def across_far(x):
    return lax.ppermute(x, "xh", [(0, 1), (1, 0)])


def across_core(x):
    return lax.ppermute(x, "c", [(0, 1), (1, 0)])


def tie(a, b):
    return lax.optimization_barrier((a, b))


def chip_order():
    xl, y = lax.axis_index("xl"), lax.axis_index("y")
    return [(xl ^ dx) * 4 + lax.rem(y + dy, 4) for dy in range(4) for dx in range(2)]


def pin(arrays):
    return [pltpu.with_memory_space_constraint(a, pltpu.HBM) for a in arrays]


def nt_dot(a, b):
    return lax.dot_general(a, b, (((1,), (1,)), ((), ())), preferred_element_type=F32)


def run(copies):
    for c in copies:
        c.start()
    for c in copies:
        c.wait()


def norm_kernel(idx, gain, b0, b1, normed, held, sem):
    run([pltpu.make_async_copy(r, held.at[i], sem.at[i]) for i, r in enumerate((b0, b1))])
    total = jnp.zeros((256, 1), F32)
    for k in range(8):
        v = held[k // 4, k % 4].astype(F32)
        total = total + jnp.sum(v * v, axis=1, keepdims=True)
    scale = lax.rsqrt(total * (1.0 / 2048) + EPS)
    for k in range(8):
        v = held[k // 4, k % 4].astype(F32) * scale * gain[idx[k]].astype(F32)
        normed[:, pl.ds(pl.multiple_of(idx[8 + k] * 256, 256), 256)] = v.astype(BF16)


def normalise(idx, gain, blocks):
    return pl.pallas_call(
        norm_kernel,
        out_shape=jax.ShapeDtypeStruct((256, 2048), BF16),
        in_specs=[SMEM, VMEM, ANY, ANY],
        out_specs=VMEM,
        scratch_shapes=[pltpu.VMEM((2, 4, 256, 256), BF16), pltpu.SemaphoreType.DMA((2,))],
        compiler_params=pltpu.CompilerParams(vmem_limit_bytes=8 << 20),
        cost_estimate=pl.CostEstimate(flops=1 << 24, bytes_accessed=2 << 20, transcendentals=0),
        name="normalise",
    )(idx, gain, *blocks)


GROUPS = ((0, 512), (512, 768))


def project_kernel(idx, routes, router, own, other, *refs):
    blocks = refs[:8]
    q_out, kv_out, gates, xs, held, sel, sem = refs[8:]
    core = idx[8]
    copies = []
    for i, r in enumerate((own, other)):
        at = pl.multiple_of((core if i == 0 else 1 - core) * 256, 256)
        copies.append(pltpu.make_async_copy(r, xs.at[pl.ds(at, 256)], sem.at[32 + i]))
    for g, (start, rows) in enumerate(GROUPS):
        for k in range(16):
            lane = (k // 2) * 256 + H * (core if k % 2 == 0 else 1 - core)
            at = pl.ds(pl.multiple_of(lane, H), H)
            copies.append(
                pltpu.make_async_copy(
                    blocks[k // 2].at[k % 2, pl.ds(start, rows)],
                    held.at[pl.ds(start, rows), at],
                    sem.at[16 * g + k],
                )
            )
    for c in copies:
        c.start()
    for c in copies[:2]:
        c.wait()
    logits = jnp.zeros((512, E), F32)
    for i in range(8):
        part = router[:, pl.ds(pl.multiple_of(idx[i] * 256, 256), 256)]
        logits += nt_dot(xs[:, i * 256 : (i + 1) * 256], part)
    lane = lax.broadcasted_iota(jnp.int32, (512, E), 1)
    chosen = [
        jnp.sum(jnp.where(routes[:, j : j + 1] == lane, logits, 0.0), axis=1, keepdims=True)
        for j in range(2)
    ]
    top = jnp.maximum(chosen[0], chosen[1])
    e0, e1 = jnp.exp(chosen[0] - top), jnp.exp(chosen[1] - top)
    gates[:, 0:1] = e0 / (e0 + e1)
    gates[:, 1:2] = e1 / (e0 + e1)

    wanted = [jnp.broadcast_to(routes[:, j : j + 1], (512, H)) for j in range(2)]
    for r in range(5):
        if r == 0:
            for c in copies[2:18]:
                c.wait()
        if r == 2:
            for c in copies[18:]:
                c.wait()
        acc = nt_dot(xs[...], held[r * 256 : (r + 1) * 256])
        if r == 4:
            kv_out[...] = acc.astype(BF16)
            continue
        for j in range(2):
            value = jnp.zeros((512, H), F32) if r == 0 else sel[j]
            for e in range(2):
                value = jnp.where(wanted[j] == 2 * r + e, acc[:, e * H : (e + 1) * H], value)
            if r < 3:
                sel[j] = value
            else:
                for half in range(2):
                    at = (half * 2 + j) * 256
                    q_out[at : at + 256] = value[half * 256 : (half + 1) * 256].astype(BF16)


def project(idx, routes, router, own, other, blocks):
    return pl.pallas_call(
        project_kernel,
        out_shape=(
            jax.ShapeDtypeStruct((1024, H), BF16),
            jax.ShapeDtypeStruct((512, 2 * H), BF16),
            jax.ShapeDtypeStruct((512, 2), F32),
        ),
        in_specs=[SMEM, VMEM, VMEM] + [HBM] * 10,
        out_specs=(VMEM, VMEM, VMEM),
        scratch_shapes=[
            pltpu.VMEM((512, 2048), BF16),
            pltpu.VMEM((1280, 2048), BF16),
            pltpu.VMEM((2, 512, H), F32),
            pltpu.SemaphoreType.DMA((34,)),
        ],
        compiler_params=pltpu.CompilerParams(vmem_limit_bytes=20 << 20),
        cost_estimate=pl.CostEstimate(flops=6 << 30, bytes_accessed=8 << 20, transcendentals=0),
        name="project",
    )(idx, routes, router, *pin([own, other, *blocks]))


def attend_kernel(count, half, idx, ends_s, ends_p, *refs):
    queries, (cache0, cache1, kv0, kv1) = refs[:count], refs[count : count + 4]
    outs = refs[count + 4 : 2 * count + 4]
    q, keep, limits, top, tot, acc, sa, sb, chunk_of, tile_of, sem = refs[2 * count + 4 :]
    tiles = count
    core = idx[0]
    copies = [
        pltpu.make_async_copy(r.at[pl.ds(half * R, R)], q.at[pl.ds(R * b, R)], sem.at[b])
        for b, r in enumerate(queries)
    ]
    for i, r in enumerate((cache0, cache1)):
        for side in range(2):
            at = pl.multiple_of(i * 1536 + 768 * (core if side == 0 else 1 - core), 256)
            copies.append(
                pltpu.make_async_copy(r.at[side], keep.at[pl.ds(at, 768)], sem.at[count + 2 * i + side])
            )
    for i, r in enumerate((kv0, kv1)):
        copies.append(
            pltpu.make_async_copy(r, keep.at[pl.ds(3072 + 512 * i, 512)], sem.at[count + 4 + i])
        )
    for c in copies:
        c.start()

    se, pe = [ends_s[0]], [ends_p[0]]
    for k in range(1, 4):
        se.append(se[-1] + ends_s[k])
        pe.append(pe[-1] + ends_p[k])

    def allowed_of(token):
        lo, hi, own = 0 * token, 0 * token + pe[0], 0 * token
        for k in range(3):
            later = token >= se[k]
            lo = jnp.where(later, pe[k], lo)
            hi = jnp.where(later, pe[k + 1], hi)
            own = jnp.where(later, se[k], own)
        return lo, hi, own

    for t in range(tiles):
        first = idx[5 + t] + half * 256
        token = first + lax.rem(lax.broadcasted_iota(jnp.int32, (1, R), 1), 256)
        lo, hi, own = allowed_of(token)
        limits[t, 0:1] = lo
        limits[t, 1:2] = hi
        limits[t, 2:3] = own
        limits[t, 3:4] = token + 1
    limits[tiles] = jnp.zeros((4, R), jnp.int32)
    top[...] = jnp.full(top.shape, FLOOR, F32)
    tot[...] = jnp.zeros(tot.shape, F32)
    acc[...] = jnp.zeros(acc.shape, F32)

    def base_of(i):
        slot = jnp.where(i < 3, idx[1] + i * CK, idx[2] + (i - 3) * CK)
        return jnp.where(i < 6, slot, jnp.where(i == 6, idx[3], idx[4]))

    def collect(want_full, start):
        def visit(n, count):
            i, t = n // tiles, lax.rem(n, tiles)
            base = base_of(i)
            first = idx[5 + t] + half * 256
            last = first + 255
            lo_a, hi_a, own_a = allowed_of(first)
            lo_b, hi_b, own_b = allowed_of(last)
            pre = i < 6
            lo_first, lo_last = jnp.where(pre, lo_a, own_a), jnp.where(pre, lo_b, own_b)
            hi_first, hi_last = jnp.where(pre, hi_a, first + 1), jnp.where(pre, hi_b, last + 1)
            some = (base + CK > lo_first) & (base < hi_last)
            full = (base >= lo_last) & (base + CK <= hi_first)
            hit = full if want_full else (some & jnp.logical_not(full))

            @pl.when(hit)
            def _():
                chunk_of[count] = i
                tile_of[count] = t

            return count + hit.astype(jnp.int32)

        count = lax.fori_loop(0, CHUNKS * tiles, visit, start)
        rounds = (count + UNROLL - 1) // UNROLL
        for k in range(UNROLL):
            chunk_of[count + k] = 0
            tile_of[count + k] = tiles
        return rounds

    full_rounds = collect(True, 0)
    all_rounds = collect(False, full_rounds * UNROLL)
    for c in copies:
        c.wait()
    q[tiles * R : (tiles + 1) * R] = jnp.zeros((R, H), BF16)

    def scores(n, out):
        keys = keep[pl.ds(pl.multiple_of(chunk_of[n] * CK, CK), CK), :H]
        out[...] = nt_dot(keys, q[pl.ds(pl.multiple_of(tile_of[n] * R, R), R), :])

    def consume(n, s_ref, masked):
        i, t = chunk_of[n], tile_of[n]
        s = s_ref[...]
        if masked:
            pos = base_of(i) + lax.broadcasted_iota(jnp.int32, (CK, R), 0)
            kind = jnp.where(i < 6, 0, 2)
            lo, hi = limits[t, pl.ds(kind, 1)], limits[t, pl.ds(kind + 1, 1)]
            s = jnp.where((pos >= lo) & (pos < hi), s, -jnp.inf)
        old = top[t]
        new = jnp.maximum(old, jnp.max(s, axis=0, keepdims=True))
        p = jnp.exp2(s * SCALE2 - new * SCALE2)
        factor = jnp.exp2((old - new) * SCALE2)
        top[t] = new
        tot[t] = tot[t] * factor + jnp.sum(p, axis=0, keepdims=True)
        values = keep[pl.ds(pl.multiple_of(i * CK, CK), CK), H:]
        acc[t] = acc[t] * factor + lax.dot_general(
            values, p.astype(BF16), (((0,), (0,)), ((), ())), preferred_element_type=F32
        )

    def rounds(masked):
        def body(n, _):
            for k in range(UNROLL):
                cur, nxt = (sa, sb) if k % 2 == 0 else (sb, sa)
                scores(n * UNROLL + k + 1, nxt)
                consume(n * UNROLL + k, cur, masked)
            return 0

        return body

    chunk_of[all_rounds * UNROLL] = 0
    tile_of[all_rounds * UNROLL] = tiles
    scores(0, sa)
    lax.fori_loop(0, full_rounds, rounds(False), 0)
    lax.fori_loop(full_rounds, all_rounds, rounds(True), 0)

    for t in range(tiles):
        total = tot[t]
        safe = jnp.where(total > 0.0, total, 1.0)
        out = outs[t]
        out[0:H] = (acc[t] / safe).astype(BF16)
        lse = jnp.where(total > 0.0, top[t] * SCALE2 + jnp.log2(safe), FLOOR)
        high = lse.astype(BF16).astype(F32)
        mid = (lse - high).astype(BF16).astype(F32)
        low = lse - high - mid
        row = lax.broadcasted_iota(jnp.int32, (16, R), 0)
        packed = jnp.where(row == 0, high, jnp.where(row == 1, mid, jnp.where(row == 2, low, 0.0)))
        out[H : H + 16] = packed.astype(BF16)


def attend(half, idx, suffix_lengths, prefix_lengths, qs, caches, kvs):
    count = tiles = len(qs)
    return pl.pallas_call(
        functools.partial(attend_kernel, count, half),
        out_shape=tuple(jax.ShapeDtypeStruct((H + 16, R), BF16) for _ in range(count)),
        in_specs=[SMEM] * 3 + [HBM] * (count + 4),
        out_specs=tuple([VMEM] * count),
        scratch_shapes=[
            pltpu.VMEM(((tiles + 1) * R, H), BF16),
            pltpu.VMEM((CHUNKS * CK, 2 * H), BF16),
            pltpu.VMEM((tiles + 1, 4, R), jnp.int32),
            pltpu.VMEM((tiles + 1, 1, R), F32),
            pltpu.VMEM((tiles + 1, 1, R), F32),
            pltpu.VMEM((tiles + 1, H, R), F32),
            pltpu.VMEM((CK, R), F32),
            pltpu.VMEM((CK, R), F32),
            pltpu.SMEM((CHUNKS * tiles + 4 * UNROLL,), jnp.int32),
            pltpu.SMEM((CHUNKS * tiles + 4 * UNROLL,), jnp.int32),
            pltpu.SemaphoreType.DMA((count + 6,)),
        ],
        compiler_params=pltpu.CompilerParams(vmem_limit_bytes=20 << 20),
        cost_estimate=pl.CostEstimate(
            flops=count * (3 << 29), bytes_accessed=4 << 20, transcendentals=count << 20
        ),
        name="attend",
    )(idx, suffix_lengths, prefix_lengths, *pin([*qs, *caches, *kvs]))


def combine_kernel(gates, p0, p1, p2, p3, out):
    parts = (p0, p1, p2, p3)
    lses = []
    for p in parts:
        rows = p[H : H + 16].astype(F32)
        lses.append(rows[0:1] + rows[1:2] + rows[2:3])
    high = jnp.maximum(jnp.maximum(lses[0], lses[1]), jnp.maximum(lses[2], lses[3]))
    share = [jnp.exp2(v - high) for v in lses]
    norm = gates[...] / (share[0] + share[1] + share[2] + share[3])
    for at in range(0, R, 256):
        cols = slice(at, at + 256)
        total = jnp.zeros((H, 256), F32)
        for p, s in zip(parts, share):
            total += p[0:H, cols].astype(F32) * s[:, cols]
        out[cols] = jnp.transpose(total * norm[:, cols]).astype(BF16)


def combine(gates, parts):
    return pl.pallas_call(
        combine_kernel,
        out_shape=jax.ShapeDtypeStruct((R, H), BF16),
        in_specs=[VMEM] * 5,
        out_specs=VMEM,
        compiler_params=pltpu.CompilerParams(vmem_limit_bytes=8 << 20),
        cost_estimate=pl.CostEstimate(flops=1 << 22, bytes_accessed=2 << 20, transcendentals=0),
        name="combine",
    )(gates, *parts)


def out_kernel(idx, routes, own, other, *refs):
    blocks = refs[:10]
    out, held, padded, sem = refs[10:]
    core = idx[8]
    copies = []
    for k, slot in enumerate((0, 1, 2, 3, 6, 7)):
        copies.append(pltpu.make_async_copy(blocks[k], held.at[idx[slot]], sem.at[k]))
    for k in range(6, 10):
        target = held.at[idx[4 + (k - 6) // 2], pl.ds((k % 2) * 1024, 1024)]
        copies.append(pltpu.make_async_copy(blocks[k], target, sem.at[k]))
    for c in copies:
        c.start()
    wanted = [jnp.broadcast_to(routes[:, j : j + 1], (256, H)) for j in range(2)]
    for side, source in enumerate((own, other)):
        head = core if side == 0 else 1 - core
        first, second = source[0:256].astype(F32), source[256:512].astype(F32)
        for e in range(E):
            value = jnp.where(wanted[1] == e, second, 0.0)
            value = jnp.where(wanted[0] == e, first, value).astype(BF16)
            padded[:, pl.ds(pl.multiple_of((head * E + e) * H, H), H)] = value
    for c in copies:
        c.wait()
    for k in range(0, 8, 2):
        w = jnp.concatenate([held[k], held[k + 1]], axis=1)
        value = jnp.dot(padded[...], w, preferred_element_type=F32)
        for s in range(2):
            out[k + s] = value[:, s * H : (s + 1) * H].astype(BF16)


def project_out(idx, routes, own, other, blocks):
    return pl.pallas_call(
        out_kernel,
        out_shape=jax.ShapeDtypeStruct((8, 256, H), BF16),
        in_specs=[SMEM, VMEM, VMEM, VMEM] + [HBM] * 10,
        out_specs=VMEM,
        scratch_shapes=[
            pltpu.VMEM((8, 2048, H), BF16),
            pltpu.VMEM((256, 2048), BF16),
            pltpu.SemaphoreType.DMA((10,)),
        ],
        compiler_params=pltpu.CompilerParams(vmem_limit_bytes=20 << 20),
        cost_estimate=pl.CostEstimate(flops=2 << 30, bytes_accessed=6 << 20, transcendentals=0),
        name="project_out",
    )(idx, routes, own, other, *pin(blocks))


def on_device(
    tokens,
    norm_gain,
    router,
    routes,
    kv_weight,
    query_weight,
    out_weight,
    prefix_cache,
    suffix_lengths,
    prefix_lengths,
):
    xl, y, c = (lax.axis_index(a) for a in WIDE)
    first_core = c == 0
    chips = chip_order()

    def table(values):
        return jnp.stack([jnp.asarray(v, jnp.int32) for v in values])

    def head_rows(w, h):
        rows = w.shape[0] // 2
        return lax.dynamic_slice_in_dim(w, h * rows, rows, 0)

    def weights_of(h):
        return jnp.concatenate([head_rows(query_weight, h), head_rows(kv_weight, h)], axis=0)

    w = jnp.stack([weights_of(c), across_core(weights_of(1 - c))])
    other_routes = across_core(routes)
    both_routes = jnp.where(
        first_core,
        jnp.concatenate([routes, other_routes]),
        jnp.concatenate([other_routes, routes]),
    )

    def cache_of(h):
        return lax.dynamic_slice_in_dim(prefix_cache, h * 2 * H, 2 * H, 1)

    cache = jnp.stack([cache_of(c), across_core(cache_of(1 - c))])
    half_row = across_far(tokens)
    far, ym, yp, a = along_y(w, 2), along_y(w, 3), along_y(w, 1), across_x(w)
    caches = [cache, across_x(cache)]
    blocks = [lax.all_gather(v, "z", axis=0) for v in (tokens, half_row)]
    xh = lax.axis_index("xh")
    token_src = [k * 2 + (xh ^ s) for s in range(2) for k in range(4)]
    places = [lax.rem(lax.rem(v, 4) + 4 - y, 4) * 2 + (v // 4 ^ xl) for v in token_src]
    normed = normalise(table(token_src + places), norm_gain.reshape(8, 1, 256), blocks)
    far, ym, yp, a, normed, caches, both_routes = lax.optimization_barrier(
        (far, ym, yp, a, normed, caches, both_routes)
    )
    am, ap, afar = along_y(a, 3), along_y(a, 1), across_x(far)
    other_normed = across_core(normed)
    gathered = [w, a, ym, am, far, afar, yp, ap]

    out_early, am, ap = lax.optimization_barrier((out_weight, am, ap))
    gathered[3], gathered[7] = am, ap
    o_ym, o_yp, o_a = along_y(out_early, 3), along_y(out_early, 1), across_x(out_early)
    q, kv, gates = project(
        table(chips + [c]), both_routes, router.T, normed, other_normed, gathered
    )
    kvs = [kv, across_x(kv)]
    qs = [q] + [along_y(q, k) for k in (1, 2, 3)]
    o_a, up, down, kvs[1] = lax.optimization_barrier((o_a, o_yp[:1024], o_ym[1024:], kvs[1]))
    far0, far1 = along_y(up, 1), along_y(down, 3)
    o_am, o_ap = across_x(o_ym), across_x(o_yp)

    firsts = [(xl * 4 + lax.rem(y + 4 - k, 4)) * 512 for k in range(4)]
    mine, partner = xl * 4 + y, (1 - xl) * 4 + y
    at = [c, mine * 1536, partner * 1536, mine * 512, partner * 512]
    lengths = (suffix_lengths, prefix_lengths)
    at = table(at + firsts)
    gate_rows = gates.reshape(2, 256, 2).transpose(0, 2, 1).reshape(2, 1, R)
    parts = [list(attend(0, at, *lengths, qs, caches, kvs))]
    parts[0][1:], far0, far1 = lax.optimization_barrier((parts[0][1:], far0, far1))
    qs, o_am, o_ap = lax.optimization_barrier((qs, o_am, o_ap))
    parts.append(list(attend(1, at, *lengths, qs, caches, kvs)))
    for k in range(1, 4):
        parts[0][k] = along_y(parts[0][k], 4 - k)
    parts = lax.optimization_barrier(parts)
    for k in range(1, 4):
        parts[1][k] = along_y(parts[1][k], 4 - k)
    afar0, afar1 = across_x(far0), across_x(far1)
    parts[0], afar0, afar1 = lax.optimization_barrier((parts[0], afar0, afar1))
    out_blocks = [out_weight, o_a, o_ym, o_am, o_yp, o_ap, far0, far1, afar0, afar1]
    totals = []
    for half in range(2):
        attended = combine(gate_rows[half], parts[half])
        sums = project_out(
            table(chips + [c]),
            both_routes[half * 256 : (half + 1) * 256],
            attended,
            across_core(attended),
            out_blocks,
        )
        sums = lax.all_to_all(sums, NARROW, 0, 0, tiled=True)
        totals.append(jnp.sum(sums.astype(F32), axis=0).astype(BF16))
    here = jnp.where(first_core, totals[0], totals[1])
    there = across_core(jnp.where(first_core, totals[1], totals[0]))
    return jnp.where(
        first_core,
        jnp.concatenate([here, there], axis=1),
        jnp.concatenate([there, here], axis=1),
    )


def solution(mesh):
    fine = Mesh(mesh.devices.reshape(SIZES), AXES)
    placed = (
        P(WIDE, NARROW),
        P(),
        P(),
        P(WIDE, None),
        P(NARROW, WIDE),
        P(NARROW, WIDE),
        P(NARROW, WIDE),
        P(WIDE, NARROW),
        P(),
        P(),
    )
    return jax.shard_map(
        on_device, mesh=fine, in_specs=placed, out_specs=P(WIDE, NARROW), check_vma=False
    )
```

```python
import functools
import math

import jax
import jax.numpy as jnp
from jax import lax
from jax.experimental import pallas as pl
from jax.experimental.pallas import tpu as pltpu
from jax.sharding import Mesh
from jax.sharding import PartitionSpec as P

H = 128
E = 8
EPS = 1e-06
FLOOR = -1e30
AXES = ("xl", "y", "c", "z", "xh")
SIZES = (2, 4, 2, 4, 2)
WIDE = ("xl", "y", "c")
NARROW = ("z", "xh")
BF16 = jnp.bfloat16
F32 = jnp.float32
SCALE2 = H ** (-0.5) * math.log2(math.e)
CK = 512
R = 512
CHUNKS = 8
UNROLL = 4

SMEM = pl.BlockSpec(memory_space=pltpu.SMEM)
VMEM = pl.BlockSpec(memory_space=pltpu.VMEM)
HBM = pl.BlockSpec(memory_space=pltpu.HBM)
ANY = pl.BlockSpec(memory_space=pl.ANY)


def along_y(x, k):
    return lax.ppermute(x, "y", [(i, (i + k) % 4) for i in range(4)])


def across_x(x):
    return lax.ppermute(x, "xl", [(0, 1), (1, 0)])


def across_far(x):
    return lax.ppermute(x, "xh", [(0, 1), (1, 0)])


def across_core(x):
    return lax.ppermute(x, "c", [(0, 1), (1, 0)])


def tie(a, b):
    return lax.optimization_barrier((a, b))


def chip_order():
    xl, y = lax.axis_index("xl"), lax.axis_index("y")
    return [(xl ^ dx) * 4 + lax.rem(y + dy, 4) for dy in range(4) for dx in range(2)]


def pin(arrays):
    return [pltpu.with_memory_space_constraint(a, pltpu.HBM) for a in arrays]


def nt_dot(a, b):
    return lax.dot_general(a, b, (((1,), (1,)), ((), ())), preferred_element_type=F32)


def run(copies):
    for c in copies:
        c.start()
    for c in copies:
        c.wait()


def norm_kernel(idx, gain, b0, b1, normed, held, sem):
    run([pltpu.make_async_copy(r, held.at[i], sem.at[i]) for i, r in enumerate((b0, b1))])
    total = jnp.zeros((256, 1), F32)
    for k in range(8):
        v = held[k // 4, k % 4].astype(F32)
        total = total + jnp.sum(v * v, axis=1, keepdims=True)
    scale = lax.rsqrt(total * (1.0 / 2048) + EPS)
    for k in range(8):
        v = held[k // 4, k % 4].astype(F32) * scale * gain[idx[k]].astype(F32)
        normed[:, pl.ds(pl.multiple_of(idx[8 + k] * 256, 256), 256)] = v.astype(BF16)


def normalise(idx, gain, blocks):
    return pl.pallas_call(
        norm_kernel,
        out_shape=jax.ShapeDtypeStruct((256, 2048), BF16),
        in_specs=[SMEM, VMEM, ANY, ANY],
        out_specs=VMEM,
        scratch_shapes=[pltpu.VMEM((2, 4, 256, 256), BF16), pltpu.SemaphoreType.DMA((2,))],
        compiler_params=pltpu.CompilerParams(vmem_limit_bytes=8 << 20),
        cost_estimate=pl.CostEstimate(flops=1 << 24, bytes_accessed=2 << 20, transcendentals=0),
        name="normalise",
    )(idx, gain, *blocks)


GROUPS = ((0, 512), (512, 768))


def project_kernel(idx, routes, router, own, other, *refs):
    blocks = refs[:8]
    q_out, kv_out, gates, xs, held, sel, sem = refs[8:]
    core = idx[8]
    copies = []
    for i, r in enumerate((own, other)):
        at = pl.multiple_of((core if i == 0 else 1 - core) * 256, 256)
        copies.append(pltpu.make_async_copy(r, xs.at[pl.ds(at, 256)], sem.at[32 + i]))
    for g, (start, rows) in enumerate(GROUPS):
        for k in range(16):
            lane = (k // 2) * 256 + H * (core if k % 2 == 0 else 1 - core)
            at = pl.ds(pl.multiple_of(lane, H), H)
            copies.append(
                pltpu.make_async_copy(
                    blocks[k // 2].at[k % 2, pl.ds(start, rows)],
                    held.at[pl.ds(start, rows), at],
                    sem.at[16 * g + k],
                )
            )
    for c in copies:
        c.start()
    for c in copies[:2]:
        c.wait()
    logits = jnp.zeros((512, E), F32)
    for i in range(8):
        part = router[:, pl.ds(pl.multiple_of(idx[i] * 256, 256), 256)]
        logits += nt_dot(xs[:, i * 256 : (i + 1) * 256], part)
    lane = lax.broadcasted_iota(jnp.int32, (512, E), 1)
    chosen = [
        jnp.sum(jnp.where(routes[:, j : j + 1] == lane, logits, 0.0), axis=1, keepdims=True)
        for j in range(2)
    ]
    top = jnp.maximum(chosen[0], chosen[1])
    e0, e1 = jnp.exp(chosen[0] - top), jnp.exp(chosen[1] - top)
    gates[:, 0:1] = e0 / (e0 + e1)
    gates[:, 1:2] = e1 / (e0 + e1)

    wanted = [jnp.broadcast_to(routes[:, j : j + 1], (512, H)) for j in range(2)]
    for r in range(5):
        if r == 0:
            for c in copies[2:18]:
                c.wait()
        if r == 2:
            for c in copies[18:]:
                c.wait()
        acc = nt_dot(xs[...], held[r * 256 : (r + 1) * 256])
        if r == 4:
            kv_out[...] = acc.astype(BF16)
            continue
        for j in range(2):
            value = jnp.zeros((512, H), F32) if r == 0 else sel[j]
            for e in range(2):
                value = jnp.where(wanted[j] == 2 * r + e, acc[:, e * H : (e + 1) * H], value)
            if r < 3:
                sel[j] = value
            else:
                for half in range(2):
                    at = (half * 2 + j) * 256
                    q_out[at : at + 256] = value[half * 256 : (half + 1) * 256].astype(BF16)


def project(idx, routes, router, own, other, blocks):
    return pl.pallas_call(
        project_kernel,
        out_shape=(
            jax.ShapeDtypeStruct((1024, H), BF16),
            jax.ShapeDtypeStruct((512, 2 * H), BF16),
            jax.ShapeDtypeStruct((512, 2), F32),
        ),
        in_specs=[SMEM, VMEM, VMEM] + [HBM] * 10,
        out_specs=(VMEM, VMEM, VMEM),
        scratch_shapes=[
            pltpu.VMEM((512, 2048), BF16),
            pltpu.VMEM((1280, 2048), BF16),
            pltpu.VMEM((2, 512, H), F32),
            pltpu.SemaphoreType.DMA((34,)),
        ],
        compiler_params=pltpu.CompilerParams(vmem_limit_bytes=20 << 20),
        cost_estimate=pl.CostEstimate(flops=6 << 30, bytes_accessed=8 << 20, transcendentals=0),
        name="project",
    )(idx, routes, router, *pin([own, other, *blocks]))


def attend_kernel(count, idx, ends_s, ends_p, *refs):
    queries, (cache0, cache1, kv0, kv1) = refs[:count], refs[count : count + 4]
    outs = refs[count + 4 : 2 * count + 4]
    q, keep, limits, top, tot, acc, sa, sb, chunk_of, tile_of, sem = refs[2 * count + 4 :]
    tiles = 2 * count
    core = idx[0]
    copies = [
        pltpu.make_async_copy(r, q.at[pl.ds(1024 * b, 1024)], sem.at[b])
        for b, r in enumerate(queries)
    ]
    for i, r in enumerate((cache0, cache1)):
        for side in range(2):
            at = pl.multiple_of(i * 1536 + 768 * (core if side == 0 else 1 - core), 256)
            copies.append(
                pltpu.make_async_copy(r.at[side], keep.at[pl.ds(at, 768)], sem.at[count + 2 * i + side])
            )
    for i, r in enumerate((kv0, kv1)):
        copies.append(
            pltpu.make_async_copy(r, keep.at[pl.ds(3072 + 512 * i, 512)], sem.at[count + 4 + i])
        )
    for c in copies:
        c.start()

    se, pe = [ends_s[0]], [ends_p[0]]
    for k in range(1, 4):
        se.append(se[-1] + ends_s[k])
        pe.append(pe[-1] + ends_p[k])

    def allowed_of(token):
        lo, hi, own = 0 * token, 0 * token + pe[0], 0 * token
        for k in range(3):
            later = token >= se[k]
            lo = jnp.where(later, pe[k], lo)
            hi = jnp.where(later, pe[k + 1], hi)
            own = jnp.where(later, se[k], own)
        return lo, hi, own

    for t in range(tiles):
        first = idx[5 + t // 2] + (t % 2) * 256
        token = first + lax.rem(lax.broadcasted_iota(jnp.int32, (1, R), 1), 256)
        lo, hi, own = allowed_of(token)
        limits[t, 0:1] = lo
        limits[t, 1:2] = hi
        limits[t, 2:3] = own
        limits[t, 3:4] = token + 1
    limits[tiles] = jnp.zeros((4, R), jnp.int32)
    top[...] = jnp.full(top.shape, FLOOR, F32)
    tot[...] = jnp.zeros(tot.shape, F32)
    acc[...] = jnp.zeros(acc.shape, F32)

    def base_of(i):
        slot = jnp.where(i < 3, idx[1] + i * CK, idx[2] + (i - 3) * CK)
        return jnp.where(i < 6, slot, jnp.where(i == 6, idx[3], idx[4]))

    def collect(want_full, start):
        def visit(n, count):
            i, t = n // tiles, lax.rem(n, tiles)
            base = base_of(i)
            first = idx[5 + t // 2] + lax.rem(t, 2) * 256
            last = first + 255
            lo_a, hi_a, own_a = allowed_of(first)
            lo_b, hi_b, own_b = allowed_of(last)
            pre = i < 6
            lo_first, lo_last = jnp.where(pre, lo_a, own_a), jnp.where(pre, lo_b, own_b)
            hi_first, hi_last = jnp.where(pre, hi_a, first + 1), jnp.where(pre, hi_b, last + 1)
            some = (base + CK > lo_first) & (base < hi_last)
            full = (base >= lo_last) & (base + CK <= hi_first)
            hit = full if want_full else (some & jnp.logical_not(full))

            @pl.when(hit)
            def _():
                chunk_of[count] = i
                tile_of[count] = t

            return count + hit.astype(jnp.int32)

        count = lax.fori_loop(0, CHUNKS * tiles, visit, start)
        rounds = (count + UNROLL - 1) // UNROLL
        for k in range(UNROLL):
            chunk_of[count + k] = 0
            tile_of[count + k] = tiles
        return rounds

    full_rounds = collect(True, 0)
    all_rounds = collect(False, full_rounds * UNROLL)
    for c in copies:
        c.wait()
    q[tiles * R : (tiles + 1) * R] = jnp.zeros((R, H), BF16)

    def scores(n, out):
        keys = keep[pl.ds(pl.multiple_of(chunk_of[n] * CK, CK), CK), :H]
        out[...] = nt_dot(keys, q[pl.ds(pl.multiple_of(tile_of[n] * R, R), R), :])

    def consume(n, s_ref, masked):
        i, t = chunk_of[n], tile_of[n]
        s = s_ref[...]
        if masked:
            pos = base_of(i) + lax.broadcasted_iota(jnp.int32, (CK, R), 0)
            kind = jnp.where(i < 6, 0, 2)
            lo, hi = limits[t, pl.ds(kind, 1)], limits[t, pl.ds(kind + 1, 1)]
            s = jnp.where((pos >= lo) & (pos < hi), s, -jnp.inf)
        old = top[t]
        new = jnp.maximum(old, jnp.max(s, axis=0, keepdims=True))
        p = jnp.exp2(s * SCALE2 - new * SCALE2)
        factor = jnp.exp2((old - new) * SCALE2)
        top[t] = new
        tot[t] = tot[t] * factor + jnp.sum(p, axis=0, keepdims=True)
        values = keep[pl.ds(pl.multiple_of(i * CK, CK), CK), H:]
        acc[t] = acc[t] * factor + lax.dot_general(
            values, p.astype(BF16), (((0,), (0,)), ((), ())), preferred_element_type=F32
        )

    def rounds(masked):
        def body(n, _):
            for k in range(UNROLL):
                cur, nxt = (sa, sb) if k % 2 == 0 else (sb, sa)
                scores(n * UNROLL + k + 1, nxt)
                consume(n * UNROLL + k, cur, masked)
            return 0

        return body

    chunk_of[all_rounds * UNROLL] = 0
    tile_of[all_rounds * UNROLL] = tiles
    scores(0, sa)
    lax.fori_loop(0, full_rounds, rounds(False), 0)
    lax.fori_loop(full_rounds, all_rounds, rounds(True), 0)

    for t in range(tiles):
        total = tot[t]
        safe = jnp.where(total > 0.0, total, 1.0)
        cols = slice((t % 2) * R, (t % 2 + 1) * R)
        out = outs[t // 2]
        out[0:H, cols] = (acc[t] / safe).astype(BF16)
        lse = jnp.where(total > 0.0, top[t] * SCALE2 + jnp.log2(safe), FLOOR)
        high = lse.astype(BF16).astype(F32)
        mid = (lse - high).astype(BF16).astype(F32)
        low = lse - high - mid
        row = lax.broadcasted_iota(jnp.int32, (16, R), 0)
        packed = jnp.where(row == 0, high, jnp.where(row == 1, mid, jnp.where(row == 2, low, 0.0)))
        out[H : H + 16, cols] = packed.astype(BF16)


def attend(idx, suffix_lengths, prefix_lengths, qs, caches, kvs):
    count, tiles = len(qs), 2 * len(qs)
    return pl.pallas_call(
        functools.partial(attend_kernel, count),
        out_shape=tuple(jax.ShapeDtypeStruct((H + 16, 1024), BF16) for _ in range(count)),
        in_specs=[SMEM] * 3 + [HBM] * (count + 4),
        out_specs=tuple([VMEM] * count),
        scratch_shapes=[
            pltpu.VMEM(((tiles + 1) * R, H), BF16),
            pltpu.VMEM((CHUNKS * CK, 2 * H), BF16),
            pltpu.VMEM((tiles + 1, 4, R), jnp.int32),
            pltpu.VMEM((tiles + 1, 1, R), F32),
            pltpu.VMEM((tiles + 1, 1, R), F32),
            pltpu.VMEM((tiles + 1, H, R), F32),
            pltpu.VMEM((CK, R), F32),
            pltpu.VMEM((CK, R), F32),
            pltpu.SMEM((CHUNKS * tiles + 4 * UNROLL,), jnp.int32),
            pltpu.SMEM((CHUNKS * tiles + 4 * UNROLL,), jnp.int32),
            pltpu.SemaphoreType.DMA((count + 6,)),
        ],
        compiler_params=pltpu.CompilerParams(vmem_limit_bytes=20 << 20),
        cost_estimate=pl.CostEstimate(
            flops=count * (3 << 30), bytes_accessed=4 << 20, transcendentals=count << 21
        ),
        name="attend",
    )(idx, suffix_lengths, prefix_lengths, *pin([*qs, *caches, *kvs]))


def combine_kernel(gates, p0, p1, p2, p3, out):
    parts = (p0, p1, p2, p3)
    lses = []
    for p in parts:
        rows = p[H : H + 16].astype(F32)
        lses.append(rows[0:1] + rows[1:2] + rows[2:3])
    high = jnp.maximum(jnp.maximum(lses[0], lses[1]), jnp.maximum(lses[2], lses[3]))
    share = [jnp.exp2(v - high) for v in lses]
    norm = gates[...] / (share[0] + share[1] + share[2] + share[3])
    for at in range(0, 1024, 256):
        cols = slice(at, at + 256)
        total = jnp.zeros((H, 256), F32)
        for p, s in zip(parts, share):
            total += p[0:H, cols].astype(F32) * s[:, cols]
        out[cols] = jnp.transpose(total * norm[:, cols]).astype(BF16)


def combine(gates, parts):
    return pl.pallas_call(
        combine_kernel,
        out_shape=jax.ShapeDtypeStruct((1024, H), BF16),
        in_specs=[VMEM] * 5,
        out_specs=VMEM,
        compiler_params=pltpu.CompilerParams(vmem_limit_bytes=8 << 20),
        cost_estimate=pl.CostEstimate(flops=1 << 22, bytes_accessed=2 << 20, transcendentals=0),
        name="combine",
    )(gates, *parts)


def out_kernel(idx, routes, own, other, *refs):
    blocks = refs[:10]
    out, held, padded, sem = refs[10:]
    core = idx[8]
    copies = []
    for k, slot in enumerate((0, 1, 2, 3, 6, 7)):
        copies.append(pltpu.make_async_copy(blocks[k], held.at[slot], sem.at[k]))
    for k in range(6, 10):
        target = held.at[4 + (k - 6) // 2, pl.ds((k % 2) * 1024, 1024)]
        copies.append(pltpu.make_async_copy(blocks[k], target, sem.at[k]))
    for c in copies:
        c.start()
    for half in range(2):
        rows = slice(half * 256, (half + 1) * 256)
        wanted = [jnp.broadcast_to(routes[rows, j : j + 1], (256, H)) for j in range(2)]
        for side, source in enumerate((own, other)):
            head = core if side == 0 else 1 - core
            first = source[half * 512 : half * 512 + 256].astype(F32)
            second = source[half * 512 + 256 : half * 512 + 512].astype(F32)
            for e in range(E):
                value = jnp.where(wanted[1] == e, second, 0.0)
                value = jnp.where(wanted[0] == e, first, value).astype(BF16)
                padded[rows, pl.ds(pl.multiple_of((head * E + e) * H, H), H)] = value
    for k, arrived in ((0, copies[0:2]), (2, copies[2:4]), (6, copies[4:6]), (4, copies[6:])):
        for c in arrived:
            c.wait()
        w = jnp.concatenate([held[k], held[k + 1]], axis=1)
        value = jnp.dot(padded[...], w, preferred_element_type=F32)
        for s in range(2):
            out[idx[k + s]] = value[:, s * H : (s + 1) * H].astype(BF16)


def project_out(idx, routes, own, other, blocks):
    return pl.pallas_call(
        out_kernel,
        out_shape=jax.ShapeDtypeStruct((8, 512, H), BF16),
        in_specs=[SMEM, VMEM, VMEM, VMEM] + [HBM] * 10,
        out_specs=VMEM,
        scratch_shapes=[
            pltpu.VMEM((8, 2048, H), BF16),
            pltpu.VMEM((512, 2048), BF16),
            pltpu.SemaphoreType.DMA((10,)),
        ],
        compiler_params=pltpu.CompilerParams(vmem_limit_bytes=20 << 20),
        cost_estimate=pl.CostEstimate(flops=4 << 30, bytes_accessed=6 << 20, transcendentals=0),
        name="project_out",
    )(idx, routes, own, other, *pin(blocks))


def on_device(
    tokens,
    norm_gain,
    router,
    routes,
    kv_weight,
    query_weight,
    out_weight,
    prefix_cache,
    suffix_lengths,
    prefix_lengths,
):
    xl, y, c = (lax.axis_index(a) for a in WIDE)
    first_core = c == 0
    chips = chip_order()

    def table(values):
        return jnp.stack([jnp.asarray(v, jnp.int32) for v in values])

    def head_rows(w, h):
        rows = w.shape[0] // 2
        return lax.dynamic_slice_in_dim(w, h * rows, rows, 0)

    def weights_of(h):
        return jnp.concatenate([head_rows(query_weight, h), head_rows(kv_weight, h)], axis=0)

    w = jnp.stack([weights_of(c), across_core(weights_of(1 - c))])
    other_routes = across_core(routes)
    both_routes = jnp.where(
        first_core,
        jnp.concatenate([routes, other_routes]),
        jnp.concatenate([other_routes, routes]),
    )

    def cache_of(h):
        return lax.dynamic_slice_in_dim(prefix_cache, h * 2 * H, 2 * H, 1)

    cache = jnp.stack([cache_of(c), across_core(cache_of(1 - c))])
    half_row = across_far(tokens)
    far, ym, yp, a = along_y(w, 2), along_y(w, 3), along_y(w, 1), across_x(w)
    caches = [cache, across_x(cache)]
    blocks = [lax.all_gather(v, "z", axis=0) for v in (tokens, half_row)]
    xh = lax.axis_index("xh")
    token_src = [k * 2 + (xh ^ s) for s in range(2) for k in range(4)]
    places = [lax.rem(lax.rem(v, 4) + 4 - y, 4) * 2 + (v // 4 ^ xl) for v in token_src]
    normed = normalise(table(token_src + places), norm_gain.reshape(8, 1, 256), blocks)
    far, ym, yp, a, normed, caches, both_routes = lax.optimization_barrier(
        (far, ym, yp, a, normed, caches, both_routes)
    )
    am, ap, afar = along_y(a, 3), along_y(a, 1), across_x(far)
    other_normed = across_core(normed)
    gathered = [w, a, ym, am, far, afar, yp, ap]

    out_early, am, ap = lax.optimization_barrier((out_weight, am, ap))
    gathered[3], gathered[7] = am, ap
    o_ym, o_yp, o_a = along_y(out_early, 3), along_y(out_early, 1), across_x(out_early)
    q, kv, gates = project(
        table(chips + [c]), both_routes, router.T, normed, other_normed, gathered
    )
    kvs = [kv, across_x(kv)]
    qs = [q] + [along_y(q, k) for k in (1, 2, 3)]
    qs[0], o_ym, o_yp = lax.optimization_barrier((q, o_ym, o_yp))
    o_a, up, down, kvs[1] = lax.optimization_barrier((o_a, o_yp[:1024], o_ym[1024:], kvs[1]))
    far0, far1 = along_y(up, 1), along_y(down, 3)
    o_am, o_ap = across_x(o_ym), across_x(o_yp)

    firsts = [(xl * 4 + lax.rem(y + 4 - k, 4)) * 512 for k in range(4)]
    mine, partner = xl * 4 + y, (1 - xl) * 4 + y
    at = [c, mine * 1536, partner * 1536, mine * 512, partner * 512]
    lengths = (suffix_lengths, prefix_lengths)
    (part2,) = attend(table(at + firsts[2:3]), *lengths, qs[2:3], caches, kvs)
    part2, qs[1], qs[3] = lax.optimization_barrier((part2, qs[1], qs[3]))
    part1, part3 = attend(table(at + firsts[1::2]), *lengths, qs[1::2], caches, kvs)
    part2 = along_y(part2, 2)
    part2, qs[0] = tie(part2, qs[0])
    (own,) = attend(table(at + firsts[:1]), *lengths, qs[:1], caches, kvs)
    part1, part3, far0, far1, o_am, o_ap = lax.optimization_barrier(
        (part1, part3, far0, far1, o_am, o_ap)
    )
    parts = [own, along_y(part1, 3), part2, along_y(part3, 1)]
    afar0, afar1 = across_x(far0), across_x(far1)
    parts, afar0, afar1 = lax.optimization_barrier((parts, afar0, afar1))
    out_blocks = [out_weight, o_a, o_ym, o_am, o_yp, o_ap, far0, far1, afar0, afar1]
    gate_row = gates.reshape(2, 256, 2).transpose(0, 2, 1).reshape(1, 1024)
    attended = combine(gate_row, parts)

    sums = project_out(
        table(chips + [c]), both_routes, attended, across_core(attended), out_blocks
    )
    sums = lax.all_to_all(sums, NARROW, 0, 0, tiled=True)
    total = jnp.sum(sums.astype(F32), axis=0)
    here = lax.dynamic_slice_in_dim(total, c * 256, 256, 0).astype(BF16)
    there = lax.dynamic_slice_in_dim(total, (1 - c) * 256, 256, 0).astype(BF16)
    there = across_core(there)
    return jnp.where(
        first_core,
        jnp.concatenate([here, there], axis=1),
        jnp.concatenate([there, here], axis=1),
    )


def solution(mesh):
    fine = Mesh(mesh.devices.reshape(SIZES), AXES)
    placed = (
        P(WIDE, NARROW),
        P(),
        P(),
        P(WIDE, None),
        P(NARROW, WIDE),
        P(NARROW, WIDE),
        P(NARROW, WIDE),
        P(WIDE, NARROW),
        P(),
        P(),
    )
    return jax.shard_map(
        on_device, mesh=fine, in_specs=placed, out_specs=P(WIDE, NARROW), check_vma=False
    )
```

```python
import functools
import math

import jax
import jax.numpy as jnp
from jax import lax
from jax.experimental import pallas as pl
from jax.experimental.pallas import tpu as pltpu
from jax.sharding import Mesh
from jax.sharding import PartitionSpec as P

H = 128
E = 8
EPS = 1e-06
FLOOR = -1e30
AXES = ("xl", "y", "c", "z", "xh")
SIZES = (2, 4, 2, 4, 2)
WIDE = ("xl", "y", "c")
NARROW = ("z", "xh")
BF16 = jnp.bfloat16
F32 = jnp.float32
SCALE2 = H ** (-0.5) * math.log2(math.e)
CK = 512
R = 512
CHUNKS = 8
UNROLL = 4

SMEM = pl.BlockSpec(memory_space=pltpu.SMEM)
VMEM = pl.BlockSpec(memory_space=pltpu.VMEM)
HBM = pl.BlockSpec(memory_space=pltpu.HBM)
ANY = pl.BlockSpec(memory_space=pl.ANY)


def along_y(x, k):
    return lax.ppermute(x, "y", [(i, (i + k) % 4) for i in range(4)])


def across_x(x):
    return lax.ppermute(x, "xl", [(0, 1), (1, 0)])


def across_far(x):
    return lax.ppermute(x, "xh", [(0, 1), (1, 0)])


def across_core(x):
    return lax.ppermute(x, "c", [(0, 1), (1, 0)])


def tie(a, b):
    return lax.optimization_barrier((a, b))


def chip_order():
    xl, y = lax.axis_index("xl"), lax.axis_index("y")
    return [(xl ^ dx) * 4 + lax.rem(y + dy, 4) for dy in range(4) for dx in range(2)]


def pin(arrays):
    return [pltpu.with_memory_space_constraint(a, pltpu.HBM) for a in arrays]


def nt_dot(a, b):
    return lax.dot_general(a, b, (((1,), (1,)), ((), ())), preferred_element_type=F32)


def run(copies):
    for c in copies:
        c.start()
    for c in copies:
        c.wait()


def norm_kernel(idx, gain, b0, b1, normed, held, sem):
    run([pltpu.make_async_copy(r, held.at[i], sem.at[i]) for i, r in enumerate((b0, b1))])
    total = jnp.zeros((256, 1), F32)
    for k in range(8):
        v = held[k // 4, k % 4].astype(F32)
        total = total + jnp.sum(v * v, axis=1, keepdims=True)
    scale = lax.rsqrt(total * (1.0 / 2048) + EPS)
    for k in range(8):
        v = held[k // 4, k % 4].astype(F32) * scale * gain[idx[k]].astype(F32)
        normed[:, pl.ds(pl.multiple_of(idx[8 + k] * 256, 256), 256)] = v.astype(BF16)


def normalise(idx, gain, blocks):
    return pl.pallas_call(
        norm_kernel,
        out_shape=jax.ShapeDtypeStruct((256, 2048), BF16),
        in_specs=[SMEM, VMEM, ANY, ANY],
        out_specs=VMEM,
        scratch_shapes=[pltpu.VMEM((2, 4, 256, 256), BF16), pltpu.SemaphoreType.DMA((2,))],
        compiler_params=pltpu.CompilerParams(vmem_limit_bytes=8 << 20),
        cost_estimate=pl.CostEstimate(flops=1 << 24, bytes_accessed=2 << 20, transcendentals=0),
        name="normalise",
    )(idx, gain, *blocks)


GROUPS = ((0, 256), (256, 512), (768, 512))


def project_kernel(idx, routes, router, own, other, *refs):
    blocks = refs[:8]
    q_out, kv_out, gates, xs, held, sel, sem = refs[8:]
    core = idx[8]
    copies = []
    for i, r in enumerate((own, other)):
        at = pl.multiple_of((core if i == 0 else 1 - core) * 256, 256)
        copies.append(pltpu.make_async_copy(r, xs.at[pl.ds(at, 256)], sem.at[48 + i]))
    for g, (start, rows) in enumerate(GROUPS):
        for k in range(16):
            lane = (k // 2) * 256 + H * (core if k % 2 == 0 else 1 - core)
            at = pl.ds(pl.multiple_of(lane, H), H)
            copies.append(
                pltpu.make_async_copy(
                    blocks[k // 2].at[k % 2, pl.ds(start, rows)],
                    held.at[pl.ds(start, rows), at],
                    sem.at[16 * g + k],
                )
            )
    for c in copies:
        c.start()
    for c in copies[:2]:
        c.wait()
    logits = jnp.zeros((512, E), F32)
    for i in range(8):
        part = router[:, pl.ds(pl.multiple_of(idx[i] * 256, 256), 256)]
        logits += nt_dot(xs[:, i * 256 : (i + 1) * 256], part)
    lane = lax.broadcasted_iota(jnp.int32, (512, E), 1)
    chosen = [
        jnp.sum(jnp.where(routes[:, j : j + 1] == lane, logits, 0.0), axis=1, keepdims=True)
        for j in range(2)
    ]
    top = jnp.maximum(chosen[0], chosen[1])
    e0, e1 = jnp.exp(chosen[0] - top), jnp.exp(chosen[1] - top)
    gates[:, 0:1] = e0 / (e0 + e1)
    gates[:, 1:2] = e1 / (e0 + e1)

    wanted = [jnp.broadcast_to(routes[:, j : j + 1], (512, H)) for j in range(2)]
    for r in range(5):
        for g, (start, rows) in enumerate(GROUPS):
            if start == r * 256:
                for c in copies[2 + 16 * g : 18 + 16 * g]:
                    c.wait()
        acc = nt_dot(xs[...], held[r * 256 : (r + 1) * 256])
        if r == 4:
            kv_out[...] = acc.astype(BF16)
            continue
        for j in range(2):
            value = jnp.zeros((512, H), F32) if r == 0 else sel[j]
            for e in range(2):
                value = jnp.where(wanted[j] == 2 * r + e, acc[:, e * H : (e + 1) * H], value)
            if r < 3:
                sel[j] = value
            else:
                for half in range(2):
                    at = (half * 2 + j) * 256
                    q_out[at : at + 256] = value[half * 256 : (half + 1) * 256].astype(BF16)


def project(idx, routes, router, own, other, blocks):
    return pl.pallas_call(
        project_kernel,
        out_shape=(
            jax.ShapeDtypeStruct((1024, H), BF16),
            jax.ShapeDtypeStruct((512, 2 * H), BF16),
            jax.ShapeDtypeStruct((512, 2), F32),
        ),
        in_specs=[SMEM, VMEM, VMEM] + [HBM] * 10,
        out_specs=(VMEM, VMEM, VMEM),
        scratch_shapes=[
            pltpu.VMEM((512, 2048), BF16),
            pltpu.VMEM((1280, 2048), BF16),
            pltpu.VMEM((2, 512, H), F32),
            pltpu.SemaphoreType.DMA((50,)),
        ],
        compiler_params=pltpu.CompilerParams(vmem_limit_bytes=20 << 20),
        cost_estimate=pl.CostEstimate(flops=6 << 30, bytes_accessed=8 << 20, transcendentals=0),
        name="project",
    )(idx, routes, router, *pin([own, other, *blocks]))


def attend_kernel(count, idx, ends_s, ends_p, *refs):
    queries, (cache0, cache1, kv0, kv1) = refs[:count], refs[count : count + 4]
    outs = refs[count + 4 : 2 * count + 4]
    q, keep, limits, top, tot, acc, sa, sb, chunk_of, tile_of, part_of, sem = refs[2 * count + 4 :]
    tiles = 2 * count
    core = idx[0]
    copies = [
        pltpu.make_async_copy(r, q.at[pl.ds(1024 * b, 1024)], sem.at[b])
        for b, r in enumerate(queries)
    ]
    for i, r in enumerate((cache0, cache1)):
        for side in range(2):
            at = pl.multiple_of(i * 1536 + 768 * (core if side == 0 else 1 - core), 256)
            copies.append(
                pltpu.make_async_copy(r.at[side], keep.at[pl.ds(at, 768)], sem.at[count + 2 * i + side])
            )
    for i, r in enumerate((kv0, kv1)):
        copies.append(
            pltpu.make_async_copy(r, keep.at[pl.ds(3072 + 512 * i, 512)], sem.at[count + 4 + i])
        )
    for c in copies:
        c.start()

    se, pe = [ends_s[0]], [ends_p[0]]
    for k in range(1, 4):
        se.append(se[-1] + ends_s[k])
        pe.append(pe[-1] + ends_p[k])

    def allowed_of(token):
        lo, hi, own = 0 * token, 0 * token + pe[0], 0 * token
        for k in range(3):
            later = token >= se[k]
            lo = jnp.where(later, pe[k], lo)
            hi = jnp.where(later, pe[k + 1], hi)
            own = jnp.where(later, se[k], own)
        return lo, hi, own

    for t in range(tiles):
        first = idx[5 + t // 2] + (t % 2) * 256
        token = first + lax.rem(lax.broadcasted_iota(jnp.int32, (1, R), 1), 256)
        lo, hi, own = allowed_of(token)
        limits[t, 0:1] = lo
        limits[t, 1:2] = hi
        limits[t, 2:3] = own
        limits[t, 3:4] = token + 1
    limits[tiles] = jnp.zeros((4, R), jnp.int32)
    top[...] = jnp.full(top.shape, FLOOR, F32)
    tot[...] = jnp.zeros(tot.shape, F32)
    acc[...] = jnp.zeros(acc.shape, F32)

    def base_of(i):
        slot = jnp.where(i < 3, idx[1] + i * CK, idx[2] + (i - 3) * CK)
        return jnp.where(i < 6, slot, jnp.where(i == 6, idx[3], idx[4]))

    def visit(n, counts):
        whole, partial = counts
        i, t = n // tiles, lax.rem(n, tiles)
        base = base_of(i)
        first = idx[5 + t // 2] + lax.rem(t, 2) * 256
        last = first + 255
        lo_a, hi_a, own_a = allowed_of(first)
        lo_b, hi_b, own_b = allowed_of(last)
        pre = i < 6
        lo_first, lo_last = jnp.where(pre, lo_a, own_a), jnp.where(pre, lo_b, own_b)
        hi_first, hi_last = jnp.where(pre, hi_a, first + 1), jnp.where(pre, hi_b, last + 1)
        some = (base + CK > lo_first) & (base < hi_last)
        full = (base >= lo_last) & (base + CK <= hi_first)
        part = some & jnp.logical_not(full)

        @pl.when(full)
        def _():
            chunk_of[whole] = i
            tile_of[whole] = t

        @pl.when(part)
        def _():
            part_of[partial] = n

        return whole + full.astype(jnp.int32), partial + part.astype(jnp.int32)

    def pad(count):
        for k in range(UNROLL):
            chunk_of[count + k] = 0
            tile_of[count + k] = tiles
        return (count + UNROLL - 1) // UNROLL

    whole, partial = lax.fori_loop(0, CHUNKS * tiles, visit, (0, 0))
    full_rounds = pad(whole)
    start = full_rounds * UNROLL

    def move(k, _):
        n = part_of[k]
        chunk_of[start + k] = n // tiles
        tile_of[start + k] = lax.rem(n, tiles)
        return 0

    lax.fori_loop(0, partial, move, 0)
    all_rounds = pad(start + partial)
    for c in copies:
        c.wait()
    q[tiles * R : (tiles + 1) * R] = jnp.zeros((R, H), BF16)

    def scores(n, out):
        keys = keep[pl.ds(pl.multiple_of(chunk_of[n] * CK, CK), CK), :H]
        out[...] = nt_dot(keys, q[pl.ds(pl.multiple_of(tile_of[n] * R, R), R), :])

    def consume(n, s_ref, masked):
        i, t = chunk_of[n], tile_of[n]
        s = s_ref[...]
        if masked:
            pos = base_of(i) + lax.broadcasted_iota(jnp.int32, (CK, R), 0)
            kind = jnp.where(i < 6, 0, 2)
            lo, hi = limits[t, pl.ds(kind, 1)], limits[t, pl.ds(kind + 1, 1)]
            s = jnp.where((pos >= lo) & (pos < hi), s, -jnp.inf)
        old = top[t]
        new = jnp.maximum(old, jnp.max(s, axis=0, keepdims=True))
        p = jnp.exp2(s * SCALE2 - new * SCALE2)
        factor = jnp.exp2((old - new) * SCALE2)
        top[t] = new
        tot[t] = tot[t] * factor + jnp.sum(p, axis=0, keepdims=True)
        values = keep[pl.ds(pl.multiple_of(i * CK, CK), CK), H:]
        acc[t] = acc[t] * factor + lax.dot_general(
            values, p.astype(BF16), (((0,), (0,)), ((), ())), preferred_element_type=F32
        )

    def rounds(masked):
        def body(n, _):
            for k in range(UNROLL):
                cur, nxt = (sa, sb) if k % 2 == 0 else (sb, sa)
                scores(n * UNROLL + k + 1, nxt)
                consume(n * UNROLL + k, cur, masked)
            return 0

        return body

    chunk_of[all_rounds * UNROLL] = 0
    tile_of[all_rounds * UNROLL] = tiles
    scores(0, sa)
    lax.fori_loop(0, full_rounds, rounds(False), 0)
    lax.fori_loop(full_rounds, all_rounds, rounds(True), 0)

    for t in range(tiles):
        total = tot[t]
        safe = jnp.where(total > 0.0, total, 1.0)
        cols = slice((t % 2) * R, (t % 2 + 1) * R)
        out = outs[t // 2]
        out[0:H, cols] = (acc[t] / safe).astype(BF16)
        lse = jnp.where(total > 0.0, top[t] * SCALE2 + jnp.log2(safe), FLOOR)
        high = lse.astype(BF16).astype(F32)
        mid = (lse - high).astype(BF16).astype(F32)
        low = lse - high - mid
        row = lax.broadcasted_iota(jnp.int32, (16, R), 0)
        packed = jnp.where(row == 0, high, jnp.where(row == 1, mid, jnp.where(row == 2, low, 0.0)))
        out[H : H + 16, cols] = packed.astype(BF16)


def attend(idx, suffix_lengths, prefix_lengths, qs, caches, kvs):
    count, tiles = len(qs), 2 * len(qs)
    return pl.pallas_call(
        functools.partial(attend_kernel, count),
        out_shape=tuple(jax.ShapeDtypeStruct((H + 16, 1024), BF16) for _ in range(count)),
        in_specs=[SMEM] * 3 + [HBM] * (count + 4),
        out_specs=tuple([VMEM] * count),
        scratch_shapes=[
            pltpu.VMEM(((tiles + 1) * R, H), BF16),
            pltpu.VMEM((CHUNKS * CK, 2 * H), BF16),
            pltpu.VMEM((tiles + 1, 4, R), jnp.int32),
            pltpu.VMEM((tiles + 1, 1, R), F32),
            pltpu.VMEM((tiles + 1, 1, R), F32),
            pltpu.VMEM((tiles + 1, H, R), F32),
            pltpu.VMEM((CK, R), F32),
            pltpu.VMEM((CK, R), F32),
            pltpu.SMEM((CHUNKS * tiles + 4 * UNROLL,), jnp.int32),
            pltpu.SMEM((CHUNKS * tiles + 4 * UNROLL,), jnp.int32),
            pltpu.SMEM((CHUNKS * tiles,), jnp.int32),
            pltpu.SemaphoreType.DMA((count + 6,)),
        ],
        compiler_params=pltpu.CompilerParams(vmem_limit_bytes=20 << 20),
        cost_estimate=pl.CostEstimate(
            flops=count * (3 << 30), bytes_accessed=4 << 20, transcendentals=count << 21
        ),
        name="attend",
    )(idx, suffix_lengths, prefix_lengths, *pin([*qs, *caches, *kvs]))


def combine_kernel(gates, p0, p1, p2, p3, out):
    parts = (p0, p1, p2, p3)
    lses = []
    for p in parts:
        rows = p[H : H + 16].astype(F32)
        lses.append(rows[0:1] + rows[1:2] + rows[2:3])
    high = jnp.maximum(jnp.maximum(lses[0], lses[1]), jnp.maximum(lses[2], lses[3]))
    share = [jnp.exp2(v - high) for v in lses]
    norm = gates[...] / (share[0] + share[1] + share[2] + share[3])
    for at in range(0, 1024, 256):
        cols = slice(at, at + 256)
        total = jnp.zeros((H, 256), F32)
        for p, s in zip(parts, share):
            total += p[0:H, cols].astype(F32) * s[:, cols]
        out[cols] = jnp.transpose(total * norm[:, cols]).astype(BF16)


def combine(gates, parts):
    return pl.pallas_call(
        combine_kernel,
        out_shape=jax.ShapeDtypeStruct((1024, H), BF16),
        in_specs=[VMEM] * 5,
        out_specs=VMEM,
        compiler_params=pltpu.CompilerParams(vmem_limit_bytes=8 << 20),
        cost_estimate=pl.CostEstimate(flops=1 << 22, bytes_accessed=2 << 20, transcendentals=0),
        name="combine",
    )(gates, *parts)


def out_kernel(idx, routes, own, other, *refs):
    blocks = refs[:10]
    out, held, padded, sem = refs[10:]
    core = idx[8]
    copies = []
    for k, slot in enumerate((0, 1, 2, 3, 6, 7)):
        copies.append(pltpu.make_async_copy(blocks[k], held.at[idx[slot]], sem.at[k]))
    for k in range(6, 10):
        target = held.at[idx[4 + (k - 6) // 2], pl.ds((k % 2) * 1024, 1024)]
        copies.append(pltpu.make_async_copy(blocks[k], target, sem.at[k]))
    for c in copies:
        c.start()
    for half in range(2):
        rows = slice(half * 256, (half + 1) * 256)
        wanted = [jnp.broadcast_to(routes[rows, j : j + 1], (256, H)) for j in range(2)]
        for side, source in enumerate((own, other)):
            head = core if side == 0 else 1 - core
            first = source[half * 512 : half * 512 + 256].astype(F32)
            second = source[half * 512 + 256 : half * 512 + 512].astype(F32)
            for e in range(E):
                value = jnp.where(wanted[1] == e, second, 0.0)
                value = jnp.where(wanted[0] == e, first, value).astype(BF16)
                padded[rows, pl.ds(pl.multiple_of((head * E + e) * H, H), H)] = value
    for c in copies:
        c.wait()
    for k in range(0, 8, 2):
        w = jnp.concatenate([held[k], held[k + 1]], axis=1)
        value = jnp.dot(padded[...], w, preferred_element_type=F32)
        for s in range(2):
            out[k + s] = value[:, s * H : (s + 1) * H].astype(BF16)


def project_out(idx, routes, own, other, blocks):
    return pl.pallas_call(
        out_kernel,
        out_shape=jax.ShapeDtypeStruct((8, 512, H), BF16),
        in_specs=[SMEM, VMEM, VMEM, VMEM] + [HBM] * 10,
        out_specs=VMEM,
        scratch_shapes=[
            pltpu.VMEM((8, 2048, H), BF16),
            pltpu.VMEM((512, 2048), BF16),
            pltpu.SemaphoreType.DMA((10,)),
        ],
        compiler_params=pltpu.CompilerParams(vmem_limit_bytes=20 << 20),
        cost_estimate=pl.CostEstimate(flops=4 << 30, bytes_accessed=6 << 20, transcendentals=0),
        name="project_out",
    )(idx, routes, own, other, *pin(blocks))


def on_device(
    tokens,
    norm_gain,
    router,
    routes,
    kv_weight,
    query_weight,
    out_weight,
    prefix_cache,
    suffix_lengths,
    prefix_lengths,
):
    xl, y, c = (lax.axis_index(a) for a in WIDE)
    first_core = c == 0
    chips = chip_order()

    def table(values):
        return jnp.stack([jnp.asarray(v, jnp.int32) for v in values])

    def head_rows(w, h):
        rows = w.shape[0] // 2
        return lax.dynamic_slice_in_dim(w, h * rows, rows, 0)

    def weights_of(h):
        return jnp.concatenate([head_rows(query_weight, h), head_rows(kv_weight, h)], axis=0)

    w = jnp.stack([weights_of(c), across_core(weights_of(1 - c))])
    other_routes = across_core(routes)
    both_routes = jnp.where(
        first_core,
        jnp.concatenate([routes, other_routes]),
        jnp.concatenate([other_routes, routes]),
    )

    def cache_of(h):
        return lax.dynamic_slice_in_dim(prefix_cache, h * 2 * H, 2 * H, 1)

    cache = jnp.stack([cache_of(c), across_core(cache_of(1 - c))])
    half_row = across_far(tokens)
    far, ym, yp, a = along_y(w, 2), along_y(w, 3), along_y(w, 1), across_x(w)
    caches = [cache, across_x(cache)]
    blocks = [lax.all_gather(v, "z", axis=0) for v in (tokens, half_row)]
    xh = lax.axis_index("xh")
    token_src = [k * 2 + (xh ^ s) for s in range(2) for k in range(4)]
    places = [lax.rem(lax.rem(v, 4) + 4 - y, 4) * 2 + (v // 4 ^ xl) for v in token_src]
    normed = normalise(table(token_src + places), norm_gain.reshape(8, 1, 256), blocks)
    far, ym, yp, a, normed, caches, both_routes = lax.optimization_barrier(
        (far, ym, yp, a, normed, caches, both_routes)
    )
    am, ap, afar = along_y(a, 3), along_y(a, 1), across_x(far)
    other_normed = across_core(normed)
    gathered = [w, a, ym, am, far, afar, yp, ap]

    out_early, am, ap = lax.optimization_barrier((out_weight, am, ap))
    gathered[3], gathered[7] = am, ap
    o_ym, o_yp, o_a = along_y(out_early, 3), along_y(out_early, 1), across_x(out_early)
    q, kv, gates = project(
        table(chips + [c]), both_routes, router.T, normed, other_normed, gathered
    )
    kvs = [kv, across_x(kv)]
    qs = [q] + [along_y(q, k) for k in (1, 2, 3)]
    qs[0], o_ym, o_yp = lax.optimization_barrier((q, o_ym, o_yp))
    o_a, up, down, kvs[1] = lax.optimization_barrier((o_a, o_yp[:1024], o_ym[1024:], kvs[1]))
    far0, far1 = along_y(up, 1), along_y(down, 3)
    o_am, o_ap = across_x(o_ym), across_x(o_yp)

    firsts = [(xl * 4 + lax.rem(y + 4 - k, 4)) * 512 for k in range(4)]
    mine, partner = xl * 4 + y, (1 - xl) * 4 + y
    at = [c, mine * 1536, partner * 1536, mine * 512, partner * 512]
    lengths = (suffix_lengths, prefix_lengths)
    parts = list(attend(table(at + firsts[:1]), *lengths, qs[:1], caches, kvs))
    parts += list(attend(table(at + firsts[1:]), *lengths, qs[1:], caches, kvs))
    parts[1:], far0, far1, o_am, o_ap = lax.optimization_barrier(
        (parts[1:], far0, far1, o_am, o_ap)
    )
    for k in range(1, 4):
        parts[k] = along_y(parts[k], 4 - k)
    afar0, afar1 = across_x(far0), across_x(far1)
    parts, afar0, afar1 = lax.optimization_barrier((parts, afar0, afar1))
    out_blocks = [out_weight, o_a, o_ym, o_am, o_yp, o_ap, far0, far1, afar0, afar1]
    gate_row = gates.reshape(2, 256, 2).transpose(0, 2, 1).reshape(1, 1024)
    attended = combine(gate_row, parts)

    sums = project_out(
        table(chips + [c]), both_routes, attended, across_core(attended), out_blocks
    )
    sums = lax.all_to_all(sums, NARROW, 0, 0, tiled=True)
    total = jnp.sum(sums.astype(F32), axis=0)
    here = lax.dynamic_slice_in_dim(total, c * 256, 256, 0).astype(BF16)
    there = lax.dynamic_slice_in_dim(total, (1 - c) * 256, 256, 0).astype(BF16)
    there = across_core(there)
    return jnp.where(
        first_core,
        jnp.concatenate([here, there], axis=1),
        jnp.concatenate([there, here], axis=1),
    )


def solution(mesh):
    fine = Mesh(mesh.devices.reshape(SIZES), AXES)
    placed = (
        P(WIDE, NARROW),
        P(),
        P(),
        P(WIDE, None),
        P(NARROW, WIDE),
        P(NARROW, WIDE),
        P(NARROW, WIDE),
        P(WIDE, NARROW),
        P(),
        P(),
    )
    return jax.shard_map(
        on_device, mesh=fine, in_specs=placed, out_specs=P(WIDE, NARROW), check_vma=False
    )
```

```python
import functools
import math

import jax
import jax.numpy as jnp
from jax import lax
from jax.experimental import pallas as pl
from jax.experimental.pallas import tpu as pltpu
from jax.sharding import Mesh
from jax.sharding import PartitionSpec as P

H = 128
E = 8
EPS = 1e-06
FLOOR = -1e30
AXES = ("xl", "y", "c", "z", "xh")
SIZES = (2, 4, 2, 4, 2)
WIDE = ("xl", "y", "c")
NARROW = ("z", "xh")
BF16 = jnp.bfloat16
F32 = jnp.float32
SCALE2 = H ** (-0.5) * math.log2(math.e)
CK = 512
R = 512
CHUNKS = 8
UNROLL = 4

SMEM = pl.BlockSpec(memory_space=pltpu.SMEM)
VMEM = pl.BlockSpec(memory_space=pltpu.VMEM)
HBM = pl.BlockSpec(memory_space=pltpu.HBM)
ANY = pl.BlockSpec(memory_space=pl.ANY)


def along_y(x, k):
    return lax.ppermute(x, "y", [(i, (i + k) % 4) for i in range(4)])


def across_x(x):
    return lax.ppermute(x, "xl", [(0, 1), (1, 0)])


def across_far(x):
    return lax.ppermute(x, "xh", [(0, 1), (1, 0)])


def across_core(x):
    return lax.ppermute(x, "c", [(0, 1), (1, 0)])


def tie(a, b):
    return lax.optimization_barrier((a, b))


def chip_order():
    xl, y = lax.axis_index("xl"), lax.axis_index("y")
    return [(xl ^ dx) * 4 + lax.rem(y + dy, 4) for dy in range(4) for dx in range(2)]


def pin(arrays):
    return [pltpu.with_memory_space_constraint(a, pltpu.HBM) for a in arrays]


def nt_dot(a, b):
    return lax.dot_general(a, b, (((1,), (1,)), ((), ())), preferred_element_type=F32)


def run(copies):
    for c in copies:
        c.start()
    for c in copies:
        c.wait()


def norm_kernel(idx, gain, b0, b1, normed, held, sem):
    run([pltpu.make_async_copy(r, held.at[i], sem.at[i]) for i, r in enumerate((b0, b1))])
    total = jnp.zeros((256, 1), F32)
    for k in range(8):
        v = held[k // 4, k % 4].astype(F32)
        total = total + jnp.sum(v * v, axis=1, keepdims=True)
    scale = lax.rsqrt(total * (1.0 / 2048) + EPS)
    for k in range(8):
        v = held[k // 4, k % 4].astype(F32) * scale * gain[idx[k]].astype(F32)
        normed[:, pl.ds(pl.multiple_of(idx[8 + k] * 256, 256), 256)] = v.astype(BF16)


def normalise(idx, gain, blocks):
    return pl.pallas_call(
        norm_kernel,
        out_shape=jax.ShapeDtypeStruct((256, 2048), BF16),
        in_specs=[SMEM, VMEM, ANY, ANY],
        out_specs=VMEM,
        scratch_shapes=[pltpu.VMEM((2, 4, 256, 256), BF16), pltpu.SemaphoreType.DMA((2,))],
        compiler_params=pltpu.CompilerParams(vmem_limit_bytes=8 << 20),
        cost_estimate=pl.CostEstimate(flops=1 << 24, bytes_accessed=2 << 20, transcendentals=0),
        name="normalise",
    )(idx, gain, *blocks)


GROUPS = ((0, 512), (512, 768))


def project_kernel(idx, routes, router, own, other, *refs):
    blocks = refs[:8]
    q_out, kv_out, gates, xs, held, sel, sem = refs[8:]
    core = idx[8]
    copies = []
    for i, r in enumerate((own, other)):
        at = pl.multiple_of((core if i == 0 else 1 - core) * 256, 256)
        copies.append(pltpu.make_async_copy(r, xs.at[pl.ds(at, 256)], sem.at[32 + i]))
    for g, (start, rows) in enumerate(GROUPS):
        for k in range(16):
            lane = (k // 2) * 256 + H * (core if k % 2 == 0 else 1 - core)
            at = pl.ds(pl.multiple_of(lane, H), H)
            copies.append(
                pltpu.make_async_copy(
                    blocks[k // 2].at[k % 2, pl.ds(start, rows)],
                    held.at[pl.ds(start, rows), at],
                    sem.at[16 * g + k],
                )
            )
    for c in copies:
        c.start()
    for c in copies[:2]:
        c.wait()
    logits = jnp.zeros((512, E), F32)
    for i in range(8):
        part = router[:, pl.ds(pl.multiple_of(idx[i] * 256, 256), 256)]
        logits += nt_dot(xs[:, i * 256 : (i + 1) * 256], part)
    lane = lax.broadcasted_iota(jnp.int32, (512, E), 1)
    chosen = [
        jnp.sum(jnp.where(routes[:, j : j + 1] == lane, logits, 0.0), axis=1, keepdims=True)
        for j in range(2)
    ]
    top = jnp.maximum(chosen[0], chosen[1])
    e0, e1 = jnp.exp(chosen[0] - top), jnp.exp(chosen[1] - top)
    gates[:, 0:1] = e0 / (e0 + e1)
    gates[:, 1:2] = e1 / (e0 + e1)

    wanted = [jnp.broadcast_to(routes[:, j : j + 1], (512, H)) for j in range(2)]
    for r in range(5):
        if r == 0:
            for c in copies[2:18]:
                c.wait()
        if r == 2:
            for c in copies[18:]:
                c.wait()
        acc = nt_dot(xs[...], held[r * 256 : (r + 1) * 256])
        if r == 4:
            kv_out[...] = acc.astype(BF16)
            continue
        for j in range(2):
            value = jnp.zeros((512, H), F32) if r == 0 else sel[j]
            for e in range(2):
                value = jnp.where(wanted[j] == 2 * r + e, acc[:, e * H : (e + 1) * H], value)
            if r < 3:
                sel[j] = value
            else:
                for half in range(2):
                    at = (half * 2 + j) * 256
                    q_out[at : at + 256] = value[half * 256 : (half + 1) * 256].astype(BF16)


def project(idx, routes, router, own, other, blocks):
    return pl.pallas_call(
        project_kernel,
        out_shape=(
            jax.ShapeDtypeStruct((1024, H), BF16),
            jax.ShapeDtypeStruct((512, 2 * H), BF16),
            jax.ShapeDtypeStruct((512, 2), F32),
        ),
        in_specs=[SMEM, VMEM, VMEM] + [HBM] * 10,
        out_specs=(VMEM, VMEM, VMEM),
        scratch_shapes=[
            pltpu.VMEM((512, 2048), BF16),
            pltpu.VMEM((1280, 2048), BF16),
            pltpu.VMEM((2, 512, H), F32),
            pltpu.SemaphoreType.DMA((34,)),
        ],
        compiler_params=pltpu.CompilerParams(vmem_limit_bytes=20 << 20),
        cost_estimate=pl.CostEstimate(flops=6 << 30, bytes_accessed=8 << 20, transcendentals=0),
        name="project",
    )(idx, routes, router, *pin([own, other, *blocks]))


def attend_kernel(count, idx, ends_s, ends_p, *refs):
    queries, (cache0, cache1, kv0, kv1) = refs[:count], refs[count : count + 4]
    outs = refs[count + 4 : 2 * count + 4]
    q, keep, limits, top, tot, acc, sa, sb, chunk_of, tile_of, sem = refs[2 * count + 4 :]
    tiles = 2 * count
    core = idx[0]
    copies = [
        pltpu.make_async_copy(r, q.at[pl.ds(1024 * b, 1024)], sem.at[b])
        for b, r in enumerate(queries)
    ]
    for i, r in enumerate((cache0, cache1)):
        for side in range(2):
            at = pl.multiple_of(i * 1536 + 768 * (core if side == 0 else 1 - core), 256)
            copies.append(
                pltpu.make_async_copy(r.at[side], keep.at[pl.ds(at, 768)], sem.at[count + 2 * i + side])
            )
    for i, r in enumerate((kv0, kv1)):
        copies.append(
            pltpu.make_async_copy(r, keep.at[pl.ds(3072 + 512 * i, 512)], sem.at[count + 4 + i])
        )
    for c in copies:
        c.start()

    se, pe = [ends_s[0]], [ends_p[0]]
    for k in range(1, 4):
        se.append(se[-1] + ends_s[k])
        pe.append(pe[-1] + ends_p[k])

    def allowed_of(token):
        lo, hi, own = 0 * token, 0 * token + pe[0], 0 * token
        for k in range(3):
            later = token >= se[k]
            lo = jnp.where(later, pe[k], lo)
            hi = jnp.where(later, pe[k + 1], hi)
            own = jnp.where(later, se[k], own)
        return lo, hi, own

    for t in range(tiles):
        first = idx[5 + t // 2] + (t % 2) * 256
        token = first + lax.rem(lax.broadcasted_iota(jnp.int32, (1, R), 1), 256)
        lo, hi, own = allowed_of(token)
        limits[t, 0:1] = lo
        limits[t, 1:2] = hi
        limits[t, 2:3] = own
        limits[t, 3:4] = token + 1
    limits[tiles] = jnp.zeros((4, R), jnp.int32)
    top[...] = jnp.full(top.shape, FLOOR, F32)
    tot[...] = jnp.zeros(tot.shape, F32)
    acc[...] = jnp.zeros(acc.shape, F32)

    def base_of(i):
        slot = jnp.where(i < 3, idx[1] + i * CK, idx[2] + (i - 3) * CK)
        return jnp.where(i < 6, slot, jnp.where(i == 6, idx[3], idx[4]))

    def collect(want_full, start):
        def visit(n, count):
            i, t = n // tiles, lax.rem(n, tiles)
            base = base_of(i)
            first = idx[5 + t // 2] + lax.rem(t, 2) * 256
            last = first + 255
            lo_a, hi_a, own_a = allowed_of(first)
            lo_b, hi_b, own_b = allowed_of(last)
            pre = i < 6
            lo_first, lo_last = jnp.where(pre, lo_a, own_a), jnp.where(pre, lo_b, own_b)
            hi_first, hi_last = jnp.where(pre, hi_a, first + 1), jnp.where(pre, hi_b, last + 1)
            some = (base + CK > lo_first) & (base < hi_last)
            full = (base >= lo_last) & (base + CK <= hi_first)
            hit = full if want_full else (some & jnp.logical_not(full))

            @pl.when(hit)
            def _():
                chunk_of[count] = i
                tile_of[count] = t

            return count + hit.astype(jnp.int32)

        count = lax.fori_loop(0, CHUNKS * tiles, visit, start)
        rounds = (count + UNROLL - 1) // UNROLL
        for k in range(UNROLL):
            chunk_of[count + k] = 0
            tile_of[count + k] = tiles
        return rounds

    full_rounds = collect(True, 0)
    all_rounds = collect(False, full_rounds * UNROLL)
    for c in copies:
        c.wait()
    q[tiles * R : (tiles + 1) * R] = jnp.zeros((R, H), BF16)

    def scores(n, out):
        keys = keep[pl.ds(pl.multiple_of(chunk_of[n] * CK, CK), CK), :H]
        out[...] = nt_dot(keys, q[pl.ds(pl.multiple_of(tile_of[n] * R, R), R), :])

    def consume(n, s_ref, masked):
        i, t = chunk_of[n], tile_of[n]
        s = s_ref[...]
        if masked:
            pos = base_of(i) + lax.broadcasted_iota(jnp.int32, (CK, R), 0)
            kind = jnp.where(i < 6, 0, 2)
            lo, hi = limits[t, pl.ds(kind, 1)], limits[t, pl.ds(kind + 1, 1)]
            s = jnp.where((pos >= lo) & (pos < hi), s, -jnp.inf)
        old = top[t]
        new = jnp.maximum(old, jnp.max(s, axis=0, keepdims=True))
        p = jnp.exp2(s * SCALE2 - new * SCALE2)
        factor = jnp.exp2((old - new) * SCALE2)
        top[t] = new
        tot[t] = tot[t] * factor + jnp.sum(p, axis=0, keepdims=True)
        values = keep[pl.ds(pl.multiple_of(i * CK, CK), CK), H:]
        acc[t] = acc[t] * factor + lax.dot_general(
            values, p.astype(BF16), (((0,), (0,)), ((), ())), preferred_element_type=F32
        )

    def rounds(masked):
        def body(n, _):
            for k in range(UNROLL):
                cur, nxt = (sa, sb) if k % 2 == 0 else (sb, sa)
                scores(n * UNROLL + k + 1, nxt)
                consume(n * UNROLL + k, cur, masked)
            return 0

        return body

    chunk_of[all_rounds * UNROLL] = 0
    tile_of[all_rounds * UNROLL] = tiles
    scores(0, sa)
    lax.fori_loop(0, full_rounds, rounds(False), 0)
    lax.fori_loop(full_rounds, all_rounds, rounds(True), 0)

    for t in range(tiles):
        total = tot[t]
        safe = jnp.where(total > 0.0, total, 1.0)
        cols = slice((t % 2) * R, (t % 2 + 1) * R)
        out = outs[t // 2]
        out[0:H, cols] = (acc[t] / safe).astype(BF16)
        lse = jnp.where(total > 0.0, top[t] * SCALE2 + jnp.log2(safe), FLOOR)
        high = lse.astype(BF16).astype(F32)
        mid = (lse - high).astype(BF16).astype(F32)
        low = lse - high - mid
        row = lax.broadcasted_iota(jnp.int32, (16, R), 0)
        packed = jnp.where(row == 0, high, jnp.where(row == 1, mid, jnp.where(row == 2, low, 0.0)))
        out[H : H + 16, cols] = packed.astype(BF16)


def attend(idx, suffix_lengths, prefix_lengths, qs, caches, kvs):
    count, tiles = len(qs), 2 * len(qs)
    return pl.pallas_call(
        functools.partial(attend_kernel, count),
        out_shape=tuple(jax.ShapeDtypeStruct((H + 16, 1024), BF16) for _ in range(count)),
        in_specs=[SMEM] * 3 + [HBM] * (count + 4),
        out_specs=tuple([VMEM] * count),
        scratch_shapes=[
            pltpu.VMEM(((tiles + 1) * R, H), BF16),
            pltpu.VMEM((CHUNKS * CK, 2 * H), BF16),
            pltpu.VMEM((tiles + 1, 4, R), jnp.int32),
            pltpu.VMEM((tiles + 1, 1, R), F32),
            pltpu.VMEM((tiles + 1, 1, R), F32),
            pltpu.VMEM((tiles + 1, H, R), F32),
            pltpu.VMEM((CK, R), F32),
            pltpu.VMEM((CK, R), F32),
            pltpu.SMEM((CHUNKS * tiles + 4 * UNROLL,), jnp.int32),
            pltpu.SMEM((CHUNKS * tiles + 4 * UNROLL,), jnp.int32),
            pltpu.SemaphoreType.DMA((count + 6,)),
        ],
        compiler_params=pltpu.CompilerParams(vmem_limit_bytes=20 << 20),
        cost_estimate=pl.CostEstimate(
            flops=count * (3 << 30), bytes_accessed=4 << 20, transcendentals=count << 21
        ),
        name="attend",
    )(idx, suffix_lengths, prefix_lengths, *pin([*qs, *caches, *kvs]))


def combine_kernel(gates, p0, p1, p2, p3, out):
    parts = (p0, p1, p2, p3)
    lses = []
    for p in parts:
        rows = p[H : H + 16].astype(F32)
        lses.append(rows[0:1] + rows[1:2] + rows[2:3])
    high = jnp.maximum(jnp.maximum(lses[0], lses[1]), jnp.maximum(lses[2], lses[3]))
    share = [jnp.exp2(v - high) for v in lses]
    norm = gates[...] / (share[0] + share[1] + share[2] + share[3])
    for at in range(0, 1024, 256):
        cols = slice(at, at + 256)
        total = jnp.zeros((H, 256), F32)
        for p, s in zip(parts, share):
            total += p[0:H, cols].astype(F32) * s[:, cols]
        out[cols] = jnp.transpose(total * norm[:, cols]).astype(BF16)


def combine(gates, parts):
    return pl.pallas_call(
        combine_kernel,
        out_shape=jax.ShapeDtypeStruct((1024, H), BF16),
        in_specs=[VMEM] * 5,
        out_specs=VMEM,
        compiler_params=pltpu.CompilerParams(vmem_limit_bytes=8 << 20),
        cost_estimate=pl.CostEstimate(flops=1 << 22, bytes_accessed=2 << 20, transcendentals=0),
        name="combine",
    )(gates, *parts)


def out_kernel(idx, routes, own, other, *refs):
    blocks = refs[:10]
    out, held, padded, sem = refs[10:]
    core = idx[8]
    copies = []
    for k, slot in enumerate((0, 1, 2, 3, 6, 7)):
        copies.append(pltpu.make_async_copy(blocks[k], held.at[idx[slot]], sem.at[k]))
    for k in range(6, 10):
        target = held.at[idx[4 + (k - 6) // 2], pl.ds((k % 2) * 1024, 1024)]
        copies.append(pltpu.make_async_copy(blocks[k], target, sem.at[k]))
    for c in copies:
        c.start()
    for half in range(2):
        rows = slice(half * 256, (half + 1) * 256)
        wanted = [jnp.broadcast_to(routes[rows, j : j + 1], (256, H)) for j in range(2)]
        for side, source in enumerate((own, other)):
            head = core if side == 0 else 1 - core
            first = source[half * 512 : half * 512 + 256].astype(F32)
            second = source[half * 512 + 256 : half * 512 + 512].astype(F32)
            for e in range(E):
                value = jnp.where(wanted[1] == e, second, 0.0)
                value = jnp.where(wanted[0] == e, first, value).astype(BF16)
                padded[rows, pl.ds(pl.multiple_of((head * E + e) * H, H), H)] = value
    for c in copies:
        c.wait()
    for k in range(0, 8, 2):
        w = jnp.concatenate([held[k], held[k + 1]], axis=1)
        value = jnp.dot(padded[...], w, preferred_element_type=F32)
        for s in range(2):
            out[k + s] = value[:, s * H : (s + 1) * H].astype(BF16)


def project_out(idx, routes, own, other, blocks):
    return pl.pallas_call(
        out_kernel,
        out_shape=jax.ShapeDtypeStruct((8, 512, H), BF16),
        in_specs=[SMEM, VMEM, VMEM, VMEM] + [HBM] * 10,
        out_specs=VMEM,
        scratch_shapes=[
            pltpu.VMEM((8, 2048, H), BF16),
            pltpu.VMEM((512, 2048), BF16),
            pltpu.SemaphoreType.DMA((10,)),
        ],
        compiler_params=pltpu.CompilerParams(vmem_limit_bytes=20 << 20),
        cost_estimate=pl.CostEstimate(flops=4 << 30, bytes_accessed=6 << 20, transcendentals=0),
        name="project_out",
    )(idx, routes, own, other, *pin(blocks))


def on_device(
    tokens,
    norm_gain,
    router,
    routes,
    kv_weight,
    query_weight,
    out_weight,
    prefix_cache,
    suffix_lengths,
    prefix_lengths,
):
    xl, y, c = (lax.axis_index(a) for a in WIDE)
    first_core = c == 0
    chips = chip_order()

    def table(values):
        return jnp.stack([jnp.asarray(v, jnp.int32) for v in values])

    def head_rows(w, h):
        rows = w.shape[0] // 2
        return lax.dynamic_slice_in_dim(w, h * rows, rows, 0)

    def weights_of(h):
        return jnp.concatenate([head_rows(query_weight, h), head_rows(kv_weight, h)], axis=0)

    w = jnp.stack([weights_of(c), across_core(weights_of(1 - c))])
    other_routes = across_core(routes)
    both_routes = jnp.where(
        first_core,
        jnp.concatenate([routes, other_routes]),
        jnp.concatenate([other_routes, routes]),
    )

    def cache_of(h):
        return lax.dynamic_slice_in_dim(prefix_cache, h * 2 * H, 2 * H, 1)

    cache = jnp.stack([cache_of(c), across_core(cache_of(1 - c))])
    half_row = across_far(tokens)
    far, ym, yp, a = along_y(w, 2), along_y(w, 3), along_y(w, 1), across_x(w)
    caches = [cache, across_x(cache)]
    blocks = [lax.all_gather(v, "z", axis=0) for v in (tokens, half_row)]
    xh = lax.axis_index("xh")
    token_src = [k * 2 + (xh ^ s) for s in range(2) for k in range(4)]
    places = [lax.rem(lax.rem(v, 4) + 4 - y, 4) * 2 + (v // 4 ^ xl) for v in token_src]
    normed = normalise(table(token_src + places), norm_gain.reshape(8, 1, 256), blocks)
    far, ym, yp, a, normed, caches, both_routes = lax.optimization_barrier(
        (far, ym, yp, a, normed, caches, both_routes)
    )
    am, ap, afar = along_y(a, 3), along_y(a, 1), across_x(far)
    other_normed = across_core(normed)
    gathered = [w, a, ym, am, far, afar, yp, ap]

    out_early, am, ap = lax.optimization_barrier((out_weight, am, ap))
    gathered[3], gathered[7] = am, ap
    o_ym, o_yp, o_a = along_y(out_early, 3), along_y(out_early, 1), across_x(out_early)
    q, kv, gates = project(
        table(chips + [c]), both_routes, router.T, normed, other_normed, gathered
    )
    kvs = [kv, across_x(kv)]
    qs = [q] + [along_y(q, k) for k in (1, 2, 3)]
    qs[0], o_ym, o_yp = lax.optimization_barrier((q, o_ym, o_yp))
    o_a, up, down, kvs[1] = lax.optimization_barrier((o_a, o_yp[:1024], o_ym[1024:], kvs[1]))
    far0, far1 = along_y(up, 1), along_y(down, 3)
    o_am, o_ap = across_x(o_ym), across_x(o_yp)

    firsts = [(xl * 4 + lax.rem(y + 4 - k, 4)) * 512 for k in range(4)]
    mine, partner = xl * 4 + y, (1 - xl) * 4 + y
    at = [c, mine * 1536, partner * 1536, mine * 512, partner * 512]
    lengths = (suffix_lengths, prefix_lengths)
    (part2,) = attend(table(at + firsts[2:3]), *lengths, qs[2:3], caches, kvs)
    part2, qs[1], qs[3] = lax.optimization_barrier((part2, qs[1], qs[3]))
    part1, part3 = attend(table(at + firsts[1::2]), *lengths, qs[1::2], caches, kvs)
    part2 = along_y(part2, 2)
    part2, qs[0] = tie(part2, qs[0])
    (own,) = attend(table(at + firsts[:1]), *lengths, qs[:1], caches, kvs)
    part1, part3, far0, far1, o_am, o_ap = lax.optimization_barrier(
        (part1, part3, far0, far1, o_am, o_ap)
    )
    parts = [own, along_y(part1, 3), part2, along_y(part3, 1)]
    afar0, afar1 = across_x(far0), across_x(far1)
    parts, afar0, afar1 = lax.optimization_barrier((parts, afar0, afar1))
    out_blocks = [out_weight, o_a, o_ym, o_am, o_yp, o_ap, far0, far1, afar0, afar1]
    gate_row = gates.reshape(2, 256, 2).transpose(0, 2, 1).reshape(1, 1024)
    attended = combine(gate_row, parts)

    sums = project_out(
        table(chips + [c]), both_routes, attended, across_core(attended), out_blocks
    )
    sums = lax.all_to_all(sums, NARROW, 0, 0, tiled=True)
    total = jnp.sum(sums.astype(F32), axis=0)
    here = lax.dynamic_slice_in_dim(total, c * 256, 256, 0).astype(BF16)
    there = lax.dynamic_slice_in_dim(total, (1 - c) * 256, 256, 0).astype(BF16)
    there = across_core(there)
    return jnp.where(
        first_core,
        jnp.concatenate([here, there], axis=1),
        jnp.concatenate([there, here], axis=1),
    )


def solution(mesh):
    fine = Mesh(mesh.devices.reshape(SIZES), AXES)
    placed = (
        P(WIDE, NARROW),
        P(),
        P(),
        P(WIDE, None),
        P(NARROW, WIDE),
        P(NARROW, WIDE),
        P(NARROW, WIDE),
        P(WIDE, NARROW),
        P(),
        P(),
    )
    return jax.shard_map(
        on_device, mesh=fine, in_specs=placed, out_specs=P(WIDE, NARROW), check_vma=False
    )
```
